256 devices in a mesh: seq: 16 (over z, x_lo), db: 16 (over x_hi, y, core).
Axes of the slice: x: 4 (x_hi: 2, x_lo: 2; x = x_hi * 2 + x_lo), y: 4, z: 8, core: 2. Of those that a mesh axis runs over, the one named last changes fastest.
Arguments:
- decoder_states: bfloat16 [16384, 4096], P('seq'), may hold values from -6 to 6
- query_weight: bfloat16 [4096, 4096], P(None, 'db'), may hold values from -0.09375 to 0.09375
- output_weight: bfloat16 [4096, 4096], P('db'), may hold values from -0.5 to 0.5
- neighbour_kv: bfloat16 [128, 128, 2, 4096], P('seq', None, None, 'db'), may hold values from -110 to 110
- neighbour_shard: int32 [256, 2], P('seq'), may hold values from 0 to 15, all different within a row; in each aligned block of 16 rows (0 to 15, 16 to 31, ...) at most 3 rows name the same one
- neighbour_entry: int32 [256, 2], P('seq'), may hold values from 0 to 7
- neighbour_count: int32 [256], P('seq'), may hold values from 1 to 2
Outputs:
- cross_out: bfloat16 [16384, 4096], P('seq', 'db')
The draws below stay inside these ranges and needn't reach their ends.
Inputs may be any that keep to these rules, and one draw needn't show every extreme that they name: `neighbour_shard`: in each aligned block of 16 spans (the spans of one index of seq), no shard is named by more than 3 spans and one shard is named by exactly 3; the 2 neighbours of one span lie on different shards.
All inputs are finite; a program needn't handle non-finite values.
Results may differ from the reference program's by a relative error of at most 0.017.
Values may be sent and summed in bfloat16 or wider, within the bound.
A program may use at most 128 MiB of HBM per device.

```python
import math
import jax
import jax.numpy as jnp
import numpy as np
from jax import lax

D = 4096
HD = 128
SPAN = 64
NLEN = 128
K = 2
CPD = 16
ENT_DEV = 8
SPANS = 256
TOKENS = 16384
ENTRIES = 128
GROUPS = 16
HEADS_GRP = 2
CAP = 3
N_SEQ = 16


def draw_neighbour_kv(key, part):
    shape_all = (ENTRIES, NLEN, 2, D)
    base = jax.random.normal(key, shape_all, jnp.float32)
    return jnp.clip(base, -6.0, 6.0).astype(jnp.bfloat16)


def touch_ends(values, rng, least, high):
    extent = values.shape
    index_at = [jax.random.randint(jax.random.fold_in(rng, axis), (), 0, extent[axis]) for axis in range(len(extent))]
    values = values.at[tuple(index_at)].set(least)
    longest = extent.index(max(extent))
    index_at[longest] = (index_at[longest] + 1) % extent[longest]
    return values.at[tuple(index_at)].set(high)


def spiked(entries, stream_key, source, target, parts, factor):
    owner, partner = [(jnp.arange(entries.shape[position]) // (entries.shape[position] // parts)).reshape([-1 if axis == position else 1 for axis in range(entries.ndim)]) for position in (source, target)]
    chosen = jax.random.permutation(stream_key, parts)[partner]
    strong = (owner == chosen) | (owner == (partner + parts // 2) % parts)
    return jnp.where(strong, factor * entries, entries)


def levels(key, extent, cuts, least, high):
    gain = 1.0
    for axis_at, parts in cuts:
        draws = jax.random.uniform(jax.random.fold_in(jax.random.fold_in(key, 6), axis_at), (parts,), jnp.float32, least / len(cuts), high / len(cuts))
        gain = gain * jnp.repeat(jnp.exp(draws), extent[axis_at] // parts).reshape((-1,) + (1,) * (len(extent) - 1 - axis_at))
    return gain


def deal_out(key, own, number, rows, count, top, limit, lean):
    order = jax.random.permutation(key, count)
    crowded, usual = load_shares(count, rows * top, limit, lean, True), load_shares(count, rows * top, limit, lean, False)
    places = jnp.arange(count)

    def named(lengths, rotation):
        used = int((lengths > 0).sum())
        fixed = max(1, used // 4)
        moved = fixed + (places - fixed + rotation * (used - fixed)) % max(1, count - fixed)
        return jnp.zeros((count,), jnp.int32).at[order[jnp.where(places < fixed, places, moved)]].set(jnp.asarray(lengths, jnp.int32))

    lengths = jnp.where(number % 4 == 0, named(crowded, number // 4), named(usual, number - number // 4 - 1))
    mixed = jax.random.permutation(jax.random.fold_in(own, 3), count)
    giver, sink = mixed[0:count // 2 * 2:2], mixed[1:count // 2 * 2:2]
    room = jnp.minimum(lengths[giver] - 1, limit - lengths[sink]) // 2
    room = jnp.where((giver == order[0]) | (sink == order[0]) | (lengths[sink] == 0), 0, jnp.maximum(room, 0))
    moved = jax.random.randint(jax.random.fold_in(own, 4), (count // 2,), 0, 1 << 20) % (room + 1)
    lengths = lengths.at[giver].add(-moved).at[sink].add(moved)
    labels = jnp.searchsorted(jnp.cumsum(lengths), jnp.arange(rows * top), side="right").astype(jnp.int32)
    table = labels.reshape(top, rows).T
    table = table[jax.random.permutation(jax.random.fold_in(own, 1), rows)]
    rotation = jax.random.randint(jax.random.fold_in(own, 2), (rows, 1), 0, top)
    return jnp.take_along_axis(table, (jnp.arange(top)[None, :] + rotation) % top, axis=1)


def load_shares(amount, total, limit, slope, full):
    portions = [(1 << 20) // math.isqrt(standing ** slope) + 1 for standing in range(1, amount + 1)]
    largest = limit if full else min(limit, max(-(-total // amount), total * portions[0] // sum(portions)))
    least = 1 if total - largest >= amount - 1 else 0
    given, rest = [largest] + [least] * (amount - 1), total - largest - least * (amount - 1)
    while rest > 0:
        free = [i for i in range(1, amount) if given[i] < largest] or [i for i in range(1, amount) if given[i] < limit]
        pool, left = sum([portions[i] for i in free]), rest
        for i in free:
            extra = min(limit - given[i], max(1, left * portions[i] // pool), rest)
            given[i] = given[i] + extra
            rest = rest - extra
    return np.array(given)


def noise(key, dims, spread, limit, pieces=(), kind=jnp.bfloat16):
    entries = jax.random.normal(key, dims, jnp.float32) * spread
    if len(pieces) > 0:
        entries = levels(key, dims, pieces, -0.22, 0.18) * entries
    return jnp.clip(entries, min=-limit, max=limit).astype(kind)


def noise_with(own_key, extent, deviation, limit, shards, heavy, kind=jnp.bfloat16):
    result = deviation * jax.random.normal(own_key, extent, jnp.float32)
    if shards:
        result = result * levels(own_key, extent, shards, -0.22, 0.18)
    return jnp.clip(spiked(result, jax.random.fold_in(own_key, 3), *heavy), -limit, limit).astype(kind)


def setup_inputs(seed: int = 0) -> dict:
    key_of = jax.random.split(jax.random.key(seed), 8)
    decoder_states = noise(key_of[0], (TOKENS, D), 1.0, 6.0, ((0, 16),))
    query_weight = noise(key_of[1], (D, D), D ** -0.5, 0.09375, ((1, 16),))
    output_weight = noise_with(key_of[2], (D, D), (D // 16) ** -0.5, 0.5, ((0, 16),), (0, 1, 16, 2.0))
    neighbour_kv = draw_neighbour_kv(jax.random.fold_in(key_of[7], 71), 0)
    neighbour_shard_keys = jax.random.split(jax.random.fold_in(key_of[4], 1), SPANS // CPD)
    neighbour_shard_turns = jax.random.permutation(jax.random.fold_in(key_of[4], 3), SPANS // CPD)
    neighbour_shard = jax.vmap(lambda own, number: deal_out(jax.random.fold_in(key_of[4], 2), own, number, CPD, N_SEQ, K, CAP, 2))(neighbour_shard_keys, neighbour_shard_turns).reshape((SPANS, K))
    neighbour_entry = touch_ends(jax.random.randint(key_of[5], (SPANS, K), 0, ENT_DEV), jax.random.fold_in(key_of[5], 1), 0, ENT_DEV - 1).astype(jnp.int32)
    neighbour_count = touch_ends(jax.random.randint(key_of[6], (SPANS,), 1, K + 1), jax.random.fold_in(key_of[6], 1), 1, K).astype(jnp.int32)
    return {"decoder_states": decoder_states, "query_weight": query_weight, "output_weight": output_weight, "neighbour_kv": neighbour_kv, "neighbour_shard": neighbour_shard, "neighbour_entry": neighbour_entry, "neighbour_count": neighbour_count}


def reference(decoder_states, query_weight, output_weight, neighbour_kv, neighbour_shard, neighbour_entry, neighbour_count):
    tokens_all = decoder_states.shape[0]
    span_total = tokens_all // SPAN
    group_width = D // GROUPS
    index_rows = (neighbour_shard * ENT_DEV + neighbour_entry).astype(jnp.int32)
    live_slots = jnp.arange(K, dtype=jnp.int32)[None, :] < neighbour_count[:, None]
    masked = live_slots[:, None, None, :, None]
    scale_factor = 1.0 / math.sqrt(HD)

    def one_group(total, group):
        first_col = (group * group_width).astype(jnp.int32)
        weight_q = lax.dynamic_slice_in_dim(query_weight, first_col, group_width, 1)
        weight_o = lax.dynamic_slice_in_dim(output_weight, first_col, group_width, 0)
        kv_cols = lax.dynamic_slice_in_dim(neighbour_kv, first_col, group_width, 3)
        queries = jnp.dot(decoder_states, weight_q, preferred_element_type=jnp.float32).astype(jnp.bfloat16)
        queries = queries.reshape(span_total, SPAN, HEADS_GRP, HD)
        blocks = kv_cols[index_rows].reshape(span_total, K, NLEN, 2, HEADS_GRP, HD)
        key_rows = blocks[:, :, :, 0]
        val_rows = blocks[:, :, :, 1]
        scores = jnp.einsum('cqhd,cknhd->chqkn', queries.astype(jnp.float32), key_rows.astype(jnp.float32)) * scale_factor
        scores = jnp.where(masked, scores, -1e+30)
        top_score = lax.optimization_barrier(jnp.max(scores, axis=(3, 4), keepdims=True))
        exponent = jnp.where(masked, jnp.exp(scores - top_score), 0.0)
        probs_bf = (exponent / lax.optimization_barrier(jnp.sum(exponent, axis=(3, 4), keepdims=True))).astype(jnp.bfloat16)
        context = jnp.einsum('chqkn,cknhd->cqhd', probs_bf.astype(jnp.float32), val_rows.astype(jnp.float32))
        context = context.astype(jnp.bfloat16).reshape(tokens_all, group_width)
        partial_value = jnp.dot(context, weight_o, preferred_element_type=jnp.float32).astype(jnp.bfloat16)
        partial_value = lax.optimization_barrier(partial_value)
        return (total + partial_value.astype(jnp.float32), None)
    total, unused = lax.scan(one_group, jnp.zeros((tokens_all, D), jnp.float32), jnp.arange(GROUPS, dtype=jnp.int32))
    return total.astype(jnp.bfloat16)
```

```python
import math

import jax
import jax.numpy as jnp
from jax import lax
from jax.sharding import PartitionSpec as P

HD = 128
SPAN = 64
K = 2
CAP = 3


def request_tables(neighbour_shard, neighbour_entry, neighbour_count, me, n_seq):
    spans_here = neighbour_shard.shape[0]
    table = jnp.concatenate(
        [neighbour_shard, neighbour_entry, neighbour_count[:, None]], axis=1
    )
    table_all = lax.all_gather(table, "seq", axis=0, tiled=False)
    shard_all = table_all[:, :, 0:K]
    entry_all = table_all[:, :, K : 2 * K]
    count_all = table_all[:, :, 2 * K]
    live_all = jnp.arange(K, dtype=jnp.int32)[None, None, :] < count_all[:, :, None]
    shard_flat = shard_all.reshape(n_seq, spans_here * K)
    entry_flat = entry_all.reshape(n_seq, spans_here * K)
    live_flat = live_all.reshape(n_seq, spans_here * K)
    match = (shard_flat == me) & live_flat
    rank = jnp.cumsum(match.astype(jnp.int32), axis=1) - 1
    slots = jnp.arange(CAP, dtype=jnp.int32)
    pick = match[:, :, None] & (rank[:, :, None] == slots[None, None, :])
    send_entry = jnp.sum(jnp.where(pick, entry_flat[:, :, None], 0), axis=1)
    own_shard = neighbour_shard.reshape(-1)
    own_live = (
        jnp.arange(K, dtype=jnp.int32)[None, :] < neighbour_count[:, None]
    ).reshape(-1)
    same = (own_shard[None, :] == own_shard[:, None]) & own_live[None, :]
    earlier = jnp.arange(own_shard.shape[0])[None, :] < jnp.arange(own_shard.shape[0])[:, None]
    own_rank = jnp.sum((same & earlier).astype(jnp.int32), axis=1)
    own_rank = jnp.minimum(own_rank, CAP - 1)
    recv_idx = own_shard * CAP + own_rank
    return send_entry, recv_idx


def on_device(
    decoder_states,
    query_weight,
    output_weight,
    neighbour_kv,
    neighbour_shard,
    neighbour_entry,
    neighbour_count,
):
    tok_rows = decoder_states.shape[0]
    span_total = tok_rows // SPAN
    row_width = query_weight.shape[1]
    heads_here = row_width // HD
    key_len = neighbour_kv.shape[1]
    n_seq = lax.psum(1, "seq")
    me = lax.axis_index("seq")
    queries = jnp.dot(decoder_states, query_weight, preferred_element_type=jnp.float32).astype(
        jnp.bfloat16
    )
    queries = queries.reshape(span_total, SPAN, heads_here, HD)

    send_entry, recv_idx = request_tables(
        neighbour_shard, neighbour_entry, neighbour_count, me, n_seq
    )
    send_buf = jnp.take(neighbour_kv, send_entry.reshape(-1), axis=0)
    send_buf = send_buf.reshape((n_seq, CAP) + neighbour_kv.shape[1:])
    recv_buf = lax.all_to_all(send_buf, "seq", 0, 0, tiled=True)
    recv_buf = recv_buf.reshape((n_seq * CAP,) + neighbour_kv.shape[1:])
    blocks = jnp.take(recv_buf, recv_idx, axis=0)

    blocks = blocks.reshape(span_total, K, key_len, 2, heads_here, HD)
    key_rows = blocks[:, :, :, 0]
    val_rows = blocks[:, :, :, 1]
    scores = jnp.einsum(
        "cqhd,cknhd->chqkn", queries, key_rows, preferred_element_type=jnp.float32
    ) * (1.0 / math.sqrt(HD))
    live_slots = jnp.arange(K, dtype=jnp.int32)[None, :] < neighbour_count[:, None]
    masked = live_slots[:, None, None, :, None]
    scores = jnp.where(masked, scores, -1e30)
    top_score = jnp.max(scores, axis=(3, 4), keepdims=True)
    exponent = jnp.where(masked, jnp.exp(scores - top_score), 0.0)
    probs_bf = (exponent / jnp.sum(exponent, axis=(3, 4), keepdims=True)).astype(jnp.bfloat16)
    context = jnp.einsum(
        "chqkn,cknhd->cqhd", probs_bf, val_rows, preferred_element_type=jnp.float32
    )
    context = context.astype(jnp.bfloat16).reshape(tok_rows, row_width)
    partial_value = jnp.dot(context, output_weight, preferred_element_type=jnp.float32)
    return lax.psum_scatter(
        partial_value.astype(jnp.bfloat16), "db", scatter_dimension=1, tiled=True
    )


def solution(mesh):
    in_specs = (
        P("seq", None),
        P(None, "db"),
        P("db", None),
        P("seq", None, None, "db"),
        P("seq", None),
        P("seq", None),
        P("seq"),
    )
    out_specs = P("seq", "db")
    return jax.shard_map(
        on_device, mesh=mesh, in_specs=in_specs, out_specs=out_specs, check_vma=False
    )
```

```python
import math

import jax
import jax.numpy as jnp
from jax import lax
from jax.sharding import PartitionSpec as P

HD = 128
SPAN = 64
K = 2
CAP = 3


def slot_places(neighbour_shard, neighbour_count):
    own_shard = neighbour_shard.reshape(-1)
    slots = own_shard.shape[0]
    own_live = (
        jnp.arange(K, dtype=jnp.int32)[None, :] < neighbour_count[:, None]
    ).reshape(-1)
    same = (own_shard[None, :] == own_shard[:, None]) & own_live[None, :]
    earlier = jnp.arange(slots)[None, :] < jnp.arange(slots)[:, None]
    own_rank = jnp.minimum(jnp.sum((same & earlier).astype(jnp.int32), axis=1), CAP - 1)
    return own_live, own_shard * CAP + own_rank


def on_device(
    decoder_states,
    query_weight,
    output_weight,
    neighbour_kv,
    neighbour_shard,
    neighbour_entry,
    neighbour_count,
):
    tok_rows = decoder_states.shape[0]
    span_total = tok_rows // SPAN
    row_width = query_weight.shape[1]
    heads_here = row_width // HD
    key_len = neighbour_kv.shape[1]
    n_seq = lax.psum(1, "seq")
    places_total = n_seq * CAP
    queries = jnp.dot(decoder_states, query_weight, preferred_element_type=jnp.float32).astype(
        jnp.bfloat16
    )
    queries = queries.reshape(span_total, SPAN, row_width)

    live, place = slot_places(neighbour_shard, neighbour_count)
    target = jnp.where(live, place, places_total)
    span_of_slot = jnp.arange(span_total * K, dtype=jnp.int32) // K
    send_q = jnp.zeros((places_total, SPAN, row_width), jnp.bfloat16)
    send_q = send_q.at[target].set(queries[span_of_slot], mode="drop")
    send_e = jnp.zeros((places_total,), jnp.int32)
    send_e = send_e.at[target].set(neighbour_entry.reshape(-1), mode="drop")
    recv_q = lax.all_to_all(
        send_q.reshape(n_seq, CAP, SPAN, row_width), "seq", 0, 0, tiled=True
    ).reshape(places_total, SPAN, heads_here, HD)
    recv_e = lax.all_to_all(send_e.reshape(n_seq, CAP), "seq", 0, 0, tiled=True).reshape(-1)

    blocks = jnp.take(neighbour_kv, recv_e, axis=0)
    blocks = blocks.reshape(places_total, key_len, 2, heads_here, HD)
    key_rows = blocks[:, :, 0]
    val_rows = blocks[:, :, 1]
    scores = jnp.einsum(
        "pqhd,pnhd->phqn", recv_q, key_rows, preferred_element_type=jnp.float32
    ) * (1.0 / math.sqrt(HD))
    top = jnp.max(scores, axis=3, keepdims=True)
    weights = jnp.exp(scores - top)
    total = jnp.sum(weights, axis=3, keepdims=True)
    part = jnp.einsum(
        "phqn,pnhd->pqhd", weights.astype(jnp.bfloat16), val_rows,
        preferred_element_type=jnp.float32,
    )
    part = part / jnp.transpose(total, (0, 2, 1, 3))
    stats = jnp.concatenate([top, total], axis=3)
    back_ctx = lax.all_to_all(
        part.astype(jnp.bfloat16).reshape(n_seq, CAP, SPAN, row_width), "seq", 0, 0, tiled=True
    ).reshape(places_total, SPAN, heads_here, HD)
    back_stats = lax.all_to_all(
        stats.reshape(n_seq, CAP, heads_here, SPAN, 2), "seq", 0, 0, tiled=True
    ).reshape(places_total, heads_here, SPAN, 2)

    slot_ctx = jnp.take(back_ctx, place, axis=0).reshape(span_total, K, SPAN, heads_here, HD)
    slot_stats = jnp.take(back_stats, place, axis=0).reshape(span_total, K, heads_here, SPAN, 2)
    live_k = live.reshape(span_total, K)[:, :, None, None]
    slot_top = jnp.where(live_k, slot_stats[..., 0], -jnp.inf)
    best = jnp.max(slot_top, axis=1, keepdims=True)
    scale = jnp.where(live_k, jnp.exp(slot_top - best) * slot_stats[..., 1], 0.0)
    share = scale / jnp.sum(scale, axis=1, keepdims=True)
    share = jnp.transpose(share, (0, 1, 3, 2))[..., None]
    slot_vals = jnp.where(live_k[..., None], slot_ctx.astype(jnp.float32), 0.0)
    context = jnp.sum(share * slot_vals, axis=1)
    context = context.astype(jnp.bfloat16).reshape(tok_rows, row_width)
    partial_value = jnp.dot(context, output_weight, preferred_element_type=jnp.float32)
    return lax.psum_scatter(
        partial_value.astype(jnp.bfloat16), "db", scatter_dimension=1, tiled=True
    )


def solution(mesh):
    in_specs = (
        P("seq", None),
        P(None, "db"),
        P("db", None),
        P("seq", None, None, "db"),
        P("seq", None),
        P("seq", None),
        P("seq"),
    )
    out_specs = P("seq", "db")
    return jax.shard_map(
        on_device, mesh=mesh, in_specs=in_specs, out_specs=out_specs, check_vma=False
    )
```

```python
import math

import jax
import jax.numpy as jnp
from jax import lax
from jax.sharding import PartitionSpec as P

HD = 128
SPAN = 64
K = 2
CAP = 3


def slot_places(neighbour_shard, neighbour_count):
    own_shard = neighbour_shard.reshape(-1)
    slots = own_shard.shape[0]
    own_live = (
        jnp.arange(K, dtype=jnp.int32)[None, :] < neighbour_count[:, None]
    ).reshape(-1)
    same = (own_shard[None, :] == own_shard[:, None]) & own_live[None, :]
    earlier = jnp.arange(slots)[None, :] < jnp.arange(slots)[:, None]
    own_rank = jnp.minimum(jnp.sum((same & earlier).astype(jnp.int32), axis=1), CAP - 1)
    return own_live, own_shard * CAP + own_rank


def on_device(
    decoder_states,
    query_weight,
    output_weight,
    neighbour_kv,
    neighbour_shard,
    neighbour_entry,
    neighbour_count,
):
    tok_rows = decoder_states.shape[0]
    span_total = tok_rows // SPAN
    row_width = query_weight.shape[1]
    heads_here = row_width // HD
    key_len = neighbour_kv.shape[1]
    n_seq = lax.psum(1, "seq")
    places_total = n_seq * CAP
    queries = jnp.dot(decoder_states, query_weight, preferred_element_type=jnp.float32).astype(
        jnp.bfloat16
    )
    queries = queries.reshape(span_total, SPAN, row_width)

    live, place = slot_places(neighbour_shard, neighbour_count)
    target = jnp.where(live, place, places_total)
    span_of_slot = jnp.arange(span_total * K, dtype=jnp.int32) // K
    send_q = jnp.zeros((places_total, SPAN, row_width), jnp.bfloat16)
    send_q = send_q.at[target].set(queries[span_of_slot], mode="drop")
    send_e = jnp.zeros((places_total,), jnp.int32)
    send_e = send_e.at[target].set(neighbour_entry.reshape(-1), mode="drop")
    recv_q = lax.all_to_all(
        send_q.reshape(n_seq, CAP, SPAN, row_width), "seq", 0, 0, tiled=True
    ).reshape(places_total, SPAN, heads_here, HD)
    recv_e = lax.all_to_all(send_e.reshape(n_seq, CAP), "seq", 0, 0, tiled=True).reshape(-1)
    n_db = lax.psum(1, "db")
    features = output_weight.shape[1] // n_db
    weight_cols = lax.all_to_all(
        output_weight.reshape(row_width, n_db, features), "db", 1, 0, tiled=True
    )
    weight_cols = weight_cols.reshape(n_db, row_width, features)
    weight_cols, recv_q = lax.optimization_barrier((weight_cols, recv_q))

    blocks = jnp.take(neighbour_kv, recv_e, axis=0)
    blocks = blocks.reshape(places_total, key_len, 2, heads_here, HD)
    key_rows = blocks[:, :, 0]
    val_rows = blocks[:, :, 1]
    scores = jnp.einsum(
        "pqhd,pnhd->phqn", recv_q, key_rows, preferred_element_type=jnp.float32
    ) * (1.0 / math.sqrt(HD))
    top = jnp.max(scores, axis=3, keepdims=True)
    weights = jnp.exp(scores - top)
    total = jnp.sum(weights, axis=3, keepdims=True)
    part = jnp.einsum(
        "phqn,pnhd->pqhd", weights.astype(jnp.bfloat16), val_rows,
        preferred_element_type=jnp.float32,
    )
    part = part / jnp.transpose(total, (0, 2, 1, 3))
    stats = jnp.concatenate([top, total], axis=3)
    back_ctx = lax.all_to_all(
        part.astype(jnp.bfloat16).reshape(n_seq, CAP, SPAN, row_width), "seq", 0, 0, tiled=True
    ).reshape(places_total, SPAN, heads_here, HD)
    back_stats = lax.all_to_all(
        stats.reshape(n_seq, CAP, heads_here, SPAN, 2), "seq", 0, 0, tiled=True
    ).reshape(places_total, heads_here, SPAN, 2)

    slot_ctx = jnp.take(back_ctx, place, axis=0).reshape(span_total, K, SPAN, heads_here, HD)
    slot_stats = jnp.take(back_stats, place, axis=0).reshape(span_total, K, heads_here, SPAN, 2)
    live_k = live.reshape(span_total, K)[:, :, None, None]
    slot_top = jnp.where(live_k, slot_stats[..., 0], -jnp.inf)
    best = jnp.max(slot_top, axis=1, keepdims=True)
    scale = jnp.where(live_k, jnp.exp(slot_top - best) * slot_stats[..., 1], 0.0)
    share = scale / jnp.sum(scale, axis=1, keepdims=True)
    share = jnp.transpose(share, (0, 1, 3, 2))[..., None]
    slot_vals = jnp.where(live_k[..., None], slot_ctx.astype(jnp.float32), 0.0)
    context = jnp.sum(share * slot_vals, axis=1)
    context = context.astype(jnp.bfloat16).reshape(tok_rows, row_width)
    contexts = lax.all_gather(context, "db", axis=0, tiled=False)
    out = jnp.einsum(
        "str,srf->tf", contexts, weight_cols, preferred_element_type=jnp.float32
    )
    return out.astype(jnp.bfloat16)


def solution(mesh):
    in_specs = (
        P("seq", None),
        P(None, "db"),
        P("db", None),
        P("seq", None, None, "db"),
        P("seq", None),
        P("seq", None),
        P("seq"),
    )
    out_specs = P("seq", "db")
    return jax.shard_map(
        on_device, mesh=mesh, in_specs=in_specs, out_specs=out_specs, check_vma=False
    )
```

```python
import math

import jax
import jax.numpy as jnp
from jax import lax
from jax.sharding import PartitionSpec as P

HD = 128
SPAN = 64
K = 2
CAP = 3


def slot_places(neighbour_shard, neighbour_count):
    own_shard = neighbour_shard.reshape(-1)
    slots = own_shard.shape[0]
    own_live = (
        jnp.arange(K, dtype=jnp.int32)[None, :] < neighbour_count[:, None]
    ).reshape(-1)
    same = (own_shard[None, :] == own_shard[:, None]) & own_live[None, :]
    earlier = jnp.arange(slots)[None, :] < jnp.arange(slots)[:, None]
    own_rank = jnp.minimum(jnp.sum((same & earlier).astype(jnp.int32), axis=1), CAP - 1)
    return own_live, own_shard * CAP + own_rank


def on_device(
    decoder_states,
    query_weight,
    output_weight,
    neighbour_kv,
    neighbour_shard,
    neighbour_entry,
    neighbour_count,
):
    tok_rows = decoder_states.shape[0]
    span_total = tok_rows // SPAN
    row_width = query_weight.shape[1]
    heads_here = row_width // HD
    key_len = neighbour_kv.shape[1]
    n_seq = lax.psum(1, "seq")
    places_total = n_seq * CAP
    queries = jnp.dot(decoder_states, query_weight, preferred_element_type=jnp.float32).astype(
        jnp.bfloat16
    )
    queries = queries.reshape(span_total, SPAN, row_width)

    live, place = slot_places(neighbour_shard, neighbour_count)
    target = jnp.where(live, place, places_total)
    span_of_slot = jnp.arange(span_total * K, dtype=jnp.int32) // K
    send_q = jnp.zeros((places_total, SPAN, row_width), jnp.bfloat16)
    send_q = send_q.at[target].set(queries[span_of_slot], mode="drop")
    send_e = jnp.zeros((places_total,), jnp.int32)
    send_e = send_e.at[target].set(neighbour_entry.reshape(-1), mode="drop")
    recv_q = lax.all_to_all(
        send_q.reshape(n_seq, CAP, SPAN, row_width), "seq", 0, 0, tiled=True
    ).reshape(places_total, SPAN, heads_here, HD)
    recv_e = lax.all_to_all(send_e.reshape(n_seq, CAP), "seq", 0, 0, tiled=True).reshape(-1)
    n_db = lax.psum(1, "db")
    features = output_weight.shape[1] // n_db
    weight_cols = lax.all_to_all(
        output_weight.reshape(row_width, n_db, features), "db", 1, 0, tiled=True
    )
    weight_cols = weight_cols.reshape(n_db, row_width, features)

    blocks = jnp.take(neighbour_kv, recv_e, axis=0)
    blocks = blocks.reshape(places_total, key_len, 2, heads_here, HD)
    key_rows = blocks[:, :, 0]
    val_rows = blocks[:, :, 1]
    scores = jnp.einsum(
        "pqhd,pnhd->phqn", recv_q, key_rows, preferred_element_type=jnp.float32
    ) * (1.0 / math.sqrt(HD))
    top = jnp.max(scores, axis=3, keepdims=True)
    weights = jnp.exp(scores - top)
    total = jnp.sum(weights, axis=3, keepdims=True)
    part = jnp.einsum(
        "phqn,pnhd->pqhd", weights.astype(jnp.bfloat16), val_rows,
        preferred_element_type=jnp.float32,
    )
    part = part / jnp.transpose(total, (0, 2, 1, 3))
    weight_cols, part = lax.optimization_barrier((weight_cols, part))
    stats = jnp.concatenate([top, total], axis=3)
    back_ctx = lax.all_to_all(
        part.astype(jnp.bfloat16).reshape(n_seq, CAP, SPAN, row_width), "seq", 0, 0, tiled=True
    ).reshape(places_total, SPAN, heads_here, HD)
    back_stats = lax.all_to_all(
        stats.reshape(n_seq, CAP, heads_here, SPAN, 2), "seq", 0, 0, tiled=True
    ).reshape(places_total, heads_here, SPAN, 2)

    slot_ctx = jnp.take(back_ctx, place, axis=0).reshape(span_total, K, SPAN, heads_here, HD)
    slot_stats = jnp.take(back_stats, place, axis=0).reshape(span_total, K, heads_here, SPAN, 2)
    live_k = live.reshape(span_total, K)[:, :, None, None]
    slot_top = jnp.where(live_k, slot_stats[..., 0], -jnp.inf)
    best = jnp.max(slot_top, axis=1, keepdims=True)
    scale = jnp.where(live_k, jnp.exp(slot_top - best) * slot_stats[..., 1], 0.0)
    share = scale / jnp.sum(scale, axis=1, keepdims=True)
    share = jnp.transpose(share, (0, 1, 3, 2))[..., None]
    slot_vals = jnp.where(live_k[..., None], slot_ctx.astype(jnp.float32), 0.0)
    context = jnp.sum(share * slot_vals, axis=1)
    context = context.astype(jnp.bfloat16).reshape(tok_rows, row_width)
    contexts = lax.all_gather(context, "db", axis=0, tiled=False)
    out = jnp.einsum(
        "str,srf->tf", contexts, weight_cols, preferred_element_type=jnp.float32
    )
    return out.astype(jnp.bfloat16)


def solution(mesh):
    in_specs = (
        P("seq", None),
        P(None, "db"),
        P("db", None),
        P("seq", None, None, "db"),
        P("seq", None),
        P("seq", None),
        P("seq"),
    )
    out_specs = P("seq", "db")
    return jax.shard_map(
        on_device, mesh=mesh, in_specs=in_specs, out_specs=out_specs, check_vma=False
    )
```

```python
import functools
import math

import jax
import jax.numpy as jnp
from jax import lax
from jax.experimental import pallas as pl
from jax.experimental.pallas import tpu as pltpu
from jax.sharding import PartitionSpec as P

HD = 128
SPAN = 64
K = 2
CAP = 3
LANES = 128
MESH = pl.DeviceIdType.MESH


def slot_places(neighbour_shard, neighbour_count):
    own_shard = neighbour_shard.reshape(-1)
    slots = own_shard.shape[0]
    own_live = (
        jnp.arange(K, dtype=jnp.int32)[None, :] < neighbour_count[:, None]
    ).reshape(-1)
    same = (own_shard[None, :] == own_shard[:, None]) & own_live[None, :]
    earlier = jnp.arange(slots)[None, :] < jnp.arange(slots)[:, None]
    own_rank = jnp.minimum(jnp.sum((same & earlier).astype(jnp.int32), axis=1), CAP - 1)
    return own_live, own_shard * CAP + own_rank


def peer_copy(src, dst, send_sem, recv_sem, device):
    return pltpu.make_async_remote_copy(
        src_ref=src, dst_ref=dst, send_sem=send_sem, recv_sem=recv_sem,
        device_id=device, device_id_type=MESH,
    )


def out_kernel(n_seq, n_db, features, send_q, send_e, w_loc, recv_q, recv_e, w_cols,
               qs, qr, es, er, ws, wr, ls):
    me_s = lax.axis_index("seq")
    me_d = lax.axis_index("db")

    def w_src(d):
        return w_loc.at[:, pl.ds(pl.multiple_of(d * features, features), features)]

    barrier = pltpu.get_barrier_semaphore()

    @pl.loop(1, n_seq)
    def _(o):
        pl.semaphore_signal(barrier, inc=1, device_id=(lax.rem(me_s + o, n_seq), me_d),
                            device_id_type=MESH)

    @pl.loop(1, n_db)
    def _(o):
        pl.semaphore_signal(barrier, inc=1, device_id=(me_s, lax.rem(me_d + o, n_db)),
                            device_id_type=MESH)

    pl.semaphore_wait(barrier, (n_seq - 1) + (n_db - 1))

    own = [
        pltpu.make_async_copy(send_q.at[me_s], recv_q.at[me_s], ls.at[0]),
        pltpu.make_async_copy(send_e.at[me_s], recv_e.at[me_s], ls.at[1]),
        pltpu.make_async_copy(w_src(me_d), w_cols.at[me_d], ls.at[2]),
    ]
    for c in own:
        c.start()

    @pl.loop(1, n_db)
    def _(o):
        d = lax.rem(me_d + o, n_db)
        peer_copy(w_src(d), w_cols.at[me_d], ws.at[d], wr.at[me_d], (me_s, d)).start()

    @pl.loop(1, n_seq)
    def _(o):
        d = lax.rem(me_s + o, n_seq)
        peer_copy(send_e.at[d], recv_e.at[me_s], es.at[d], er.at[me_s], (d, me_d)).start()
        peer_copy(send_q.at[d], recv_q.at[me_s], qs.at[d], qr.at[me_s], (d, me_d)).start()

    for c in own:
        c.wait()

    @pl.loop(1, n_seq)
    def _(o):
        d = lax.rem(me_s + o, n_seq)
        s = lax.rem(me_s + n_seq - o, n_seq)
        peer_copy(send_e.at[d], recv_e.at[me_s], es.at[d], er.at[me_s], (d, me_d)).wait_send()
        peer_copy(send_q.at[d], recv_q.at[me_s], qs.at[d], qr.at[me_s], (d, me_d)).wait_send()
        peer_copy(send_e.at[me_s], recv_e.at[s], es.at[s], er.at[s], (s, me_d)).wait_recv()
        peer_copy(send_q.at[me_s], recv_q.at[s], qs.at[s], qr.at[s], (s, me_d)).wait_recv()

    @pl.loop(1, n_db)
    def _(o):
        d = lax.rem(me_d + o, n_db)
        s = lax.rem(me_d + n_db - o, n_db)
        peer_copy(w_src(d), w_cols.at[me_d], ws.at[d], wr.at[me_d], (me_s, d)).wait_send()
        peer_copy(w_src(me_d), w_cols.at[s], ws.at[s], wr.at[s], (me_s, s)).wait_recv()


def back_kernel(n_seq, ctx, stats, back_ctx, back_stats, cs, cr, ss, sr, ls):
    me_s = lax.axis_index("seq")
    me_d = lax.axis_index("db")
    barrier = pltpu.get_barrier_semaphore()

    @pl.loop(1, n_seq)
    def _(o):
        pl.semaphore_signal(barrier, inc=1, device_id=(lax.rem(me_s + o, n_seq), me_d),
                            device_id_type=MESH)

    pl.semaphore_wait(barrier, n_seq - 1)

    own = [
        pltpu.make_async_copy(ctx.at[me_s], back_ctx.at[me_s], ls.at[0]),
        pltpu.make_async_copy(stats.at[me_s], back_stats.at[me_s], ls.at[1]),
    ]
    for c in own:
        c.start()

    @pl.loop(1, n_seq)
    def _(o):
        d = lax.rem(me_s + o, n_seq)
        peer_copy(stats.at[d], back_stats.at[me_s], ss.at[d], sr.at[me_s], (d, me_d)).start()
        peer_copy(ctx.at[d], back_ctx.at[me_s], cs.at[d], cr.at[me_s], (d, me_d)).start()

    for c in own:
        c.wait()

    @pl.loop(1, n_seq)
    def _(o):
        d = lax.rem(me_s + o, n_seq)
        s = lax.rem(me_s + n_seq - o, n_seq)
        peer_copy(stats.at[d], back_stats.at[me_s], ss.at[d], sr.at[me_s], (d, me_d)).wait_send()
        peer_copy(ctx.at[d], back_ctx.at[me_s], cs.at[d], cr.at[me_s], (d, me_d)).wait_send()
        peer_copy(stats.at[me_s], back_stats.at[s], ss.at[s], sr.at[s], (s, me_d)).wait_recv()
        peer_copy(ctx.at[me_s], back_ctx.at[s], cs.at[s], cr.at[s], (s, me_d)).wait_recv()


def any_spec():
    return pl.BlockSpec(memory_space=pl.ANY)


def exchange_out(send_q, send_e, w_loc, n_seq, n_db):
    features = w_loc.shape[1] // n_db
    dma = pltpu.SemaphoreType.DMA
    return pl.pallas_call(
        functools.partial(out_kernel, n_seq, n_db, features),
        out_shape=(
            jax.ShapeDtypeStruct(send_q.shape, send_q.dtype),
            jax.ShapeDtypeStruct(send_e.shape, send_e.dtype),
            jax.ShapeDtypeStruct((n_db, w_loc.shape[0], features), w_loc.dtype),
        ),
        in_specs=[any_spec()] * 3,
        out_specs=(any_spec(), any_spec(), any_spec()),
        scratch_shapes=[
            dma((n_seq,)), dma((n_seq,)), dma((n_seq,)), dma((n_seq,)),
            dma((n_db,)), dma((n_db,)), dma((3,)),
        ],
        compiler_params=pltpu.CompilerParams(collective_id=0, has_side_effects=True),
    )(send_q, send_e, w_loc)


def exchange_back(ctx, stats, n_seq):
    dma = pltpu.SemaphoreType.DMA
    return pl.pallas_call(
        functools.partial(back_kernel, n_seq),
        out_shape=(
            jax.ShapeDtypeStruct(ctx.shape, ctx.dtype),
            jax.ShapeDtypeStruct(stats.shape, stats.dtype),
        ),
        in_specs=[any_spec()] * 2,
        out_specs=(any_spec(), any_spec()),
        scratch_shapes=[dma((n_seq,)), dma((n_seq,)), dma((n_seq,)), dma((n_seq,)), dma((2,))],
        compiler_params=pltpu.CompilerParams(collective_id=1, has_side_effects=True),
    )(ctx, stats)


def on_device(
    decoder_states,
    query_weight,
    output_weight,
    neighbour_kv,
    neighbour_shard,
    neighbour_entry,
    neighbour_count,
):
    tok_rows = decoder_states.shape[0]
    span_total = tok_rows // SPAN
    row_width = query_weight.shape[1]
    heads_here = row_width // HD
    key_len = neighbour_kv.shape[1]
    n_seq = lax.psum(1, "seq")
    n_db = lax.psum(1, "db")
    places_total = n_seq * CAP
    queries = jnp.dot(decoder_states, query_weight, preferred_element_type=jnp.float32).astype(
        jnp.bfloat16
    )
    queries = queries.reshape(span_total, SPAN, row_width)

    live, place = slot_places(neighbour_shard, neighbour_count)
    target = jnp.where(live, place, places_total)
    span_of_slot = jnp.arange(span_total * K, dtype=jnp.int32) // K
    send_q = jnp.zeros((places_total, SPAN, row_width), jnp.bfloat16)
    send_q = send_q.at[target].set(queries[span_of_slot], mode="drop")
    send_e = jnp.zeros((places_total,), jnp.int32)
    send_e = send_e.at[target].set(neighbour_entry.reshape(-1), mode="drop")
    send_e = jnp.pad(send_e.reshape(n_seq, CAP), ((0, 0), (0, LANES - CAP)))
    recv_q, recv_e, weight_cols = exchange_out(
        send_q.reshape(n_seq, CAP, SPAN, row_width), send_e, output_weight, n_seq, n_db
    )
    recv_q = recv_q.reshape(places_total, SPAN, heads_here, HD)
    recv_e = recv_e[:, :CAP].reshape(-1)

    blocks = jnp.take(neighbour_kv, recv_e, axis=0)
    blocks = blocks.reshape(places_total, key_len, 2, heads_here, HD)
    key_rows = blocks[:, :, 0]
    val_rows = blocks[:, :, 1]
    scores = jnp.einsum(
        "pqhd,pnhd->phqn", recv_q, key_rows, preferred_element_type=jnp.float32
    ) * (1.0 / math.sqrt(HD))
    top = jnp.max(scores, axis=3, keepdims=True)
    weights = jnp.exp(scores - top)
    total = jnp.sum(weights, axis=3, keepdims=True)
    part = jnp.einsum(
        "phqn,pnhd->pqhd", weights.astype(jnp.bfloat16), val_rows,
        preferred_element_type=jnp.float32,
    )
    part = part / jnp.transpose(total, (0, 2, 1, 3))
    stats = jnp.concatenate([top, total], axis=3)
    back_ctx, back_stats = exchange_back(
        part.astype(jnp.bfloat16).reshape(n_seq, CAP, SPAN, row_width),
        stats.reshape(n_seq, CAP * heads_here * SPAN * 2 // LANES, LANES),
        n_seq,
    )
    back_ctx = back_ctx.reshape(places_total, SPAN, heads_here, HD)
    back_stats = back_stats.reshape(places_total, heads_here, SPAN, 2)

    slot_ctx = jnp.take(back_ctx, place, axis=0).reshape(span_total, K, SPAN, heads_here, HD)
    slot_stats = jnp.take(back_stats, place, axis=0).reshape(span_total, K, heads_here, SPAN, 2)
    live_k = live.reshape(span_total, K)[:, :, None, None]
    slot_top = jnp.where(live_k, slot_stats[..., 0], -jnp.inf)
    best = jnp.max(slot_top, axis=1, keepdims=True)
    scale = jnp.where(live_k, jnp.exp(slot_top - best) * slot_stats[..., 1], 0.0)
    share = scale / jnp.sum(scale, axis=1, keepdims=True)
    share = jnp.transpose(share, (0, 1, 3, 2))[..., None]
    slot_vals = jnp.where(live_k[..., None], slot_ctx.astype(jnp.float32), 0.0)
    context = jnp.sum(share * slot_vals, axis=1)
    context = context.astype(jnp.bfloat16).reshape(tok_rows, row_width)

    contexts = lax.all_gather(context, "db", axis=0, tiled=False)
    out = jnp.einsum(
        "str,srf->tf", contexts, weight_cols, preferred_element_type=jnp.float32
    )
    return out.astype(jnp.bfloat16)


def solution(mesh):
    in_specs = (
        P("seq", None),
        P(None, "db"),
        P("db", None),
        P("seq", None, None, "db"),
        P("seq", None),
        P("seq", None),
        P("seq"),
    )
    out_specs = P("seq", "db")
    return jax.shard_map(
        on_device, mesh=mesh, in_specs=in_specs, out_specs=out_specs, check_vma=False
    )
```

```python
import functools
import math

import jax
import jax.numpy as jnp
from jax import lax
from jax.experimental import pallas as pl
from jax.experimental.pallas import tpu as pltpu
from jax.sharding import PartitionSpec as P

HD = 128
SPAN = 64
K = 2
CAP = 3
LANES = 128
MESH = pl.DeviceIdType.MESH


def slot_places(neighbour_shard, neighbour_count):
    own_shard = neighbour_shard.reshape(-1)
    slots = own_shard.shape[0]
    own_live = (
        jnp.arange(K, dtype=jnp.int32)[None, :] < neighbour_count[:, None]
    ).reshape(-1)
    same = (own_shard[None, :] == own_shard[:, None]) & own_live[None, :]
    earlier = jnp.arange(slots)[None, :] < jnp.arange(slots)[:, None]
    own_rank = jnp.minimum(jnp.sum((same & earlier).astype(jnp.int32), axis=1), CAP - 1)
    return own_live, own_shard * CAP + own_rank


def peer_copy(src, dst, send_sem, recv_sem, device):
    return pltpu.make_async_remote_copy(
        src_ref=src, dst_ref=dst, send_sem=send_sem, recv_sem=recv_sem,
        device_id=device, device_id_type=MESH,
    )


def out_kernel(n_seq, n_db, features, send_q, send_e, w_loc, recv_q, recv_e, w_cols,
               qs, qr, es, er, ws, wr, ls):
    me_s = lax.axis_index("seq")
    me_d = lax.axis_index("db")

    def w_src(d):
        return w_loc.at[:, pl.ds(pl.multiple_of(d * features, features), features)]

    barrier = pltpu.get_barrier_semaphore()

    @pl.loop(1, n_seq)
    def _(o):
        pl.semaphore_signal(barrier, inc=1, device_id=(lax.rem(me_s + o, n_seq), me_d),
                            device_id_type=MESH)

    @pl.loop(1, n_db)
    def _(o):
        pl.semaphore_signal(barrier, inc=1, device_id=(me_s, lax.rem(me_d + o, n_db)),
                            device_id_type=MESH)

    pl.semaphore_wait(barrier, (n_seq - 1) + (n_db - 1))

    own = [
        pltpu.make_async_copy(send_q.at[me_s], recv_q.at[me_s], ls.at[0]),
        pltpu.make_async_copy(send_e.at[me_s], recv_e.at[me_s], ls.at[1]),
        pltpu.make_async_copy(w_src(me_d), w_cols.at[me_d], ls.at[2]),
    ]
    for c in own:
        c.start()

    @pl.loop(1, n_db)
    def _(o):
        d = lax.rem(me_d + o, n_db)
        peer_copy(w_src(d), w_cols.at[me_d], ws.at[d], wr.at[me_d], (me_s, d)).start()

    @pl.loop(1, n_seq)
    def _(o):
        d = lax.rem(me_s + o, n_seq)
        peer_copy(send_e.at[d], recv_e.at[me_s], es.at[d], er.at[me_s], (d, me_d)).start()
        peer_copy(send_q.at[d], recv_q.at[me_s], qs.at[d], qr.at[me_s], (d, me_d)).start()

    for c in own:
        c.wait()

    @pl.loop(1, n_seq)
    def _(o):
        d = lax.rem(me_s + o, n_seq)
        s = lax.rem(me_s + n_seq - o, n_seq)
        peer_copy(send_e.at[d], recv_e.at[me_s], es.at[d], er.at[me_s], (d, me_d)).wait_send()
        peer_copy(send_q.at[d], recv_q.at[me_s], qs.at[d], qr.at[me_s], (d, me_d)).wait_send()
        peer_copy(send_e.at[me_s], recv_e.at[s], es.at[s], er.at[s], (s, me_d)).wait_recv()
        peer_copy(send_q.at[me_s], recv_q.at[s], qs.at[s], qr.at[s], (s, me_d)).wait_recv()

    @pl.loop(1, n_db)
    def _(o):
        d = lax.rem(me_d + o, n_db)
        s = lax.rem(me_d + n_db - o, n_db)
        peer_copy(w_src(d), w_cols.at[me_d], ws.at[d], wr.at[me_d], (me_s, d)).wait_send()
        peer_copy(w_src(me_d), w_cols.at[s], ws.at[s], wr.at[s], (me_s, s)).wait_recv()


def back_kernel(n_seq, ctx, stats, back_ctx, back_stats, cs, cr, ss, sr, ls):
    me_s = lax.axis_index("seq")
    me_d = lax.axis_index("db")
    barrier = pltpu.get_barrier_semaphore()

    @pl.loop(1, n_seq)
    def _(o):
        pl.semaphore_signal(barrier, inc=1, device_id=(lax.rem(me_s + o, n_seq), me_d),
                            device_id_type=MESH)

    pl.semaphore_wait(barrier, n_seq - 1)

    own = [
        pltpu.make_async_copy(ctx.at[me_s], back_ctx.at[me_s], ls.at[0]),
        pltpu.make_async_copy(stats.at[me_s], back_stats.at[me_s], ls.at[1]),
    ]
    for c in own:
        c.start()

    @pl.loop(1, n_seq)
    def _(o):
        d = lax.rem(me_s + o, n_seq)
        peer_copy(stats.at[d], back_stats.at[me_s], ss.at[d], sr.at[me_s], (d, me_d)).start()
        peer_copy(ctx.at[d], back_ctx.at[me_s], cs.at[d], cr.at[me_s], (d, me_d)).start()

    for c in own:
        c.wait()

    @pl.loop(1, n_seq)
    def _(o):
        d = lax.rem(me_s + o, n_seq)
        s = lax.rem(me_s + n_seq - o, n_seq)
        peer_copy(stats.at[d], back_stats.at[me_s], ss.at[d], sr.at[me_s], (d, me_d)).wait_send()
        peer_copy(ctx.at[d], back_ctx.at[me_s], cs.at[d], cr.at[me_s], (d, me_d)).wait_send()
        peer_copy(stats.at[me_s], back_stats.at[s], ss.at[s], sr.at[s], (s, me_d)).wait_recv()
        peer_copy(ctx.at[me_s], back_ctx.at[s], cs.at[s], cr.at[s], (s, me_d)).wait_recv()


def attend_kernel(scale, heads, e_ref, q_ref, kv0, kv1, kv2, ctx_ref, stats_ref):
    for j, kv_ref in enumerate((kv0, kv1, kv2)):
        width = heads * HD
        for h in range(heads):
            q = q_ref[0, j, :, h * HD:(h + 1) * HD]
            k = kv_ref[0, :, h * HD:(h + 1) * HD]
            v = kv_ref[0, :, width + h * HD:width + (h + 1) * HD]
            s = lax.dot_general(
                q, k, (((1,), (1,)), ((), ())), preferred_element_type=jnp.float32
            ) * scale
            top = jnp.max(s, axis=1, keepdims=True)
            w = jnp.exp(s - top)
            total = jnp.sum(w, axis=1, keepdims=True)
            ctx = jnp.dot(w.astype(jnp.bfloat16), v, preferred_element_type=jnp.float32)
            ctx_ref[0, j, :, h * HD:(h + 1) * HD] = (ctx / total).astype(ctx_ref.dtype)
            stats_ref[0, j, :, 2 * h:2 * h + 1] = top
            stats_ref[0, j, :, 2 * h + 1:2 * h + 2] = total


def attend(recv_q, recv_e, kv_flat, heads):
    n_src, cap, span, width = recv_q.shape
    key_len = kv_flat.shape[1]

    def kv_spec(j):
        return pl.BlockSpec((1, key_len, kv_flat.shape[2]), lambda i, e: (e[i * CAP + j], 0, 0))

    grid_spec = pltpu.PrefetchScalarGridSpec(
        num_scalar_prefetch=1,
        grid=(n_src,),
        in_specs=[pl.BlockSpec((1, cap, span, width), lambda i, e: (i, 0, 0, 0))]
        + [kv_spec(j) for j in range(CAP)],
        out_specs=[
            pl.BlockSpec((1, cap, span, width), lambda i, e: (i, 0, 0, 0)),
            pl.BlockSpec((1, cap, span, 2 * heads), lambda i, e: (i, 0, 0, 0)),
        ],
    )
    return pl.pallas_call(
        functools.partial(attend_kernel, 1.0 / math.sqrt(HD), heads),
        grid_spec=grid_spec,
        out_shape=(
            jax.ShapeDtypeStruct(recv_q.shape, jnp.bfloat16),
            jax.ShapeDtypeStruct((n_src, cap, span, 2 * heads), jnp.float32),
        ),
    )(recv_e, recv_q, kv_flat, kv_flat, kv_flat)


def any_spec():
    return pl.BlockSpec(memory_space=pl.ANY)


def exchange_out(send_q, send_e, w_loc, n_seq, n_db):
    features = w_loc.shape[1] // n_db
    dma = pltpu.SemaphoreType.DMA
    return pl.pallas_call(
        functools.partial(out_kernel, n_seq, n_db, features),
        out_shape=(
            jax.ShapeDtypeStruct(send_q.shape, send_q.dtype),
            jax.ShapeDtypeStruct(send_e.shape, send_e.dtype),
            jax.ShapeDtypeStruct((n_db, w_loc.shape[0], features), w_loc.dtype),
        ),
        in_specs=[any_spec()] * 3,
        out_specs=(any_spec(), any_spec(), any_spec()),
        scratch_shapes=[
            dma((n_seq,)), dma((n_seq,)), dma((n_seq,)), dma((n_seq,)),
            dma((n_db,)), dma((n_db,)), dma((3,)),
        ],
        compiler_params=pltpu.CompilerParams(collective_id=0, has_side_effects=True),
    )(send_q, send_e, w_loc)


def exchange_back(ctx, stats, n_seq):
    dma = pltpu.SemaphoreType.DMA
    return pl.pallas_call(
        functools.partial(back_kernel, n_seq),
        out_shape=(
            jax.ShapeDtypeStruct(ctx.shape, ctx.dtype),
            jax.ShapeDtypeStruct(stats.shape, stats.dtype),
        ),
        in_specs=[any_spec()] * 2,
        out_specs=(any_spec(), any_spec()),
        scratch_shapes=[dma((n_seq,)), dma((n_seq,)), dma((n_seq,)), dma((n_seq,)), dma((2,))],
        compiler_params=pltpu.CompilerParams(collective_id=1, has_side_effects=True),
    )(ctx, stats)


def on_device(
    decoder_states,
    query_weight,
    output_weight,
    neighbour_kv,
    neighbour_shard,
    neighbour_entry,
    neighbour_count,
):
    tok_rows = decoder_states.shape[0]
    span_total = tok_rows // SPAN
    row_width = query_weight.shape[1]
    heads_here = row_width // HD
    key_len = neighbour_kv.shape[1]
    n_seq = lax.psum(1, "seq")
    n_db = lax.psum(1, "db")
    places_total = n_seq * CAP
    queries = jnp.dot(decoder_states, query_weight, preferred_element_type=jnp.float32).astype(
        jnp.bfloat16
    )
    queries = queries.reshape(span_total, SPAN, row_width)

    live, place = slot_places(neighbour_shard, neighbour_count)
    target = jnp.where(live, place, places_total)
    span_of_slot = jnp.arange(span_total * K, dtype=jnp.int32) // K
    send_q = jnp.zeros((places_total, SPAN, row_width), jnp.bfloat16)
    send_q = send_q.at[target].set(queries[span_of_slot], mode="drop")
    send_e = jnp.zeros((places_total,), jnp.int32)
    send_e = send_e.at[target].set(neighbour_entry.reshape(-1), mode="drop")
    send_e = jnp.pad(send_e.reshape(n_seq, CAP), ((0, 0), (0, LANES - CAP)))
    recv_q, recv_e, weight_cols = exchange_out(
        send_q.reshape(n_seq, CAP, SPAN, row_width), send_e, output_weight, n_seq, n_db
    )
    recv_e = recv_e[:, :CAP].reshape(-1)
    kv_flat = neighbour_kv.reshape(neighbour_kv.shape[0], key_len, 2 * row_width)
    part, stats = attend(recv_q, recv_e, kv_flat, heads_here)
    back_ctx, back_stats = exchange_back(
        part, stats.reshape(n_seq, CAP * SPAN * 2 * heads_here // LANES, LANES), n_seq
    )
    back_ctx = back_ctx.reshape(places_total, SPAN, heads_here, HD)
    back_stats = back_stats.reshape(places_total, SPAN, heads_here, 2)

    slot_ctx = jnp.take(back_ctx, place, axis=0).reshape(span_total, K, SPAN, heads_here, HD)
    slot_stats = jnp.take(back_stats, place, axis=0).reshape(span_total, K, SPAN, heads_here, 2)
    live_k = live.reshape(span_total, K)[:, :, None, None]
    slot_top = jnp.where(live_k, slot_stats[..., 0], -jnp.inf)
    best = jnp.max(slot_top, axis=1, keepdims=True)
    scale = jnp.where(live_k, jnp.exp(slot_top - best) * slot_stats[..., 1], 0.0)
    share = (scale / jnp.sum(scale, axis=1, keepdims=True))[..., None]
    slot_vals = jnp.where(live_k[..., None], slot_ctx.astype(jnp.float32), 0.0)
    context = jnp.sum(share * slot_vals, axis=1)
    context = context.astype(jnp.bfloat16).reshape(tok_rows, row_width)

    contexts = lax.all_gather(context, "db", axis=0, tiled=False)
    out = jnp.einsum(
        "str,srf->tf", contexts, weight_cols, preferred_element_type=jnp.float32
    )
    return out.astype(jnp.bfloat16)


def solution(mesh):
    in_specs = (
        P("seq", None),
        P(None, "db"),
        P("db", None),
        P("seq", None, None, "db"),
        P("seq", None),
        P("seq", None),
        P("seq"),
    )
    out_specs = P("seq", "db")
    return jax.shard_map(
        on_device, mesh=mesh, in_specs=in_specs, out_specs=out_specs, check_vma=False
    )
```

```python
import functools
import math

import jax
import jax.numpy as jnp
from jax import lax
from jax.experimental import pallas as pl
from jax.experimental.pallas import tpu as pltpu
from jax.sharding import PartitionSpec as P

HD = 128
SPAN = 64
K = 2
CAP = 3
LANES = 128
MESH = pl.DeviceIdType.MESH


def slot_places(neighbour_shard, neighbour_count):
    own_shard = neighbour_shard.reshape(-1)
    slots = own_shard.shape[0]
    own_live = (
        jnp.arange(K, dtype=jnp.int32)[None, :] < neighbour_count[:, None]
    ).reshape(-1)
    same = (own_shard[None, :] == own_shard[:, None]) & own_live[None, :]
    earlier = jnp.arange(slots)[None, :] < jnp.arange(slots)[:, None]
    own_rank = jnp.minimum(jnp.sum((same & earlier).astype(jnp.int32), axis=1), CAP - 1)
    return own_live, own_shard * CAP + own_rank


def peer_copy(src, dst, send_sem, recv_sem, device):
    return pltpu.make_async_remote_copy(
        src_ref=src, dst_ref=dst, send_sem=send_sem, recv_sem=recv_sem,
        device_id=device, device_id_type=MESH,
    )


def out_kernel(n_seq, n_db, features, send_q, send_e, w_loc, recv_q, recv_e, w_cols,
               qs, qr, es, er, ws, wr, ls):
    me_s = lax.axis_index("seq")
    me_d = lax.axis_index("db")

    def w_src(d):
        return w_loc.at[:, pl.ds(pl.multiple_of(d * features, features), features)]

    barrier = pltpu.get_barrier_semaphore()

    @pl.loop(1, n_seq)
    def _(o):
        pl.semaphore_signal(barrier, inc=1, device_id=(lax.rem(me_s + o, n_seq), me_d),
                            device_id_type=MESH)

    @pl.loop(1, n_db)
    def _(o):
        pl.semaphore_signal(barrier, inc=1, device_id=(me_s, lax.rem(me_d + o, n_db)),
                            device_id_type=MESH)

    pl.semaphore_wait(barrier, (n_seq - 1) + (n_db - 1))

    own = [
        pltpu.make_async_copy(send_q.at[me_s], recv_q.at[me_s], ls.at[0]),
        pltpu.make_async_copy(send_e.at[me_s], recv_e.at[me_s], ls.at[1]),
        pltpu.make_async_copy(w_src(me_d), w_cols.at[me_d], ls.at[2]),
    ]
    for c in own:
        c.start()

    @pl.loop(1, n_db)
    def _(o):
        d = lax.rem(me_d + o, n_db)
        peer_copy(w_src(d), w_cols.at[me_d], ws.at[d], wr.at[me_d], (me_s, d)).start()

    @pl.loop(1, n_seq)
    def _(o):
        d = lax.rem(me_s + o, n_seq)
        peer_copy(send_e.at[d], recv_e.at[me_s], es.at[d], er.at[me_s], (d, me_d)).start()
        peer_copy(send_q.at[d], recv_q.at[me_s], qs.at[d], qr.at[me_s], (d, me_d)).start()

    for c in own:
        c.wait()

    @pl.loop(1, n_seq)
    def _(o):
        d = lax.rem(me_s + o, n_seq)
        s = lax.rem(me_s + n_seq - o, n_seq)
        peer_copy(send_e.at[d], recv_e.at[me_s], es.at[d], er.at[me_s], (d, me_d)).wait_send()
        peer_copy(send_q.at[d], recv_q.at[me_s], qs.at[d], qr.at[me_s], (d, me_d)).wait_send()
        peer_copy(send_e.at[me_s], recv_e.at[s], es.at[s], er.at[s], (s, me_d)).wait_recv()
        peer_copy(send_q.at[me_s], recv_q.at[s], qs.at[s], qr.at[s], (s, me_d)).wait_recv()

    @pl.loop(1, n_db)
    def _(o):
        d = lax.rem(me_d + o, n_db)
        s = lax.rem(me_d + n_db - o, n_db)
        peer_copy(w_src(d), w_cols.at[me_d], ws.at[d], wr.at[me_d], (me_s, d)).wait_send()
        peer_copy(w_src(me_d), w_cols.at[s], ws.at[s], wr.at[s], (me_s, s)).wait_recv()


def back_kernel(n_seq, ctx, stats, back_ctx, back_stats, cs, cr, ss, sr, ls):
    me_s = lax.axis_index("seq")
    me_d = lax.axis_index("db")
    barrier = pltpu.get_barrier_semaphore()

    @pl.loop(1, n_seq)
    def _(o):
        pl.semaphore_signal(barrier, inc=1, device_id=(lax.rem(me_s + o, n_seq), me_d),
                            device_id_type=MESH)

    pl.semaphore_wait(barrier, n_seq - 1)

    own = [
        pltpu.make_async_copy(ctx.at[me_s], back_ctx.at[me_s], ls.at[0]),
        pltpu.make_async_copy(stats.at[me_s], back_stats.at[me_s], ls.at[1]),
    ]
    for c in own:
        c.start()

    @pl.loop(1, n_seq)
    def _(o):
        d = lax.rem(me_s + o, n_seq)
        peer_copy(stats.at[d], back_stats.at[me_s], ss.at[d], sr.at[me_s], (d, me_d)).start()
        peer_copy(ctx.at[d], back_ctx.at[me_s], cs.at[d], cr.at[me_s], (d, me_d)).start()

    for c in own:
        c.wait()

    @pl.loop(1, n_seq)
    def _(o):
        d = lax.rem(me_s + o, n_seq)
        s = lax.rem(me_s + n_seq - o, n_seq)
        peer_copy(stats.at[d], back_stats.at[me_s], ss.at[d], sr.at[me_s], (d, me_d)).wait_send()
        peer_copy(ctx.at[d], back_ctx.at[me_s], cs.at[d], cr.at[me_s], (d, me_d)).wait_send()
        peer_copy(stats.at[me_s], back_stats.at[s], ss.at[s], sr.at[s], (s, me_d)).wait_recv()
        peer_copy(ctx.at[me_s], back_ctx.at[s], cs.at[s], cr.at[s], (s, me_d)).wait_recv()


def attend_kernel(scale, heads, e_ref, q_ref, kv0, kv1, kv2, ctx_ref, stats_ref):
    for j, kv_ref in enumerate((kv0, kv1, kv2)):
        width = heads * HD
        for h in range(heads):
            q = q_ref[0, j, :, h * HD:(h + 1) * HD]
            k = kv_ref[0, :, h * HD:(h + 1) * HD]
            v = kv_ref[0, :, width + h * HD:width + (h + 1) * HD]
            s = lax.dot_general(
                q, k, (((1,), (1,)), ((), ())), preferred_element_type=jnp.float32
            ) * scale
            top = jnp.max(s, axis=1, keepdims=True)
            w = jnp.exp(s - top)
            total = jnp.sum(w, axis=1, keepdims=True)
            ctx = jnp.dot(w.astype(jnp.bfloat16), v, preferred_element_type=jnp.float32)
            ctx_ref[0, j, :, h * HD:(h + 1) * HD] = (ctx / total).astype(ctx_ref.dtype)
            stats_ref[0, j, :, 2 * h:2 * h + 1] = top
            stats_ref[0, j, :, 2 * h + 1:2 * h + 2] = total


def attend(recv_q, recv_e, kv_flat, heads):
    n_src, cap, span, width = recv_q.shape
    key_len = kv_flat.shape[1]

    def kv_spec(j):
        return pl.BlockSpec((1, key_len, kv_flat.shape[2]), lambda i, e: (e[i * CAP + j], 0, 0))

    grid_spec = pltpu.PrefetchScalarGridSpec(
        num_scalar_prefetch=1,
        grid=(n_src,),
        in_specs=[pl.BlockSpec((1, cap, span, width), lambda i, e: (i, 0, 0, 0))]
        + [kv_spec(j) for j in range(CAP)],
        out_specs=[
            pl.BlockSpec((1, cap, span, width), lambda i, e: (i, 0, 0, 0)),
            pl.BlockSpec((1, cap, span, 2 * heads), lambda i, e: (i, 0, 0, 0)),
        ],
    )
    return pl.pallas_call(
        functools.partial(attend_kernel, 1.0 / math.sqrt(HD), heads),
        grid_spec=grid_spec,
        out_shape=(
            jax.ShapeDtypeStruct(recv_q.shape, jnp.bfloat16),
            jax.ShapeDtypeStruct((n_src, cap, span, 2 * heads), jnp.float32),
        ),
    )(recv_e, recv_q, kv_flat, kv_flat, kv_flat)


def combine_kernel(heads, place_ref, count_ref, c0, c1, s0, s1, out_ref):
    live1 = count_ref[pl.program_id(0)] > 1
    for h in range(heads):
        cols = slice(h * HD, (h + 1) * HD)
        m0 = s0[0, :, 2 * h:2 * h + 1]
        l0 = s0[0, :, 2 * h + 1:2 * h + 2]
        m1 = s1[0, :, 2 * h:2 * h + 1]
        l1 = s1[0, :, 2 * h + 1:2 * h + 2]
        best = jnp.where(live1, jnp.maximum(m0, m1), m0)
        a0 = jnp.exp(m0 - best) * l0
        a1 = jnp.where(live1, jnp.exp(m1 - best) * l1, 0.0)
        v0 = c0[0, :, cols].astype(jnp.float32)
        v1 = jnp.where(live1, c1[0, :, cols].astype(jnp.float32), 0.0)
        out_ref[0, :, cols] = ((a0 * v0 + a1 * v1) / (a0 + a1)).astype(out_ref.dtype)


def combine(back_ctx, back_stats, place, neighbour_count, heads):
    places, span, width = back_ctx.shape
    spans = neighbour_count.shape[0]

    def by_place(k, shape):
        return pl.BlockSpec((1,) + shape, lambda c, p, n: (p[c * K + k], 0, 0))

    grid_spec = pltpu.PrefetchScalarGridSpec(
        num_scalar_prefetch=2,
        grid=(spans,),
        in_specs=[by_place(0, (span, width)), by_place(1, (span, width)),
                  by_place(0, (span, 2 * heads)), by_place(1, (span, 2 * heads))],
        out_specs=pl.BlockSpec((1, span, width), lambda c, p, n: (c, 0, 0)),
    )
    return pl.pallas_call(
        functools.partial(combine_kernel, heads),
        grid_spec=grid_spec,
        out_shape=jax.ShapeDtypeStruct((spans, span, width), jnp.bfloat16),
    )(place, neighbour_count, back_ctx, back_ctx, back_stats, back_stats)


def any_spec():
    return pl.BlockSpec(memory_space=pl.ANY)


def exchange_out(send_q, send_e, w_loc, n_seq, n_db):
    features = w_loc.shape[1] // n_db
    dma = pltpu.SemaphoreType.DMA
    return pl.pallas_call(
        functools.partial(out_kernel, n_seq, n_db, features),
        out_shape=(
            jax.ShapeDtypeStruct(send_q.shape, send_q.dtype),
            jax.ShapeDtypeStruct(send_e.shape, send_e.dtype),
            jax.ShapeDtypeStruct((n_db, w_loc.shape[0], features), w_loc.dtype),
        ),
        in_specs=[any_spec()] * 3,
        out_specs=(any_spec(), any_spec(), any_spec()),
        scratch_shapes=[
            dma((n_seq,)), dma((n_seq,)), dma((n_seq,)), dma((n_seq,)),
            dma((n_db,)), dma((n_db,)), dma((3,)),
        ],
        compiler_params=pltpu.CompilerParams(collective_id=0, has_side_effects=True),
    )(send_q, send_e, w_loc)


def exchange_back(ctx, stats, n_seq):
    dma = pltpu.SemaphoreType.DMA
    return pl.pallas_call(
        functools.partial(back_kernel, n_seq),
        out_shape=(
            jax.ShapeDtypeStruct(ctx.shape, ctx.dtype),
            jax.ShapeDtypeStruct(stats.shape, stats.dtype),
        ),
        in_specs=[any_spec()] * 2,
        out_specs=(any_spec(), any_spec()),
        scratch_shapes=[dma((n_seq,)), dma((n_seq,)), dma((n_seq,)), dma((n_seq,)), dma((2,))],
        compiler_params=pltpu.CompilerParams(collective_id=1, has_side_effects=True),
    )(ctx, stats)


def on_device(
    decoder_states,
    query_weight,
    output_weight,
    neighbour_kv,
    neighbour_shard,
    neighbour_entry,
    neighbour_count,
):
    tok_rows = decoder_states.shape[0]
    span_total = tok_rows // SPAN
    row_width = query_weight.shape[1]
    heads_here = row_width // HD
    key_len = neighbour_kv.shape[1]
    n_seq = lax.psum(1, "seq")
    n_db = lax.psum(1, "db")
    places_total = n_seq * CAP
    queries = jnp.dot(decoder_states, query_weight, preferred_element_type=jnp.float32).astype(
        jnp.bfloat16
    )
    queries = queries.reshape(span_total, SPAN, row_width)

    live, place = slot_places(neighbour_shard, neighbour_count)
    target = jnp.where(live, place, places_total)
    span_of_slot = jnp.arange(span_total * K, dtype=jnp.int32) // K
    send_q = jnp.zeros((places_total, SPAN, row_width), jnp.bfloat16)
    send_q = send_q.at[target].set(queries[span_of_slot], mode="drop")
    send_e = jnp.zeros((places_total,), jnp.int32)
    send_e = send_e.at[target].set(neighbour_entry.reshape(-1), mode="drop")
    send_e = jnp.pad(send_e.reshape(n_seq, CAP), ((0, 0), (0, LANES - CAP)))
    recv_q, recv_e, weight_cols = exchange_out(
        send_q.reshape(n_seq, CAP, SPAN, row_width), send_e, output_weight, n_seq, n_db
    )
    recv_e = recv_e[:, :CAP].reshape(-1)
    kv_flat = neighbour_kv.reshape(neighbour_kv.shape[0], key_len, 2 * row_width)
    part, stats = attend(recv_q, recv_e, kv_flat, heads_here)
    back_ctx, back_stats = exchange_back(
        part, stats.reshape(n_seq, CAP * SPAN * 2 * heads_here // LANES, LANES), n_seq
    )
    back_ctx = back_ctx.reshape(places_total, SPAN, row_width)
    back_stats = back_stats.reshape(places_total, SPAN, 2 * heads_here)
    context = combine(back_ctx, back_stats, place, neighbour_count, heads_here)
    context = context.reshape(tok_rows, row_width)

    contexts = lax.all_gather(context, "db", axis=0, tiled=False)
    out = jnp.einsum(
        "str,srf->tf", contexts, weight_cols, preferred_element_type=jnp.float32
    )
    return out.astype(jnp.bfloat16)


def solution(mesh):
    in_specs = (
        P("seq", None),
        P(None, "db"),
        P("db", None),
        P("seq", None, None, "db"),
        P("seq", None),
        P("seq", None),
        P("seq"),
    )
    out_specs = P("seq", "db")
    return jax.shard_map(
        on_device, mesh=mesh, in_specs=in_specs, out_specs=out_specs, check_vma=False
    )
```

```python
import functools
import math

import jax
import jax.numpy as jnp
from jax import lax
from jax.experimental import pallas as pl
from jax.experimental.pallas import tpu as pltpu
from jax.sharding import PartitionSpec as P

HD = 128
SPAN = 64
K = 2
CAP = 3
LANES = 128
MESH = pl.DeviceIdType.MESH


def slot_places(neighbour_shard, neighbour_count):
    own_shard = neighbour_shard.reshape(-1)
    slots = own_shard.shape[0]
    own_live = (
        jnp.arange(K, dtype=jnp.int32)[None, :] < neighbour_count[:, None]
    ).reshape(-1)
    same = (own_shard[None, :] == own_shard[:, None]) & own_live[None, :]
    earlier = jnp.arange(slots)[None, :] < jnp.arange(slots)[:, None]
    own_rank = jnp.minimum(jnp.sum((same & earlier).astype(jnp.int32), axis=1), CAP - 1)
    return own_live, own_shard * CAP + own_rank


def peer_copy(src, dst, send_sem, recv_sem, device):
    return pltpu.make_async_remote_copy(
        src_ref=src, dst_ref=dst, send_sem=send_sem, recv_sem=recv_sem,
        device_id=device, device_id_type=MESH,
    )


def out_kernel(n_seq, n_db, features, send_q, send_e, w_loc, recv_q, recv_e, w_cols,
               qs, qr, es, er, ws, wr, ls):
    me_s = lax.axis_index("seq")
    me_d = lax.axis_index("db")

    def w_src(d):
        return w_loc.at[:, pl.ds(pl.multiple_of(d * features, features), features)]

    barrier = pltpu.get_barrier_semaphore()

    @pl.loop(1, n_seq)
    def _(o):
        pl.semaphore_signal(barrier, inc=1, device_id=(lax.rem(me_s + o, n_seq), me_d),
                            device_id_type=MESH)

    @pl.loop(1, n_db)
    def _(o):
        pl.semaphore_signal(barrier, inc=1, device_id=(me_s, lax.rem(me_d + o, n_db)),
                            device_id_type=MESH)

    pl.semaphore_wait(barrier, (n_seq - 1) + (n_db - 1))

    own = [
        pltpu.make_async_copy(send_q.at[me_s], recv_q.at[me_s], ls.at[0]),
        pltpu.make_async_copy(send_e.at[me_s], recv_e.at[me_s], ls.at[1]),
        pltpu.make_async_copy(w_src(me_d), w_cols.at[me_d], ls.at[2]),
    ]
    for c in own:
        c.start()

    @pl.loop(1, n_db)
    def _(o):
        d = lax.rem(me_d + o, n_db)
        peer_copy(w_src(d), w_cols.at[me_d], ws.at[d], wr.at[me_d], (me_s, d)).start()

    @pl.loop(1, n_seq)
    def _(o):
        d = lax.rem(me_s + o, n_seq)
        peer_copy(send_e.at[d], recv_e.at[me_s], es.at[d], er.at[me_s], (d, me_d)).start()
        peer_copy(send_q.at[d], recv_q.at[me_s], qs.at[d], qr.at[me_s], (d, me_d)).start()

    for c in own:
        c.wait()

    @pl.loop(1, n_seq)
    def _(o):
        d = lax.rem(me_s + o, n_seq)
        s = lax.rem(me_s + n_seq - o, n_seq)
        peer_copy(send_e.at[d], recv_e.at[me_s], es.at[d], er.at[me_s], (d, me_d)).wait_send()
        peer_copy(send_q.at[d], recv_q.at[me_s], qs.at[d], qr.at[me_s], (d, me_d)).wait_send()
        peer_copy(send_e.at[me_s], recv_e.at[s], es.at[s], er.at[s], (s, me_d)).wait_recv()
        peer_copy(send_q.at[me_s], recv_q.at[s], qs.at[s], qr.at[s], (s, me_d)).wait_recv()

    @pl.loop(1, n_db)
    def _(o):
        d = lax.rem(me_d + o, n_db)
        s = lax.rem(me_d + n_db - o, n_db)
        peer_copy(w_src(d), w_cols.at[me_d], ws.at[d], wr.at[me_d], (me_s, d)).wait_send()
        peer_copy(w_src(me_d), w_cols.at[s], ws.at[s], wr.at[s], (me_s, s)).wait_recv()


def back_kernel(n_seq, ctx, stats, back_ctx, back_stats, cs, cr, ss, sr, ls):
    me_s = lax.axis_index("seq")
    me_d = lax.axis_index("db")
    barrier = pltpu.get_barrier_semaphore()

    @pl.loop(1, n_seq)
    def _(o):
        pl.semaphore_signal(barrier, inc=1, device_id=(lax.rem(me_s + o, n_seq), me_d),
                            device_id_type=MESH)

    pl.semaphore_wait(barrier, n_seq - 1)

    own = [
        pltpu.make_async_copy(ctx.at[me_s], back_ctx.at[me_s], ls.at[0]),
        pltpu.make_async_copy(stats.at[me_s], back_stats.at[me_s], ls.at[1]),
    ]
    for c in own:
        c.start()

    @pl.loop(1, n_seq)
    def _(o):
        d = lax.rem(me_s + o, n_seq)
        peer_copy(stats.at[d], back_stats.at[me_s], ss.at[d], sr.at[me_s], (d, me_d)).start()
        peer_copy(ctx.at[d], back_ctx.at[me_s], cs.at[d], cr.at[me_s], (d, me_d)).start()

    for c in own:
        c.wait()

    @pl.loop(1, n_seq)
    def _(o):
        d = lax.rem(me_s + o, n_seq)
        s = lax.rem(me_s + n_seq - o, n_seq)
        peer_copy(stats.at[d], back_stats.at[me_s], ss.at[d], sr.at[me_s], (d, me_d)).wait_send()
        peer_copy(ctx.at[d], back_ctx.at[me_s], cs.at[d], cr.at[me_s], (d, me_d)).wait_send()
        peer_copy(stats.at[me_s], back_stats.at[s], ss.at[s], sr.at[s], (s, me_d)).wait_recv()
        peer_copy(ctx.at[me_s], back_ctx.at[s], cs.at[s], cr.at[s], (s, me_d)).wait_recv()


def attend_kernel(scale, heads, head, e_ref, q_ref, kv0, kv1, kv2, ctx_ref, stats_ref):
    for j, kv_ref in enumerate((kv0, kv1, kv2)):
        width = heads * HD
        for h in (head,):
            q = q_ref[0, j, :, h * HD:(h + 1) * HD]
            k = kv_ref[0, :, h * HD:(h + 1) * HD]
            v = kv_ref[0, :, width + h * HD:width + (h + 1) * HD]
            s = lax.dot_general(
                q, k, (((1,), (1,)), ((), ())), preferred_element_type=jnp.float32
            ) * scale
            top = jnp.max(s, axis=1, keepdims=True)
            w = jnp.exp(s - top)
            total = jnp.sum(w, axis=1, keepdims=True)
            ctx = jnp.dot(w.astype(jnp.bfloat16), v, preferred_element_type=jnp.float32)
            ctx_ref[0, j] = (ctx / total).astype(ctx_ref.dtype)
            stats_ref[0, j, :, 0:1] = top
            stats_ref[0, j, :, 1:2] = total


def attend(recv_q, recv_e, kv_flat, heads, head):
    n_src, cap, span, width = recv_q.shape
    key_len = kv_flat.shape[1]

    def kv_spec(j):
        return pl.BlockSpec((1, key_len, kv_flat.shape[2]), lambda i, e: (e[i * CAP + j], 0, 0))

    grid_spec = pltpu.PrefetchScalarGridSpec(
        num_scalar_prefetch=1,
        grid=(n_src,),
        in_specs=[pl.BlockSpec((1, cap, span, width), lambda i, e: (i, 0, 0, 0))]
        + [kv_spec(j) for j in range(CAP)],
        out_specs=[
            pl.BlockSpec((1, cap, span, HD), lambda i, e: (i, 0, 0, 0)),
            pl.BlockSpec((1, cap, span, 2), lambda i, e: (i, 0, 0, 0)),
        ],
    )
    return pl.pallas_call(
        functools.partial(attend_kernel, 1.0 / math.sqrt(HD), heads, head),
        grid_spec=grid_spec,
        out_shape=(
            jax.ShapeDtypeStruct((n_src, cap, span, HD), jnp.bfloat16),
            jax.ShapeDtypeStruct((n_src, cap, span, 2), jnp.float32),
        ),
    )(recv_e, recv_q, kv_flat, kv_flat, kv_flat)


def combine_kernel(heads, place_ref, count_ref, c0, c1, s0, s1, out_ref):
    live1 = count_ref[pl.program_id(0)] > 1
    for h in range(heads):
        cols = slice(h * HD, (h + 1) * HD)
        m0 = s0[0, :, 2 * h:2 * h + 1]
        l0 = s0[0, :, 2 * h + 1:2 * h + 2]
        m1 = s1[0, :, 2 * h:2 * h + 1]
        l1 = s1[0, :, 2 * h + 1:2 * h + 2]
        best = jnp.where(live1, jnp.maximum(m0, m1), m0)
        a0 = jnp.exp(m0 - best) * l0
        a1 = jnp.where(live1, jnp.exp(m1 - best) * l1, 0.0)
        v0 = c0[0, :, cols].astype(jnp.float32)
        v1 = jnp.where(live1, c1[0, :, cols].astype(jnp.float32), 0.0)
        out_ref[0, :, cols] = ((a0 * v0 + a1 * v1) / (a0 + a1)).astype(out_ref.dtype)


def combine(back_ctx, back_stats, place, neighbour_count, heads):
    places, span, width = back_ctx.shape
    spans = neighbour_count.shape[0]

    def by_place(k, shape):
        return pl.BlockSpec((1,) + shape, lambda c, p, n: (p[c * K + k], 0, 0))

    grid_spec = pltpu.PrefetchScalarGridSpec(
        num_scalar_prefetch=2,
        grid=(spans,),
        in_specs=[by_place(0, (span, width)), by_place(1, (span, width)),
                  by_place(0, (span, 2 * heads)), by_place(1, (span, 2 * heads))],
        out_specs=pl.BlockSpec((1, span, width), lambda c, p, n: (c, 0, 0)),
    )
    return pl.pallas_call(
        functools.partial(combine_kernel, heads),
        grid_spec=grid_spec,
        out_shape=jax.ShapeDtypeStruct((spans, span, width), jnp.bfloat16),
    )(place, neighbour_count, back_ctx, back_ctx, back_stats, back_stats)


def any_spec():
    return pl.BlockSpec(memory_space=pl.ANY)


def exchange_out(send_q, send_e, w_loc, n_seq, n_db):
    features = w_loc.shape[1] // n_db
    dma = pltpu.SemaphoreType.DMA
    return pl.pallas_call(
        functools.partial(out_kernel, n_seq, n_db, features),
        out_shape=(
            jax.ShapeDtypeStruct(send_q.shape, send_q.dtype),
            jax.ShapeDtypeStruct(send_e.shape, send_e.dtype),
            jax.ShapeDtypeStruct((n_db, w_loc.shape[0], features), w_loc.dtype),
        ),
        in_specs=[any_spec()] * 3,
        out_specs=(any_spec(), any_spec(), any_spec()),
        scratch_shapes=[
            dma((n_seq,)), dma((n_seq,)), dma((n_seq,)), dma((n_seq,)),
            dma((n_db,)), dma((n_db,)), dma((3,)),
        ],
        compiler_params=pltpu.CompilerParams(collective_id=0, has_side_effects=True),
    )(send_q, send_e, w_loc)


def exchange_back(ctx, stats, n_seq, collective_id):
    dma = pltpu.SemaphoreType.DMA
    return pl.pallas_call(
        functools.partial(back_kernel, n_seq),
        out_shape=(
            jax.ShapeDtypeStruct(ctx.shape, ctx.dtype),
            jax.ShapeDtypeStruct(stats.shape, stats.dtype),
        ),
        in_specs=[any_spec()] * 2,
        out_specs=(any_spec(), any_spec()),
        scratch_shapes=[dma((n_seq,)), dma((n_seq,)), dma((n_seq,)), dma((n_seq,)), dma((2,))],
        compiler_params=pltpu.CompilerParams(collective_id=collective_id, has_side_effects=True),
    )(ctx, stats)


def on_device(
    decoder_states,
    query_weight,
    output_weight,
    neighbour_kv,
    neighbour_shard,
    neighbour_entry,
    neighbour_count,
):
    tok_rows = decoder_states.shape[0]
    span_total = tok_rows // SPAN
    row_width = query_weight.shape[1]
    heads_here = row_width // HD
    key_len = neighbour_kv.shape[1]
    n_seq = lax.psum(1, "seq")
    n_db = lax.psum(1, "db")
    places_total = n_seq * CAP
    queries = jnp.dot(decoder_states, query_weight, preferred_element_type=jnp.float32).astype(
        jnp.bfloat16
    )
    queries = queries.reshape(span_total, SPAN, row_width)

    live, place = slot_places(neighbour_shard, neighbour_count)
    target = jnp.where(live, place, places_total)
    span_of_slot = jnp.arange(span_total * K, dtype=jnp.int32) // K
    send_q = jnp.zeros((places_total, SPAN, row_width), jnp.bfloat16)
    send_q = send_q.at[target].set(queries[span_of_slot], mode="drop")
    send_e = jnp.zeros((places_total,), jnp.int32)
    send_e = send_e.at[target].set(neighbour_entry.reshape(-1), mode="drop")
    send_e = jnp.pad(send_e.reshape(n_seq, CAP), ((0, 0), (0, LANES - CAP)))
    recv_q, recv_e, weight_cols = exchange_out(
        send_q.reshape(n_seq, CAP, SPAN, row_width), send_e, output_weight, n_seq, n_db
    )
    recv_e = recv_e[:, :CAP].reshape(-1)
    kv_flat = neighbour_kv.reshape(neighbour_kv.shape[0], key_len, 2 * row_width)
    weight_cols = weight_cols.reshape(n_db, heads_here, HD, weight_cols.shape[2])
    out = None
    for head in range(heads_here):
        part, stats = attend(recv_q, recv_e, kv_flat, heads_here, head)
        back_ctx, back_stats = exchange_back(
            part, stats.reshape(n_seq, CAP * SPAN * 2 // LANES, LANES), n_seq, 1 + head
        )
        back_ctx = back_ctx.reshape(places_total, SPAN, HD)
        back_stats = back_stats.reshape(places_total, SPAN, 2)
        context = combine(back_ctx, back_stats, place, neighbour_count, 1)
        context = context.reshape(tok_rows, HD)
        contexts = lax.all_gather(context, "db", axis=0, tiled=False)
        term = jnp.einsum(
            "str,srf->tf", contexts, weight_cols[:, head], preferred_element_type=jnp.float32
        )
        out = term if out is None else out + term
    return out.astype(jnp.bfloat16)


def solution(mesh):
    in_specs = (
        P("seq", None),
        P(None, "db"),
        P("db", None),
        P("seq", None, None, "db"),
        P("seq", None),
        P("seq", None),
        P("seq"),
    )
    out_specs = P("seq", "db")
    return jax.shard_map(
        on_device, mesh=mesh, in_specs=in_specs, out_specs=out_specs, check_vma=False
    )
```

```python
import functools
import math

import jax
import jax.numpy as jnp
from jax import lax
from jax.experimental import pallas as pl
from jax.experimental.pallas import tpu as pltpu
from jax.sharding import PartitionSpec as P

HD = 128
SPAN = 64
K = 2
CAP = 3
LANES = 128
MESH = pl.DeviceIdType.MESH


def slot_places(neighbour_shard, neighbour_count):
    own_shard = neighbour_shard.reshape(-1)
    slots = own_shard.shape[0]
    own_live = (
        jnp.arange(K, dtype=jnp.int32)[None, :] < neighbour_count[:, None]
    ).reshape(-1)
    same = (own_shard[None, :] == own_shard[:, None]) & own_live[None, :]
    earlier = jnp.arange(slots)[None, :] < jnp.arange(slots)[:, None]
    own_rank = jnp.minimum(jnp.sum((same & earlier).astype(jnp.int32), axis=1), CAP - 1)
    return own_live, own_shard * CAP + own_rank


def peer_copy(src, dst, send_sem, recv_sem, device):
    return pltpu.make_async_remote_copy(
        src_ref=src, dst_ref=dst, send_sem=send_sem, recv_sem=recv_sem,
        device_id=device, device_id_type=MESH,
    )


def out_kernel(n_seq, n_db, features, send_q, send_e, w_loc, recv_q, recv_e, w_cols,
               qs, qr, es, er, ws, wr, ls):
    me_s = lax.axis_index("seq")
    me_d = lax.axis_index("db")

    def w_src(d):
        return w_loc.at[:, pl.ds(pl.multiple_of(d * features, features), features)]

    barrier = pltpu.get_barrier_semaphore()

    @pl.loop(1, n_seq)
    def _(o):
        pl.semaphore_signal(barrier, inc=1, device_id=(lax.rem(me_s + o, n_seq), me_d),
                            device_id_type=MESH)

    @pl.loop(1, n_db)
    def _(o):
        pl.semaphore_signal(barrier, inc=1, device_id=(me_s, lax.rem(me_d + o, n_db)),
                            device_id_type=MESH)

    pl.semaphore_wait(barrier, (n_seq - 1) + (n_db - 1))

    own = [
        pltpu.make_async_copy(send_q.at[me_s], recv_q.at[me_s], ls.at[0]),
        pltpu.make_async_copy(send_e.at[me_s], recv_e.at[me_s], ls.at[1]),
        pltpu.make_async_copy(w_src(me_d), w_cols.at[me_d], ls.at[2]),
    ]
    for c in own:
        c.start()

    @pl.loop(1, n_db)
    def _(o):
        d = lax.rem(me_d + o, n_db)
        peer_copy(w_src(d), w_cols.at[me_d], ws.at[d], wr.at[me_d], (me_s, d)).start()

    @pl.loop(1, n_seq)
    def _(o):
        d = lax.rem(me_s + o, n_seq)
        peer_copy(send_e.at[d], recv_e.at[me_s], es.at[d], er.at[me_s], (d, me_d)).start()
        peer_copy(send_q.at[d], recv_q.at[me_s], qs.at[d], qr.at[me_s], (d, me_d)).start()

    for c in own:
        c.wait()

    @pl.loop(1, n_seq)
    def _(o):
        d = lax.rem(me_s + o, n_seq)
        s = lax.rem(me_s + n_seq - o, n_seq)
        peer_copy(send_e.at[d], recv_e.at[me_s], es.at[d], er.at[me_s], (d, me_d)).wait_send()
        peer_copy(send_q.at[d], recv_q.at[me_s], qs.at[d], qr.at[me_s], (d, me_d)).wait_send()
        peer_copy(send_e.at[me_s], recv_e.at[s], es.at[s], er.at[s], (s, me_d)).wait_recv()
        peer_copy(send_q.at[me_s], recv_q.at[s], qs.at[s], qr.at[s], (s, me_d)).wait_recv()

    @pl.loop(1, n_db)
    def _(o):
        d = lax.rem(me_d + o, n_db)
        s = lax.rem(me_d + n_db - o, n_db)
        peer_copy(w_src(d), w_cols.at[me_d], ws.at[d], wr.at[me_d], (me_s, d)).wait_send()
        peer_copy(w_src(me_d), w_cols.at[s], ws.at[s], wr.at[s], (me_s, s)).wait_recv()


def back_kernel(n_seq, ctx, stats, back_ctx, back_stats, cs, cr, ss, sr, ls):
    me_s = lax.axis_index("seq")
    me_d = lax.axis_index("db")
    barrier = pltpu.get_barrier_semaphore()

    @pl.loop(1, n_seq)
    def _(o):
        pl.semaphore_signal(barrier, inc=1, device_id=(lax.rem(me_s + o, n_seq), me_d),
                            device_id_type=MESH)

    pl.semaphore_wait(barrier, n_seq - 1)

    own = [
        pltpu.make_async_copy(ctx.at[me_s], back_ctx.at[me_s], ls.at[0]),
        pltpu.make_async_copy(stats.at[me_s], back_stats.at[me_s], ls.at[1]),
    ]
    for c in own:
        c.start()

    @pl.loop(1, n_seq)
    def _(o):
        d = lax.rem(me_s + o, n_seq)
        peer_copy(stats.at[d], back_stats.at[me_s], ss.at[d], sr.at[me_s], (d, me_d)).start()
        peer_copy(ctx.at[d], back_ctx.at[me_s], cs.at[d], cr.at[me_s], (d, me_d)).start()

    for c in own:
        c.wait()

    @pl.loop(1, n_seq)
    def _(o):
        d = lax.rem(me_s + o, n_seq)
        s = lax.rem(me_s + n_seq - o, n_seq)
        peer_copy(stats.at[d], back_stats.at[me_s], ss.at[d], sr.at[me_s], (d, me_d)).wait_send()
        peer_copy(ctx.at[d], back_ctx.at[me_s], cs.at[d], cr.at[me_s], (d, me_d)).wait_send()
        peer_copy(stats.at[me_s], back_stats.at[s], ss.at[s], sr.at[s], (s, me_d)).wait_recv()
        peer_copy(ctx.at[me_s], back_ctx.at[s], cs.at[s], cr.at[s], (s, me_d)).wait_recv()


def attend_kernel(scale, heads, e_ref, q_ref, kv_ref, ctx_ref, stats_ref):
    n_src, cap = q_ref.shape[0], q_ref.shape[1]
    width = heads * HD

    def one_source(i, carry):
        for j in range(cap):
            kv = kv_ref.at[e_ref[i * cap + j]]
            for h in range(heads):
                q = q_ref[i, j, :, h * HD:(h + 1) * HD]
                k = kv[:, h * HD:(h + 1) * HD]
                v = kv[:, width + h * HD:width + (h + 1) * HD]
                s = lax.dot_general(
                    q, k, (((1,), (1,)), ((), ())), preferred_element_type=jnp.float32
                ) * scale
                top = jnp.max(s, axis=1, keepdims=True)
                w = jnp.exp(s - top)
                total = jnp.sum(w, axis=1, keepdims=True)
                ctx = jnp.dot(w.astype(jnp.bfloat16), v, preferred_element_type=jnp.float32)
                ctx_ref[i, j, :, h * HD:(h + 1) * HD] = (ctx / total).astype(ctx_ref.dtype)
                stats_ref[i, j, :, 2 * h:2 * h + 1] = top
                stats_ref[i, j, :, 2 * h + 1:2 * h + 2] = total
        return carry

    lax.fori_loop(0, n_src, one_source, 0)


def vmem_whole(shape):
    return pl.BlockSpec(shape, lambda *_: (0,) * len(shape))


def attend(recv_q, recv_e, kv_flat, heads):
    n_src, cap, span, width = recv_q.shape
    stats_shape = (n_src, cap, span, 2 * heads)
    grid_spec = pltpu.PrefetchScalarGridSpec(
        num_scalar_prefetch=1,
        grid=(1,),
        in_specs=[vmem_whole(recv_q.shape), vmem_whole(kv_flat.shape)],
        out_specs=[vmem_whole(recv_q.shape), vmem_whole(stats_shape)],
    )
    return pl.pallas_call(
        functools.partial(attend_kernel, 1.0 / math.sqrt(HD), heads),
        grid_spec=grid_spec,
        out_shape=(
            jax.ShapeDtypeStruct(recv_q.shape, jnp.bfloat16),
            jax.ShapeDtypeStruct(stats_shape, jnp.float32),
        ),
    )(recv_e, recv_q, kv_flat)


def combine_kernel(heads, place_ref, count_ref, ctx_ref, stats_ref, out_ref):
    def one_span(c, carry):
        p0 = place_ref[c * K]
        p1 = place_ref[c * K + 1]
        live1 = count_ref[c] > 1
        for h in range(heads):
            cols = slice(h * HD, (h + 1) * HD)
            m0 = stats_ref[p0, :, 2 * h:2 * h + 1]
            l0 = stats_ref[p0, :, 2 * h + 1:2 * h + 2]
            m1 = stats_ref[p1, :, 2 * h:2 * h + 1]
            l1 = stats_ref[p1, :, 2 * h + 1:2 * h + 2]
            best = jnp.where(live1, jnp.maximum(m0, m1), m0)
            a0 = jnp.exp(m0 - best) * l0
            a1 = jnp.where(live1, jnp.exp(m1 - best) * l1, 0.0)
            v0 = ctx_ref[p0, :, cols].astype(jnp.float32)
            v1 = jnp.where(live1, ctx_ref[p1, :, cols].astype(jnp.float32), 0.0)
            out_ref[c, :, cols] = ((a0 * v0 + a1 * v1) / (a0 + a1)).astype(out_ref.dtype)
        return carry

    lax.fori_loop(0, out_ref.shape[0], one_span, 0)


def combine(back_ctx, back_stats, place, neighbour_count, heads):
    places, span, width = back_ctx.shape
    spans = neighbour_count.shape[0]
    grid_spec = pltpu.PrefetchScalarGridSpec(
        num_scalar_prefetch=2,
        grid=(1,),
        in_specs=[vmem_whole(back_ctx.shape), vmem_whole(back_stats.shape)],
        out_specs=vmem_whole((spans, span, width)),
    )
    return pl.pallas_call(
        functools.partial(combine_kernel, heads),
        grid_spec=grid_spec,
        out_shape=jax.ShapeDtypeStruct((spans, span, width), jnp.bfloat16),
    )(place, neighbour_count, back_ctx, back_stats)


def any_spec():
    return pl.BlockSpec(memory_space=pl.ANY)


def exchange_out(send_q, send_e, w_loc, n_seq, n_db):
    features = w_loc.shape[1] // n_db
    dma = pltpu.SemaphoreType.DMA
    return pl.pallas_call(
        functools.partial(out_kernel, n_seq, n_db, features),
        out_shape=(
            jax.ShapeDtypeStruct(send_q.shape, send_q.dtype),
            jax.ShapeDtypeStruct(send_e.shape, send_e.dtype),
            jax.ShapeDtypeStruct((n_db, w_loc.shape[0], features), w_loc.dtype),
        ),
        in_specs=[any_spec()] * 3,
        out_specs=(any_spec(), any_spec(), any_spec()),
        scratch_shapes=[
            dma((n_seq,)), dma((n_seq,)), dma((n_seq,)), dma((n_seq,)),
            dma((n_db,)), dma((n_db,)), dma((3,)),
        ],
        compiler_params=pltpu.CompilerParams(collective_id=0, has_side_effects=True),
    )(send_q, send_e, w_loc)


def exchange_back(ctx, stats, n_seq):
    dma = pltpu.SemaphoreType.DMA
    return pl.pallas_call(
        functools.partial(back_kernel, n_seq),
        out_shape=(
            jax.ShapeDtypeStruct(ctx.shape, ctx.dtype),
            jax.ShapeDtypeStruct(stats.shape, stats.dtype),
        ),
        in_specs=[any_spec()] * 2,
        out_specs=(any_spec(), any_spec()),
        scratch_shapes=[dma((n_seq,)), dma((n_seq,)), dma((n_seq,)), dma((n_seq,)), dma((2,))],
        compiler_params=pltpu.CompilerParams(collective_id=1, has_side_effects=True),
    )(ctx, stats)


def on_device(
    decoder_states,
    query_weight,
    output_weight,
    neighbour_kv,
    neighbour_shard,
    neighbour_entry,
    neighbour_count,
):
    tok_rows = decoder_states.shape[0]
    span_total = tok_rows // SPAN
    row_width = query_weight.shape[1]
    heads_here = row_width // HD
    key_len = neighbour_kv.shape[1]
    n_seq = lax.psum(1, "seq")
    n_db = lax.psum(1, "db")
    places_total = n_seq * CAP
    queries = jnp.dot(decoder_states, query_weight, preferred_element_type=jnp.float32).astype(
        jnp.bfloat16
    )
    queries = queries.reshape(span_total, SPAN, row_width)

    live, place = slot_places(neighbour_shard, neighbour_count)
    target = jnp.where(live, place, places_total)
    span_of_slot = jnp.arange(span_total * K, dtype=jnp.int32) // K
    send_q = jnp.zeros((places_total, SPAN, row_width), jnp.bfloat16)
    send_q = send_q.at[target].set(queries[span_of_slot], mode="drop")
    send_e = jnp.zeros((places_total,), jnp.int32)
    send_e = send_e.at[target].set(neighbour_entry.reshape(-1), mode="drop")
    send_e = jnp.pad(send_e.reshape(n_seq, CAP), ((0, 0), (0, LANES - CAP)))
    recv_q, recv_e, weight_cols = exchange_out(
        send_q.reshape(n_seq, CAP, SPAN, row_width), send_e, output_weight, n_seq, n_db
    )
    recv_e = recv_e[:, :CAP].reshape(-1)
    kv_flat = neighbour_kv.reshape(neighbour_kv.shape[0], key_len, 2 * row_width)
    part, stats = attend(recv_q, recv_e, kv_flat, heads_here)
    back_ctx, back_stats = exchange_back(
        part, stats.reshape(n_seq, CAP * SPAN * 2 * heads_here // LANES, LANES), n_seq
    )
    back_ctx = back_ctx.reshape(places_total, SPAN, row_width)
    back_stats = back_stats.reshape(places_total, SPAN, 2 * heads_here)
    context = combine(back_ctx, back_stats, place, neighbour_count, heads_here)
    context = context.reshape(tok_rows, row_width)

    contexts = lax.all_gather(context, "db", axis=0, tiled=False)
    out = jnp.einsum(
        "str,srf->tf", contexts, weight_cols, preferred_element_type=jnp.float32
    )
    return out.astype(jnp.bfloat16)


def solution(mesh):
    in_specs = (
        P("seq", None),
        P(None, "db"),
        P("db", None),
        P("seq", None, None, "db"),
        P("seq", None),
        P("seq", None),
        P("seq"),
    )
    out_specs = P("seq", "db")
    return jax.shard_map(
        on_device, mesh=mesh, in_specs=in_specs, out_specs=out_specs, check_vma=False
    )
```

```python
import functools
import math

import jax
import jax.numpy as jnp
from jax import lax
from jax.experimental import pallas as pl
from jax.experimental.pallas import tpu as pltpu
from jax.sharding import PartitionSpec as P

HD = 128
SPAN = 64
K = 2
CAP = 3
LANES = 128
MESH = pl.DeviceIdType.MESH


def slot_places(neighbour_shard, neighbour_count):
    own_shard = neighbour_shard.reshape(-1)
    slots = own_shard.shape[0]
    own_live = (
        jnp.arange(K, dtype=jnp.int32)[None, :] < neighbour_count[:, None]
    ).reshape(-1)
    same = (own_shard[None, :] == own_shard[:, None]) & own_live[None, :]
    earlier = jnp.arange(slots)[None, :] < jnp.arange(slots)[:, None]
    own_rank = jnp.minimum(jnp.sum((same & earlier).astype(jnp.int32), axis=1), CAP - 1)
    return own_live, own_shard * CAP + own_rank


def peer_copy(src, dst, send_sem, recv_sem, device):
    return pltpu.make_async_remote_copy(
        src_ref=src, dst_ref=dst, send_sem=send_sem, recv_sem=recv_sem,
        device_id=device, device_id_type=MESH,
    )


def out_kernel(n_seq, n_db, features, send_q, send_e, w_loc, recv_q, recv_e, w_cols,
               qs, qr, es, er, ws, wr, ls):
    me_s = lax.axis_index("seq")
    me_d = lax.axis_index("db")

    def w_src(d):
        return w_loc.at[:, pl.ds(pl.multiple_of(d * features, features), features)]

    barrier = pltpu.get_barrier_semaphore()

    @pl.loop(1, n_seq)
    def _(o):
        pl.semaphore_signal(barrier, inc=1, device_id=(lax.rem(me_s + o, n_seq), me_d),
                            device_id_type=MESH)

    @pl.loop(1, n_db)
    def _(o):
        pl.semaphore_signal(barrier, inc=1, device_id=(me_s, lax.rem(me_d + o, n_db)),
                            device_id_type=MESH)

    pl.semaphore_wait(barrier, (n_seq - 1) + (n_db - 1))

    own = [
        pltpu.make_async_copy(send_q.at[me_s], recv_q.at[me_s], ls.at[0]),
        pltpu.make_async_copy(send_e.at[me_s], recv_e.at[me_s], ls.at[1]),
        pltpu.make_async_copy(w_src(me_d), w_cols.at[me_d], ls.at[2]),
    ]
    for c in own:
        c.start()

    @pl.loop(1, n_db)
    def _(o):
        d = lax.rem(me_d + o, n_db)
        peer_copy(w_src(d), w_cols.at[me_d], ws.at[d], wr.at[me_d], (me_s, d)).start()

    @pl.loop(1, n_seq)
    def _(o):
        d = lax.rem(me_s + o, n_seq)
        peer_copy(send_e.at[d], recv_e.at[me_s], es.at[d], er.at[me_s], (d, me_d)).start()
        peer_copy(send_q.at[d], recv_q.at[me_s], qs.at[d], qr.at[me_s], (d, me_d)).start()

    for c in own:
        c.wait()

    @pl.loop(1, n_seq)
    def _(o):
        d = lax.rem(me_s + o, n_seq)
        s = lax.rem(me_s + n_seq - o, n_seq)
        peer_copy(send_e.at[d], recv_e.at[me_s], es.at[d], er.at[me_s], (d, me_d)).wait_send()
        peer_copy(send_q.at[d], recv_q.at[me_s], qs.at[d], qr.at[me_s], (d, me_d)).wait_send()
        peer_copy(send_e.at[me_s], recv_e.at[s], es.at[s], er.at[s], (s, me_d)).wait_recv()
        peer_copy(send_q.at[me_s], recv_q.at[s], qs.at[s], qr.at[s], (s, me_d)).wait_recv()

    @pl.loop(1, n_db)
    def _(o):
        d = lax.rem(me_d + o, n_db)
        s = lax.rem(me_d + n_db - o, n_db)
        peer_copy(w_src(d), w_cols.at[me_d], ws.at[d], wr.at[me_d], (me_s, d)).wait_send()
        peer_copy(w_src(me_d), w_cols.at[s], ws.at[s], wr.at[s], (me_s, s)).wait_recv()


def back_kernel(n_seq, ctx, stats, back_ctx, back_stats, cs, cr, ss, sr, ls):
    me_s = lax.axis_index("seq")
    me_d = lax.axis_index("db")
    barrier = pltpu.get_barrier_semaphore()

    @pl.loop(1, n_seq)
    def _(o):
        pl.semaphore_signal(barrier, inc=1, device_id=(lax.rem(me_s + o, n_seq), me_d),
                            device_id_type=MESH)

    pl.semaphore_wait(barrier, n_seq - 1)

    own = [
        pltpu.make_async_copy(ctx.at[me_s], back_ctx.at[me_s], ls.at[0]),
        pltpu.make_async_copy(stats.at[me_s], back_stats.at[me_s], ls.at[1]),
    ]
    for c in own:
        c.start()

    @pl.loop(1, n_seq)
    def _(o):
        d = lax.rem(me_s + o, n_seq)
        peer_copy(stats.at[d], back_stats.at[me_s], ss.at[d], sr.at[me_s], (d, me_d)).start()
        peer_copy(ctx.at[d], back_ctx.at[me_s], cs.at[d], cr.at[me_s], (d, me_d)).start()

    for c in own:
        c.wait()

    @pl.loop(1, n_seq)
    def _(o):
        d = lax.rem(me_s + o, n_seq)
        s = lax.rem(me_s + n_seq - o, n_seq)
        peer_copy(stats.at[d], back_stats.at[me_s], ss.at[d], sr.at[me_s], (d, me_d)).wait_send()
        peer_copy(ctx.at[d], back_ctx.at[me_s], cs.at[d], cr.at[me_s], (d, me_d)).wait_send()
        peer_copy(stats.at[me_s], back_stats.at[s], ss.at[s], sr.at[s], (s, me_d)).wait_recv()
        peer_copy(ctx.at[me_s], back_ctx.at[s], cs.at[s], cr.at[s], (s, me_d)).wait_recv()


def attend_kernel(scale, heads, rows, e_ref, q_ref, kv_ref, ctx_ref, stats_ref):
    key_len = SPAN * 2
    keys_total, width = kv_ref.shape[0], heads * HD
    per_tile = rows // SPAN
    col_block = lax.broadcasted_iota(jnp.int32, (1, keys_total), 1) // key_len
    row_block = lax.broadcasted_iota(jnp.int32, (rows, 1), 0) // SPAN

    def one_tile(t, carry):
        start = pl.multiple_of(t * rows, rows)
        row_entry = jnp.zeros((rows, 1), jnp.int32)
        for j in range(per_tile):
            row_entry = jnp.where(row_block == j, e_ref[t * per_tile + j], row_entry)
        named = col_block == row_entry
        for h in range(heads):
            q = q_ref[pl.ds(start, rows), h * HD:(h + 1) * HD]
            k = kv_ref[:, h * HD:(h + 1) * HD]
            v = kv_ref[:, width + h * HD:width + (h + 1) * HD]
            s = lax.dot_general(
                q, k, (((1,), (1,)), ((), ())), preferred_element_type=jnp.float32
            ) * scale
            s = jnp.where(named, s, -jnp.inf)
            top = jnp.max(s, axis=1, keepdims=True)
            w = jnp.exp(s - top)
            total = jnp.sum(w, axis=1, keepdims=True)
            ctx = jnp.dot(w.astype(jnp.bfloat16), v, preferred_element_type=jnp.float32)
            ctx_ref[pl.ds(start, rows), h * HD:(h + 1) * HD] = (ctx / total).astype(ctx_ref.dtype)
            stats_ref[pl.ds(start, rows), 2 * h:2 * h + 1] = top
            stats_ref[pl.ds(start, rows), 2 * h + 1:2 * h + 2] = total
        return carry

    lax.fori_loop(0, q_ref.shape[0] // rows, one_tile, 0)


def vmem_whole(shape):
    return pl.BlockSpec(shape, lambda *_: (0,) * len(shape))


def attend(recv_q, recv_e, kv_flat, heads):
    n_src, cap, span, width = recv_q.shape
    q_rows = recv_q.reshape(n_src * cap * span, width)
    kv_rows = kv_flat.reshape(-1, kv_flat.shape[2])
    stats_shape = (q_rows.shape[0], 2 * heads)
    grid_spec = pltpu.PrefetchScalarGridSpec(
        num_scalar_prefetch=1,
        grid=(1,),
        in_specs=[vmem_whole(q_rows.shape), vmem_whole(kv_rows.shape)],
        out_specs=[vmem_whole(q_rows.shape), vmem_whole(stats_shape)],
    )
    ctx, stats = pl.pallas_call(
        functools.partial(attend_kernel, 1.0 / math.sqrt(HD), heads, 4 * span),
        grid_spec=grid_spec,
        out_shape=(
            jax.ShapeDtypeStruct(q_rows.shape, jnp.bfloat16),
            jax.ShapeDtypeStruct(stats_shape, jnp.float32),
        ),
    )(recv_e, q_rows, kv_rows)
    return ctx.reshape(recv_q.shape), stats.reshape(n_src, cap, span, 2 * heads)


def combine_kernel(heads, place_ref, count_ref, ctx_ref, stats_ref, out_ref):
    def one_span(c, carry):
        p0 = place_ref[c * K]
        p1 = place_ref[c * K + 1]
        live1 = count_ref[c] > 1
        for h in range(heads):
            cols = slice(h * HD, (h + 1) * HD)
            m0 = stats_ref[p0, :, 2 * h:2 * h + 1]
            l0 = stats_ref[p0, :, 2 * h + 1:2 * h + 2]
            m1 = stats_ref[p1, :, 2 * h:2 * h + 1]
            l1 = stats_ref[p1, :, 2 * h + 1:2 * h + 2]
            best = jnp.where(live1, jnp.maximum(m0, m1), m0)
            a0 = jnp.exp(m0 - best) * l0
            a1 = jnp.where(live1, jnp.exp(m1 - best) * l1, 0.0)
            v0 = ctx_ref[p0, :, cols].astype(jnp.float32)
            v1 = jnp.where(live1, ctx_ref[p1, :, cols].astype(jnp.float32), 0.0)
            out_ref[c, :, cols] = ((a0 * v0 + a1 * v1) / (a0 + a1)).astype(out_ref.dtype)
        return carry

    lax.fori_loop(0, out_ref.shape[0], one_span, 0)


def combine(back_ctx, back_stats, place, neighbour_count, heads):
    places, span, width = back_ctx.shape
    spans = neighbour_count.shape[0]
    grid_spec = pltpu.PrefetchScalarGridSpec(
        num_scalar_prefetch=2,
        grid=(1,),
        in_specs=[vmem_whole(back_ctx.shape), vmem_whole(back_stats.shape)],
        out_specs=vmem_whole((spans, span, width)),
    )
    return pl.pallas_call(
        functools.partial(combine_kernel, heads),
        grid_spec=grid_spec,
        out_shape=jax.ShapeDtypeStruct((spans, span, width), jnp.bfloat16),
    )(place, neighbour_count, back_ctx, back_stats)


def any_spec():
    return pl.BlockSpec(memory_space=pl.ANY)


def exchange_out(send_q, send_e, w_loc, n_seq, n_db):
    features = w_loc.shape[1] // n_db
    dma = pltpu.SemaphoreType.DMA
    return pl.pallas_call(
        functools.partial(out_kernel, n_seq, n_db, features),
        out_shape=(
            jax.ShapeDtypeStruct(send_q.shape, send_q.dtype),
            jax.ShapeDtypeStruct(send_e.shape, send_e.dtype),
            jax.ShapeDtypeStruct((n_db, w_loc.shape[0], features), w_loc.dtype),
        ),
        in_specs=[any_spec()] * 3,
        out_specs=(any_spec(), any_spec(), any_spec()),
        scratch_shapes=[
            dma((n_seq,)), dma((n_seq,)), dma((n_seq,)), dma((n_seq,)),
            dma((n_db,)), dma((n_db,)), dma((3,)),
        ],
        compiler_params=pltpu.CompilerParams(collective_id=0, has_side_effects=True),
    )(send_q, send_e, w_loc)


def exchange_back(ctx, stats, n_seq):
    dma = pltpu.SemaphoreType.DMA
    return pl.pallas_call(
        functools.partial(back_kernel, n_seq),
        out_shape=(
            jax.ShapeDtypeStruct(ctx.shape, ctx.dtype),
            jax.ShapeDtypeStruct(stats.shape, stats.dtype),
        ),
        in_specs=[any_spec()] * 2,
        out_specs=(any_spec(), any_spec()),
        scratch_shapes=[dma((n_seq,)), dma((n_seq,)), dma((n_seq,)), dma((n_seq,)), dma((2,))],
        compiler_params=pltpu.CompilerParams(collective_id=1, has_side_effects=True),
    )(ctx, stats)


def on_device(
    decoder_states,
    query_weight,
    output_weight,
    neighbour_kv,
    neighbour_shard,
    neighbour_entry,
    neighbour_count,
):
    tok_rows = decoder_states.shape[0]
    span_total = tok_rows // SPAN
    row_width = query_weight.shape[1]
    heads_here = row_width // HD
    key_len = neighbour_kv.shape[1]
    n_seq = lax.psum(1, "seq")
    n_db = lax.psum(1, "db")
    places_total = n_seq * CAP
    queries = jnp.dot(decoder_states, query_weight, preferred_element_type=jnp.float32).astype(
        jnp.bfloat16
    )
    queries = queries.reshape(span_total, SPAN, row_width)

    live, place = slot_places(neighbour_shard, neighbour_count)
    target = jnp.where(live, place, places_total)
    span_of_slot = jnp.arange(span_total * K, dtype=jnp.int32) // K
    send_q = jnp.zeros((places_total, SPAN, row_width), jnp.bfloat16)
    send_q = send_q.at[target].set(queries[span_of_slot], mode="drop")
    send_e = jnp.zeros((places_total,), jnp.int32)
    send_e = send_e.at[target].set(neighbour_entry.reshape(-1), mode="drop")
    send_e = jnp.pad(send_e.reshape(n_seq, CAP), ((0, 0), (0, LANES - CAP)))
    recv_q, recv_e, weight_cols = exchange_out(
        send_q.reshape(n_seq, CAP, SPAN, row_width), send_e, output_weight, n_seq, n_db
    )
    recv_e = recv_e[:, :CAP].reshape(-1)
    kv_flat = neighbour_kv.reshape(neighbour_kv.shape[0], key_len, 2 * row_width)
    part, stats = attend(recv_q, recv_e, kv_flat, heads_here)
    back_ctx, back_stats = exchange_back(
        part, stats.reshape(n_seq, CAP * SPAN * 2 * heads_here // LANES, LANES), n_seq
    )
    back_ctx = back_ctx.reshape(places_total, SPAN, row_width)
    back_stats = back_stats.reshape(places_total, SPAN, 2 * heads_here)
    context = combine(back_ctx, back_stats, place, neighbour_count, heads_here)
    context = context.reshape(tok_rows, row_width)

    contexts = lax.all_gather(context, "db", axis=0, tiled=False)
    out = jnp.einsum(
        "str,srf->tf", contexts, weight_cols, preferred_element_type=jnp.float32
    )
    return out.astype(jnp.bfloat16)


def solution(mesh):
    in_specs = (
        P("seq", None),
        P(None, "db"),
        P("db", None),
        P("seq", None, None, "db"),
        P("seq", None),
        P("seq", None),
        P("seq"),
    )
    out_specs = P("seq", "db")
    return jax.shard_map(
        on_device, mesh=mesh, in_specs=in_specs, out_specs=out_specs, check_vma=False
    )
```

```python
import functools
import math

import jax
import jax.numpy as jnp
from jax import lax
from jax.experimental import pallas as pl
from jax.experimental.pallas import tpu as pltpu
from jax.sharding import Mesh, PartitionSpec as P

HD = 128
SPAN = 64
K = 2
CAP = 3
LANES = 128
MESH = pl.DeviceIdType.MESH
DB = ("xh", "yy", "cc")


def db_coords(d, n_y, n_core):
    return (d // (n_y * n_core), lax.rem(d // n_core, n_y), lax.rem(d, n_core))


def my_db():
    n_y, n_core = lax.psum(1, "yy"), lax.psum(1, "cc")
    xh, yy, cc = lax.axis_index("xh"), lax.axis_index("yy"), lax.axis_index("cc")
    return (xh * n_y + yy) * n_core + cc, (xh, yy, cc), n_y, n_core


def slot_places(neighbour_shard, neighbour_count):
    own_shard = neighbour_shard.reshape(-1)
    slots = own_shard.shape[0]
    own_live = (
        jnp.arange(K, dtype=jnp.int32)[None, :] < neighbour_count[:, None]
    ).reshape(-1)
    same = (own_shard[None, :] == own_shard[:, None]) & own_live[None, :]
    earlier = jnp.arange(slots)[None, :] < jnp.arange(slots)[:, None]
    own_rank = jnp.minimum(jnp.sum((same & earlier).astype(jnp.int32), axis=1), CAP - 1)
    return own_live, own_shard * CAP + own_rank


def peer_copy(src, dst, send_sem, recv_sem, device):
    return pltpu.make_async_remote_copy(
        src_ref=src, dst_ref=dst, send_sem=send_sem, recv_sem=recv_sem,
        device_id=device, device_id_type=MESH,
    )


def out_kernel(n_seq, n_db, features, send_q, send_e, w_loc, recv_q, recv_e, w_cols,
               qs, qr, es, er, ws, wr, ls):
    me_s = lax.axis_index("seq")
    me_d, mine, n_y, n_core = my_db()

    def seq_peer(d):
        return (d,) + mine

    def db_peer(d):
        return (me_s,) + db_coords(d, n_y, n_core)

    def w_src(d):
        return w_loc.at[:, pl.ds(pl.multiple_of(d * features, features), features)]

    barrier = pltpu.get_barrier_semaphore()

    @pl.loop(1, n_seq)
    def _(o):
        pl.semaphore_signal(barrier, inc=1, device_id=seq_peer(lax.rem(me_s + o, n_seq)),
                            device_id_type=MESH)

    @pl.loop(1, n_db)
    def _(o):
        pl.semaphore_signal(barrier, inc=1, device_id=db_peer(lax.rem(me_d + o, n_db)),
                            device_id_type=MESH)

    pl.semaphore_wait(barrier, (n_seq - 1) + (n_db - 1))

    own = [
        pltpu.make_async_copy(send_q.at[me_s], recv_q.at[me_s], ls.at[0]),
        pltpu.make_async_copy(send_e.at[me_s], recv_e.at[me_s], ls.at[1]),
        pltpu.make_async_copy(w_src(me_d), w_cols.at[me_d], ls.at[2]),
    ]
    for c in own:
        c.start()

    @pl.loop(1, n_db)
    def _(o):
        d = lax.rem(me_d + o, n_db)
        peer_copy(w_src(d), w_cols.at[me_d], ws.at[d], wr.at[me_d], db_peer(d)).start()

    @pl.loop(1, n_seq)
    def _(o):
        d = lax.rem(me_s + o, n_seq)
        peer_copy(send_e.at[d], recv_e.at[me_s], es.at[d], er.at[me_s], seq_peer(d)).start()
        peer_copy(send_q.at[d], recv_q.at[me_s], qs.at[d], qr.at[me_s], seq_peer(d)).start()

    for c in own:
        c.wait()

    @pl.loop(1, n_seq)
    def _(o):
        d = lax.rem(me_s + o, n_seq)
        s = lax.rem(me_s + n_seq - o, n_seq)
        peer_copy(send_e.at[d], recv_e.at[me_s], es.at[d], er.at[me_s], seq_peer(d)).wait_send()
        peer_copy(send_q.at[d], recv_q.at[me_s], qs.at[d], qr.at[me_s], seq_peer(d)).wait_send()
        peer_copy(send_e.at[me_s], recv_e.at[s], es.at[s], er.at[s], seq_peer(s)).wait_recv()
        peer_copy(send_q.at[me_s], recv_q.at[s], qs.at[s], qr.at[s], seq_peer(s)).wait_recv()

    @pl.loop(1, n_db)
    def _(o):
        d = lax.rem(me_d + o, n_db)
        s = lax.rem(me_d + n_db - o, n_db)
        peer_copy(w_src(d), w_cols.at[me_d], ws.at[d], wr.at[me_d], db_peer(d)).wait_send()
        peer_copy(w_src(me_d), w_cols.at[s], ws.at[s], wr.at[s], db_peer(s)).wait_recv()


def back_kernel(n_seq, ctx, stats, back_ctx, back_stats, cs, cr, ss, sr, ls):
    me_s = lax.axis_index("seq")
    _, mine, _, _ = my_db()

    def seq_peer(d):
        return (d,) + mine

    barrier = pltpu.get_barrier_semaphore()

    @pl.loop(1, n_seq)
    def _(o):
        pl.semaphore_signal(barrier, inc=1, device_id=seq_peer(lax.rem(me_s + o, n_seq)),
                            device_id_type=MESH)

    pl.semaphore_wait(barrier, n_seq - 1)

    own = [
        pltpu.make_async_copy(ctx.at[me_s], back_ctx.at[me_s], ls.at[0]),
        pltpu.make_async_copy(stats.at[me_s], back_stats.at[me_s], ls.at[1]),
    ]
    for c in own:
        c.start()

    @pl.loop(1, n_seq)
    def _(o):
        d = lax.rem(me_s + o, n_seq)
        peer_copy(stats.at[d], back_stats.at[me_s], ss.at[d], sr.at[me_s], seq_peer(d)).start()
        peer_copy(ctx.at[d], back_ctx.at[me_s], cs.at[d], cr.at[me_s], seq_peer(d)).start()

    for c in own:
        c.wait()

    @pl.loop(1, n_seq)
    def _(o):
        d = lax.rem(me_s + o, n_seq)
        s = lax.rem(me_s + n_seq - o, n_seq)
        peer_copy(stats.at[d], back_stats.at[me_s], ss.at[d], sr.at[me_s], seq_peer(d)).wait_send()
        peer_copy(ctx.at[d], back_ctx.at[me_s], cs.at[d], cr.at[me_s], seq_peer(d)).wait_send()
        peer_copy(stats.at[me_s], back_stats.at[s], ss.at[s], sr.at[s], seq_peer(s)).wait_recv()
        peer_copy(ctx.at[me_s], back_ctx.at[s], cs.at[s], cr.at[s], seq_peer(s)).wait_recv()


def attend_kernel(scale, heads, rows, e_ref, q_ref, kv_ref, ctx_ref, stats_ref):
    key_len = SPAN * 2
    keys_total, width = kv_ref.shape[0], heads * HD
    per_tile = rows // SPAN
    col_block = lax.broadcasted_iota(jnp.int32, (1, keys_total), 1) // key_len
    row_block = lax.broadcasted_iota(jnp.int32, (rows, 1), 0) // SPAN

    def one_tile(t, carry):
        start = pl.multiple_of(t * rows, rows)
        row_entry = jnp.zeros((rows, 1), jnp.int32)
        for j in range(per_tile):
            row_entry = jnp.where(row_block == j, e_ref[t * per_tile + j], row_entry)
        named = col_block == row_entry
        for h in range(heads):
            q = q_ref[pl.ds(start, rows), h * HD:(h + 1) * HD]
            k = kv_ref[:, h * HD:(h + 1) * HD]
            v = kv_ref[:, width + h * HD:width + (h + 1) * HD]
            s = lax.dot_general(
                q, k, (((1,), (1,)), ((), ())), preferred_element_type=jnp.float32
            ) * scale
            s = jnp.where(named, s, -jnp.inf)
            top = jnp.max(s, axis=1, keepdims=True)
            w = jnp.exp(s - top)
            total = jnp.sum(w, axis=1, keepdims=True)
            ctx = jnp.dot(w.astype(jnp.bfloat16), v, preferred_element_type=jnp.float32)
            ctx_ref[pl.ds(start, rows), h * HD:(h + 1) * HD] = (ctx / total).astype(ctx_ref.dtype)
            stats_ref[pl.ds(start, rows), 2 * h:2 * h + 1] = top
            stats_ref[pl.ds(start, rows), 2 * h + 1:2 * h + 2] = total
        return carry

    lax.fori_loop(0, q_ref.shape[0] // rows, one_tile, 0)


def vmem_whole(shape):
    return pl.BlockSpec(shape, lambda *_: (0,) * len(shape))


def attend(recv_q, recv_e, kv_flat, heads):
    n_src, cap, span, width = recv_q.shape
    q_rows = recv_q.reshape(n_src * cap * span, width)
    kv_rows = kv_flat.reshape(-1, kv_flat.shape[2])
    stats_shape = (q_rows.shape[0], 2 * heads)
    grid_spec = pltpu.PrefetchScalarGridSpec(
        num_scalar_prefetch=1,
        grid=(1,),
        in_specs=[vmem_whole(q_rows.shape), vmem_whole(kv_rows.shape)],
        out_specs=[vmem_whole(q_rows.shape), vmem_whole(stats_shape)],
    )
    ctx, stats = pl.pallas_call(
        functools.partial(attend_kernel, 1.0 / math.sqrt(HD), heads, 4 * span),
        grid_spec=grid_spec,
        out_shape=(
            jax.ShapeDtypeStruct(q_rows.shape, jnp.bfloat16),
            jax.ShapeDtypeStruct(stats_shape, jnp.float32),
        ),
    )(recv_e, q_rows, kv_rows)
    return ctx.reshape(recv_q.shape), stats.reshape(n_src, cap, span, 2 * heads)


def combine_kernel(heads, place_ref, count_ref, ctx_ref, stats_ref, out_ref):
    def one_span(c, carry):
        p0 = place_ref[c * K]
        p1 = place_ref[c * K + 1]
        live1 = count_ref[c] > 1
        for h in range(heads):
            cols = slice(h * HD, (h + 1) * HD)
            m0 = stats_ref[p0, :, 2 * h:2 * h + 1]
            l0 = stats_ref[p0, :, 2 * h + 1:2 * h + 2]
            m1 = stats_ref[p1, :, 2 * h:2 * h + 1]
            l1 = stats_ref[p1, :, 2 * h + 1:2 * h + 2]
            best = jnp.where(live1, jnp.maximum(m0, m1), m0)
            a0 = jnp.exp(m0 - best) * l0
            a1 = jnp.where(live1, jnp.exp(m1 - best) * l1, 0.0)
            v0 = ctx_ref[p0, :, cols].astype(jnp.float32)
            v1 = jnp.where(live1, ctx_ref[p1, :, cols].astype(jnp.float32), 0.0)
            out_ref[c, :, cols] = ((a0 * v0 + a1 * v1) / (a0 + a1)).astype(out_ref.dtype)
        return carry

    lax.fori_loop(0, out_ref.shape[0], one_span, 0)


def combine(back_ctx, back_stats, place, neighbour_count, heads):
    places, span, width = back_ctx.shape
    spans = neighbour_count.shape[0]
    grid_spec = pltpu.PrefetchScalarGridSpec(
        num_scalar_prefetch=2,
        grid=(1,),
        in_specs=[vmem_whole(back_ctx.shape), vmem_whole(back_stats.shape)],
        out_specs=vmem_whole((spans, span, width)),
    )
    return pl.pallas_call(
        functools.partial(combine_kernel, heads),
        grid_spec=grid_spec,
        out_shape=jax.ShapeDtypeStruct((spans, span, width), jnp.bfloat16),
    )(place, neighbour_count, back_ctx, back_stats)


def any_spec():
    return pl.BlockSpec(memory_space=pl.ANY)


def exchange_out(send_q, send_e, w_loc, n_seq, n_db):
    features = w_loc.shape[1] // n_db
    dma = pltpu.SemaphoreType.DMA
    return pl.pallas_call(
        functools.partial(out_kernel, n_seq, n_db, features),
        out_shape=(
            jax.ShapeDtypeStruct(send_q.shape, send_q.dtype),
            jax.ShapeDtypeStruct(send_e.shape, send_e.dtype),
            jax.ShapeDtypeStruct((n_db, w_loc.shape[0], features), w_loc.dtype),
        ),
        in_specs=[any_spec()] * 3,
        out_specs=(any_spec(), any_spec(), any_spec()),
        scratch_shapes=[
            dma((n_seq,)), dma((n_seq,)), dma((n_seq,)), dma((n_seq,)),
            dma((n_db,)), dma((n_db,)), dma((3,)),
        ],
        compiler_params=pltpu.CompilerParams(collective_id=0, has_side_effects=True),
    )(send_q, send_e, w_loc)


def exchange_back(ctx, stats, n_seq):
    dma = pltpu.SemaphoreType.DMA
    return pl.pallas_call(
        functools.partial(back_kernel, n_seq),
        out_shape=(
            jax.ShapeDtypeStruct(ctx.shape, ctx.dtype),
            jax.ShapeDtypeStruct(stats.shape, stats.dtype),
        ),
        in_specs=[any_spec()] * 2,
        out_specs=(any_spec(), any_spec()),
        scratch_shapes=[dma((n_seq,)), dma((n_seq,)), dma((n_seq,)), dma((n_seq,)), dma((2,))],
        compiler_params=pltpu.CompilerParams(collective_id=1, has_side_effects=True),
    )(ctx, stats)


def on_device(
    decoder_states,
    query_weight,
    output_weight,
    neighbour_kv,
    neighbour_shard,
    neighbour_entry,
    neighbour_count,
):
    tok_rows = decoder_states.shape[0]
    span_total = tok_rows // SPAN
    row_width = query_weight.shape[1]
    heads_here = row_width // HD
    key_len = neighbour_kv.shape[1]
    n_seq = lax.psum(1, "seq")
    n_db = lax.psum(1, DB)
    places_total = n_seq * CAP
    queries = jnp.dot(decoder_states, query_weight, preferred_element_type=jnp.float32).astype(
        jnp.bfloat16
    )
    queries = queries.reshape(span_total, SPAN, row_width)

    live, place = slot_places(neighbour_shard, neighbour_count)
    target = jnp.where(live, place, places_total)
    span_of_slot = jnp.arange(span_total * K, dtype=jnp.int32) // K
    send_q = jnp.zeros((places_total, SPAN, row_width), jnp.bfloat16)
    send_q = send_q.at[target].set(queries[span_of_slot], mode="drop")
    send_e = jnp.zeros((places_total,), jnp.int32)
    send_e = send_e.at[target].set(neighbour_entry.reshape(-1), mode="drop")
    send_e = jnp.pad(send_e.reshape(n_seq, CAP), ((0, 0), (0, LANES - CAP)))
    recv_q, recv_e, weight_cols = exchange_out(
        send_q.reshape(n_seq, CAP, SPAN, row_width), send_e, output_weight, n_seq, n_db
    )
    recv_e = recv_e[:, :CAP].reshape(-1)
    kv_flat = neighbour_kv.reshape(neighbour_kv.shape[0], key_len, 2 * row_width)
    part, stats = attend(recv_q, recv_e, kv_flat, heads_here)
    back_ctx, back_stats = exchange_back(
        part, stats.reshape(n_seq, CAP * SPAN * 2 * heads_here // LANES, LANES), n_seq
    )
    back_ctx = back_ctx.reshape(places_total, SPAN, row_width)
    back_stats = back_stats.reshape(places_total, SPAN, 2 * heads_here)
    context = combine(back_ctx, back_stats, place, neighbour_count, heads_here)
    context = context.reshape(tok_rows, row_width)

    n_core = lax.psum(1, "cc")
    contexts = lax.all_gather(context, ("xh", "yy"), axis=0, tiled=False)
    contexts = lax.all_gather(contexts, "cc", axis=0, tiled=False)
    weight_cols = weight_cols.reshape(n_db // n_core, n_core, row_width, weight_cols.shape[2])
    out = jnp.einsum(
        "cgtr,gcrf->tf", contexts, weight_cols, preferred_element_type=jnp.float32
    )
    return out.astype(jnp.bfloat16)


def solution(mesh):
    n_core, n_xh = 2, 2
    n_y = mesh.shape["db"] // (n_core * n_xh)
    fine = Mesh(mesh.devices.reshape(mesh.shape["seq"], n_xh, n_y, n_core), ("seq",) + DB)
    in_specs = (
        P("seq", None),
        P(None, DB),
        P(DB, None),
        P("seq", None, None, DB),
        P("seq", None),
        P("seq", None),
        P("seq"),
    )
    out_specs = P("seq", DB)
    return jax.shard_map(
        on_device, mesh=fine, in_specs=in_specs, out_specs=out_specs, check_vma=False
    )
```

```python
import functools
import math

import jax
import jax.numpy as jnp
from jax import lax
from jax.experimental import pallas as pl
from jax.experimental.pallas import tpu as pltpu
from jax.sharding import PartitionSpec as P

HD = 128
SPAN = 64
K = 2
CAP = 3
LANES = 128
MESH = pl.DeviceIdType.MESH


def slot_places(neighbour_shard, neighbour_count):
    own_shard = neighbour_shard.reshape(-1)
    slots = own_shard.shape[0]
    own_live = (
        jnp.arange(K, dtype=jnp.int32)[None, :] < neighbour_count[:, None]
    ).reshape(-1)
    same = (own_shard[None, :] == own_shard[:, None]) & own_live[None, :]
    earlier = jnp.arange(slots)[None, :] < jnp.arange(slots)[:, None]
    own_rank = jnp.minimum(jnp.sum((same & earlier).astype(jnp.int32), axis=1), CAP - 1)
    return own_live, own_shard * CAP + own_rank


def peer_copy(src, dst, send_sem, recv_sem, device):
    return pltpu.make_async_remote_copy(
        src_ref=src, dst_ref=dst, send_sem=send_sem, recv_sem=recv_sem,
        device_id=device, device_id_type=MESH,
    )


def out_kernel(n_seq, n_db, features, send_q, send_e, w_loc, recv_q, recv_e, w_cols,
               qs, qr, es, er, ws, wr, ls):
    me_s = lax.axis_index("seq")
    me_d = lax.axis_index("db")

    def w_src(d):
        return w_loc.at[:, pl.ds(pl.multiple_of(d * features, features), features)]

    barrier = pltpu.get_barrier_semaphore()

    @pl.loop(1, n_seq)
    def _(o):
        pl.semaphore_signal(barrier, inc=1, device_id=(lax.rem(me_s + o, n_seq), me_d),
                            device_id_type=MESH)

    @pl.loop(1, n_db)
    def _(o):
        pl.semaphore_signal(barrier, inc=1, device_id=(me_s, lax.rem(me_d + o, n_db)),
                            device_id_type=MESH)

    pl.semaphore_wait(barrier, (n_seq - 1) + (n_db - 1))

    own = [
        pltpu.make_async_copy(send_q.at[me_s], recv_q.at[me_s], ls.at[0]),
        pltpu.make_async_copy(send_e.at[me_s], recv_e.at[me_s], ls.at[1]),
        pltpu.make_async_copy(w_src(me_d), w_cols.at[me_d], ls.at[2]),
    ]
    for c in own:
        c.start()

    @pl.loop(1, n_db)
    def _(o):
        d = lax.rem(me_d + o, n_db)
        peer_copy(w_src(d), w_cols.at[me_d], ws.at[d], wr.at[me_d], (me_s, d)).start()

    @pl.loop(1, n_seq)
    def _(o):
        d = lax.rem(me_s + o, n_seq)
        peer_copy(send_e.at[d], recv_e.at[me_s], es.at[d], er.at[me_s], (d, me_d)).start()
        peer_copy(send_q.at[d], recv_q.at[me_s], qs.at[d], qr.at[me_s], (d, me_d)).start()

    for c in own:
        c.wait()

    @pl.loop(1, n_seq)
    def _(o):
        d = lax.rem(me_s + o, n_seq)
        s = lax.rem(me_s + n_seq - o, n_seq)
        peer_copy(send_e.at[d], recv_e.at[me_s], es.at[d], er.at[me_s], (d, me_d)).wait_send()
        peer_copy(send_q.at[d], recv_q.at[me_s], qs.at[d], qr.at[me_s], (d, me_d)).wait_send()
        peer_copy(send_e.at[me_s], recv_e.at[s], es.at[s], er.at[s], (s, me_d)).wait_recv()
        peer_copy(send_q.at[me_s], recv_q.at[s], qs.at[s], qr.at[s], (s, me_d)).wait_recv()

    @pl.loop(1, n_db)
    def _(o):
        d = lax.rem(me_d + o, n_db)
        s = lax.rem(me_d + n_db - o, n_db)
        peer_copy(w_src(d), w_cols.at[me_d], ws.at[d], wr.at[me_d], (me_s, d)).wait_send()
        peer_copy(w_src(me_d), w_cols.at[s], ws.at[s], wr.at[s], (me_s, s)).wait_recv()


def back_kernel(n_seq, ctx, stats, back_ctx, back_stats, cs, cr, ss, sr, ls):
    me_s = lax.axis_index("seq")
    me_d = lax.axis_index("db")
    barrier = pltpu.get_barrier_semaphore()

    @pl.loop(1, n_seq)
    def _(o):
        pl.semaphore_signal(barrier, inc=1, device_id=(lax.rem(me_s + o, n_seq), me_d),
                            device_id_type=MESH)

    pl.semaphore_wait(barrier, n_seq - 1)

    own = [
        pltpu.make_async_copy(ctx.at[me_s], back_ctx.at[me_s], ls.at[0]),
        pltpu.make_async_copy(stats.at[me_s], back_stats.at[me_s], ls.at[1]),
    ]
    for c in own:
        c.start()

    @pl.loop(1, n_seq)
    def _(o):
        d = lax.rem(me_s + o, n_seq)
        peer_copy(stats.at[d], back_stats.at[me_s], ss.at[d], sr.at[me_s], (d, me_d)).start()
        peer_copy(ctx.at[d], back_ctx.at[me_s], cs.at[d], cr.at[me_s], (d, me_d)).start()

    for c in own:
        c.wait()

    @pl.loop(1, n_seq)
    def _(o):
        d = lax.rem(me_s + o, n_seq)
        s = lax.rem(me_s + n_seq - o, n_seq)
        peer_copy(stats.at[d], back_stats.at[me_s], ss.at[d], sr.at[me_s], (d, me_d)).wait_send()
        peer_copy(ctx.at[d], back_ctx.at[me_s], cs.at[d], cr.at[me_s], (d, me_d)).wait_send()
        peer_copy(stats.at[me_s], back_stats.at[s], ss.at[s], sr.at[s], (s, me_d)).wait_recv()
        peer_copy(ctx.at[me_s], back_ctx.at[s], cs.at[s], cr.at[s], (s, me_d)).wait_recv()


def attend_kernel(scale, heads, rows, e_ref, q_ref, kv_ref, ctx_ref, stats_ref):
    key_len = SPAN * 2
    keys_total, width = kv_ref.shape[0], heads * HD
    per_tile = rows // SPAN
    col_block = lax.broadcasted_iota(jnp.int32, (1, keys_total), 1) // key_len
    row_block = lax.broadcasted_iota(jnp.int32, (rows, 1), 0) // SPAN

    def one_tile(t, carry):
        start = pl.multiple_of(t * rows, rows)
        row_entry = jnp.zeros((rows, 1), jnp.int32)
        for j in range(per_tile):
            row_entry = jnp.where(row_block == j, e_ref[t * per_tile + j], row_entry)
        named = col_block == row_entry
        for h in range(heads):
            q = q_ref[pl.ds(start, rows), h * HD:(h + 1) * HD]
            k = kv_ref[:, h * HD:(h + 1) * HD]
            v = kv_ref[:, width + h * HD:width + (h + 1) * HD]
            s = lax.dot_general(
                q, k, (((1,), (1,)), ((), ())), preferred_element_type=jnp.float32
            ) * scale
            s = jnp.where(named, s, -jnp.inf)
            top = jnp.max(s, axis=1, keepdims=True)
            w = jnp.exp(s - top)
            total = jnp.sum(w, axis=1, keepdims=True)
            ctx = jnp.dot(w.astype(jnp.bfloat16), v, preferred_element_type=jnp.float32)
            ctx_ref[pl.ds(start, rows), h * HD:(h + 1) * HD] = (ctx / total).astype(ctx_ref.dtype)
            stats_ref[pl.ds(start, rows), 2 * h:2 * h + 1] = top
            stats_ref[pl.ds(start, rows), 2 * h + 1:2 * h + 2] = total
        return carry

    lax.fori_loop(0, q_ref.shape[0] // rows, one_tile, 0)


def vmem_whole(shape):
    return pl.BlockSpec(shape, lambda *_: (0,) * len(shape))


def attend(recv_q, recv_e, kv_flat, heads):
    n_src, cap, span, width = recv_q.shape
    q_rows = recv_q.reshape(n_src * cap * span, width)
    kv_rows = kv_flat.reshape(-1, kv_flat.shape[2])
    stats_shape = (q_rows.shape[0], 2 * heads)
    grid_spec = pltpu.PrefetchScalarGridSpec(
        num_scalar_prefetch=1,
        grid=(1,),
        in_specs=[vmem_whole(q_rows.shape), vmem_whole(kv_rows.shape)],
        out_specs=[vmem_whole(q_rows.shape), vmem_whole(stats_shape)],
    )
    ctx, stats = pl.pallas_call(
        functools.partial(attend_kernel, 1.0 / math.sqrt(HD), heads, 4 * span),
        grid_spec=grid_spec,
        out_shape=(
            jax.ShapeDtypeStruct(q_rows.shape, jnp.bfloat16),
            jax.ShapeDtypeStruct(stats_shape, jnp.float32),
        ),
    )(recv_e, q_rows, kv_rows)
    return ctx.reshape(recv_q.shape), stats.reshape(n_src, cap, span, 2 * heads)


def attend_back_kernel(n_seq, heads, scale, e_ref, q_ref, kv_ref, back_ctx, back_stats,
                       stage_ctx, stage_stats, ctx_v, stats_v, cs, cr, ss, sr, ls):
    me_s = lax.axis_index("seq")
    me_d = lax.axis_index("db")
    rows = stage_ctx.shape[1]
    keys_total = kv_ref.shape[0]
    width = heads * HD
    cap = rows // SPAN
    key_block = lax.broadcasted_iota(jnp.int32, (keys_total, 1), 0) // (2 * SPAN)
    lane_place = lax.broadcasted_iota(jnp.int32, (1, rows), 1) // SPAN

    barrier = pltpu.get_barrier_semaphore()

    @pl.loop(1, n_seq)
    def _(o):
        pl.semaphore_signal(barrier, inc=1, device_id=(lax.rem(me_s + o, n_seq), me_d),
                            device_id_type=MESH)

    pl.semaphore_wait(barrier, n_seq - 1)

    def compute(d):
        entry = jnp.zeros((1, rows), jnp.int32)
        for j in range(cap):
            entry = jnp.where(lane_place == j, e_ref[d, j], entry)
        named = key_block == entry
        start = pl.multiple_of(d * rows, rows)
        stats_v[...] = jnp.zeros_like(stats_v)
        for h in range(heads):
            q = q_ref[pl.ds(start, rows), h * HD:(h + 1) * HD]
            k = kv_ref[:, h * HD:(h + 1) * HD]
            v = kv_ref[:, width + h * HD:width + (h + 1) * HD]
            st = lax.dot_general(
                k, q, (((1,), (1,)), ((), ())), preferred_element_type=jnp.float32
            ) * scale
            st = jnp.where(named, st, -jnp.inf)
            top = jnp.max(st, axis=0, keepdims=True)
            w = jnp.exp(st - top)
            total = jnp.sum(w, axis=0, keepdims=True)
            u = lax.dot_general(
                w.astype(jnp.bfloat16), v, (((0,), (0,)), ((), ())),
                preferred_element_type=jnp.float32,
            )
            ctx_v[:, h * HD:(h + 1) * HD] = u.astype(ctx_v.dtype)
            stats_v[2 * h:2 * h + 1, 0:rows] = top
            stats_v[2 * h + 1:2 * h + 2, 0:rows] = total
        staged = [
            pltpu.make_async_copy(ctx_v, stage_ctx.at[d], ls.at[0]),
            pltpu.make_async_copy(stats_v, stage_stats.at[d], ls.at[1]),
        ]
        for c in staged:
            c.start()
        for c in staged:
            c.wait()

    compute(me_s)
    own = [
        pltpu.make_async_copy(stage_ctx.at[me_s], back_ctx.at[me_s], ls.at[2]),
        pltpu.make_async_copy(stage_stats.at[me_s], back_stats.at[me_s], ls.at[3]),
    ]
    for c in own:
        c.start()

    @pl.loop(1, n_seq)
    def _(o):
        d = lax.rem(me_s + o, n_seq)
        compute(d)
        peer_copy(stage_stats.at[d], back_stats.at[me_s], ss.at[d], sr.at[me_s], (d, me_d)).start()
        peer_copy(stage_ctx.at[d], back_ctx.at[me_s], cs.at[d], cr.at[me_s], (d, me_d)).start()

    for c in own:
        c.wait()

    @pl.loop(1, n_seq)
    def _(o):
        d = lax.rem(me_s + o, n_seq)
        s = lax.rem(me_s + n_seq - o, n_seq)
        peer_copy(stage_stats.at[d], back_stats.at[me_s], ss.at[d], sr.at[me_s], (d, me_d)).wait_send()
        peer_copy(stage_ctx.at[d], back_ctx.at[me_s], cs.at[d], cr.at[me_s], (d, me_d)).wait_send()
        peer_copy(stage_stats.at[me_s], back_stats.at[s], ss.at[s], sr.at[s], (s, me_d)).wait_recv()
        peer_copy(stage_ctx.at[me_s], back_ctx.at[s], cs.at[s], cr.at[s], (s, me_d)).wait_recv()


def attend_back(recv_q, recv_e, kv_flat, heads, n_seq):
    n_src, cap, span, width = recv_q.shape
    rows = cap * span
    q_rows = recv_q.reshape(n_src * rows, width)
    kv_rows = kv_flat.reshape(-1, kv_flat.shape[2])
    stats_shape = (n_src, 8, 2 * LANES)
    ctx_shape = (n_src, rows, width)
    dma = pltpu.SemaphoreType.DMA
    outs = pl.pallas_call(
        functools.partial(attend_back_kernel, n_seq, heads, 1.0 / math.sqrt(HD)),
        out_shape=(
            jax.ShapeDtypeStruct(ctx_shape, jnp.bfloat16),
            jax.ShapeDtypeStruct(stats_shape, jnp.float32),
            jax.ShapeDtypeStruct(ctx_shape, jnp.bfloat16),
            jax.ShapeDtypeStruct(stats_shape, jnp.float32),
        ),
        in_specs=[
            pl.BlockSpec(memory_space=pltpu.SMEM),
            pl.BlockSpec(memory_space=pltpu.VMEM),
            pl.BlockSpec(memory_space=pltpu.VMEM),
        ],
        out_specs=(any_spec(), any_spec(), any_spec(), any_spec()),
        scratch_shapes=[
            pltpu.VMEM((rows, width), jnp.bfloat16),
            pltpu.VMEM(stats_shape[1:], jnp.float32),
            dma((n_seq,)), dma((n_seq,)), dma((n_seq,)), dma((n_seq,)), dma((4,)),
        ],
        compiler_params=pltpu.CompilerParams(collective_id=1, has_side_effects=True),
    )(recv_e, q_rows, kv_rows)
    return outs[0], outs[1]


def combine_kernel(heads, place_ref, count_ref, ctx_ref, stats_ref, out_ref, stats_t):
    for s in range(stats_ref.shape[0]):
        stats_t[s] = jnp.transpose(stats_ref[s])

    def one_span(c, carry):
        p0 = place_ref[c * K]
        p1 = place_ref[c * K + 1]
        r0 = pl.multiple_of(lax.rem(p0, CAP) * SPAN, SPAN)
        r1 = pl.multiple_of(lax.rem(p1, CAP) * SPAN, SPAN)
        st0 = stats_t[p0 // CAP, pl.ds(r0, SPAN), :]
        st1 = stats_t[p1 // CAP, pl.ds(r1, SPAN), :]
        live1 = count_ref[c] > 1
        for h in range(heads):
            cols = slice(h * HD, (h + 1) * HD)
            m0, l0 = st0[:, 2 * h:2 * h + 1], st0[:, 2 * h + 1:2 * h + 2]
            m1, l1 = st1[:, 2 * h:2 * h + 1], st1[:, 2 * h + 1:2 * h + 2]
            best = jnp.where(live1, jnp.maximum(m0, m1), m0)
            a0 = jnp.exp(m0 - best)
            a1 = jnp.where(live1, jnp.exp(m1 - best), 0.0)
            u0 = ctx_ref[p0, :, cols].astype(jnp.float32)
            u1 = jnp.where(live1, ctx_ref[p1, :, cols].astype(jnp.float32), 0.0)
            out_ref[c, :, cols] = (
                (a0 * u0 + a1 * u1) / (a0 * l0 + a1 * l1)
            ).astype(out_ref.dtype)
        return carry

    lax.fori_loop(0, out_ref.shape[0], one_span, 0)


def combine(back_ctx, back_stats, place, neighbour_count, heads):
    places, span, width = back_ctx.shape
    spans = neighbour_count.shape[0]
    n_src, st_rows, st_cols = back_stats.shape
    grid_spec = pltpu.PrefetchScalarGridSpec(
        num_scalar_prefetch=2,
        grid=(1,),
        in_specs=[vmem_whole(back_ctx.shape), vmem_whole(back_stats.shape)],
        out_specs=vmem_whole((spans, span, width)),
        scratch_shapes=[pltpu.VMEM((n_src, st_cols, st_rows), jnp.float32)],
    )
    return pl.pallas_call(
        functools.partial(combine_kernel, heads),
        grid_spec=grid_spec,
        out_shape=jax.ShapeDtypeStruct((spans, span, width), jnp.bfloat16),
    )(place, neighbour_count, back_ctx, back_stats)


def any_spec():
    return pl.BlockSpec(memory_space=pl.ANY)


def exchange_out(send_q, send_e, w_loc, n_seq, n_db):
    features = w_loc.shape[1] // n_db
    dma = pltpu.SemaphoreType.DMA
    return pl.pallas_call(
        functools.partial(out_kernel, n_seq, n_db, features),
        out_shape=(
            jax.ShapeDtypeStruct(send_q.shape, send_q.dtype),
            jax.ShapeDtypeStruct(send_e.shape, send_e.dtype),
            jax.ShapeDtypeStruct((n_db, w_loc.shape[0], features), w_loc.dtype),
        ),
        in_specs=[any_spec()] * 3,
        out_specs=(any_spec(), any_spec(), any_spec()),
        scratch_shapes=[
            dma((n_seq,)), dma((n_seq,)), dma((n_seq,)), dma((n_seq,)),
            dma((n_db,)), dma((n_db,)), dma((3,)),
        ],
        compiler_params=pltpu.CompilerParams(collective_id=0, has_side_effects=True),
    )(send_q, send_e, w_loc)


def exchange_back(ctx, stats, n_seq):
    dma = pltpu.SemaphoreType.DMA
    return pl.pallas_call(
        functools.partial(back_kernel, n_seq),
        out_shape=(
            jax.ShapeDtypeStruct(ctx.shape, ctx.dtype),
            jax.ShapeDtypeStruct(stats.shape, stats.dtype),
        ),
        in_specs=[any_spec()] * 2,
        out_specs=(any_spec(), any_spec()),
        scratch_shapes=[dma((n_seq,)), dma((n_seq,)), dma((n_seq,)), dma((n_seq,)), dma((2,))],
        compiler_params=pltpu.CompilerParams(collective_id=1, has_side_effects=True),
    )(ctx, stats)


def on_device(
    decoder_states,
    query_weight,
    output_weight,
    neighbour_kv,
    neighbour_shard,
    neighbour_entry,
    neighbour_count,
):
    tok_rows = decoder_states.shape[0]
    span_total = tok_rows // SPAN
    row_width = query_weight.shape[1]
    heads_here = row_width // HD
    key_len = neighbour_kv.shape[1]
    n_seq = lax.psum(1, "seq")
    n_db = lax.psum(1, "db")
    places_total = n_seq * CAP
    queries = jnp.dot(decoder_states, query_weight, preferred_element_type=jnp.float32).astype(
        jnp.bfloat16
    )
    queries = queries.reshape(span_total, SPAN, row_width)

    live, place = slot_places(neighbour_shard, neighbour_count)
    target = jnp.where(live, place, places_total)
    span_of_slot = jnp.arange(span_total * K, dtype=jnp.int32) // K
    send_q = jnp.zeros((places_total, SPAN, row_width), jnp.bfloat16)
    send_q = send_q.at[target].set(queries[span_of_slot], mode="drop")
    send_e = jnp.zeros((places_total,), jnp.int32)
    send_e = send_e.at[target].set(neighbour_entry.reshape(-1), mode="drop")
    send_e = jnp.pad(send_e.reshape(n_seq, CAP), ((0, 0), (0, LANES - CAP)))
    recv_q, recv_e, weight_cols = exchange_out(
        send_q.reshape(n_seq, CAP, SPAN, row_width), send_e, output_weight, n_seq, n_db
    )
    kv_flat = neighbour_kv.reshape(neighbour_kv.shape[0], key_len, 2 * row_width)
    back_ctx, back_stats = attend_back(recv_q, recv_e, kv_flat, heads_here, n_seq)
    back_ctx = back_ctx.reshape(places_total, SPAN, row_width)
    context = combine(back_ctx, back_stats, place, neighbour_count, heads_here)
    context = context.reshape(tok_rows, row_width)

    contexts = lax.all_gather(context, "db", axis=0, tiled=False)
    out = jnp.einsum(
        "str,srf->tf", contexts, weight_cols, preferred_element_type=jnp.float32
    )
    return out.astype(jnp.bfloat16)


def solution(mesh):
    in_specs = (
        P("seq", None),
        P(None, "db"),
        P("db", None),
        P("seq", None, None, "db"),
        P("seq", None),
        P("seq", None),
        P("seq"),
    )
    out_specs = P("seq", "db")
    return jax.shard_map(
        on_device, mesh=mesh, in_specs=in_specs, out_specs=out_specs, check_vma=False
    )
```

```python
import functools
import math

import jax
import jax.numpy as jnp
from jax import lax
from jax.experimental import pallas as pl
from jax.experimental.pallas import tpu as pltpu
from jax.sharding import PartitionSpec as P

HD = 128
SPAN = 64
K = 2
CAP = 3
LANES = 128
MESH = pl.DeviceIdType.MESH


def slot_places(neighbour_shard, neighbour_count):
    own_shard = neighbour_shard.reshape(-1)
    slots = own_shard.shape[0]
    own_live = (
        jnp.arange(K, dtype=jnp.int32)[None, :] < neighbour_count[:, None]
    ).reshape(-1)
    same = (own_shard[None, :] == own_shard[:, None]) & own_live[None, :]
    earlier = jnp.arange(slots)[None, :] < jnp.arange(slots)[:, None]
    own_rank = jnp.minimum(jnp.sum((same & earlier).astype(jnp.int32), axis=1), CAP - 1)
    return own_live, own_shard * CAP + own_rank


def peer_copy(src, dst, send_sem, recv_sem, device):
    return pltpu.make_async_remote_copy(
        src_ref=src, dst_ref=dst, send_sem=send_sem, recv_sem=recv_sem,
        device_id=device, device_id_type=MESH,
    )


def out_kernel(n_seq, send_q, send_e, recv_q, recv_e, qs, qr, es, er, ls):
    me_s = lax.axis_index("seq")
    me_d = lax.axis_index("db")

    barrier = pltpu.get_barrier_semaphore()

    @pl.loop(1, n_seq)
    def _(o):
        pl.semaphore_signal(barrier, inc=1, device_id=(lax.rem(me_s + o, n_seq), me_d),
                            device_id_type=MESH)

    pl.semaphore_wait(barrier, n_seq - 1)

    own = [
        pltpu.make_async_copy(send_q.at[me_s], recv_q.at[me_s], ls.at[0]),
        pltpu.make_async_copy(send_e.at[me_s], recv_e.at[me_s], ls.at[1]),
    ]
    for c in own:
        c.start()

    @pl.loop(1, n_seq)
    def _(o):
        d = lax.rem(me_s + o, n_seq)
        peer_copy(send_e.at[d], recv_e.at[me_s], es.at[d], er.at[me_s], (d, me_d)).start()
        peer_copy(send_q.at[d], recv_q.at[me_s], qs.at[d], qr.at[me_s], (d, me_d)).start()

    for c in own:
        c.wait()

    @pl.loop(1, n_seq)
    def _(o):
        d = lax.rem(me_s + o, n_seq)
        s = lax.rem(me_s + n_seq - o, n_seq)
        peer_copy(send_e.at[d], recv_e.at[me_s], es.at[d], er.at[me_s], (d, me_d)).wait_send()
        peer_copy(send_q.at[d], recv_q.at[me_s], qs.at[d], qr.at[me_s], (d, me_d)).wait_send()
        peer_copy(send_e.at[me_s], recv_e.at[s], es.at[s], er.at[s], (s, me_d)).wait_recv()
        peer_copy(send_q.at[me_s], recv_q.at[s], qs.at[s], qr.at[s], (s, me_d)).wait_recv()


def back_kernel(n_seq, ctx, stats, back_ctx, back_stats, cs, cr, ss, sr, ls):
    me_s = lax.axis_index("seq")
    me_d = lax.axis_index("db")
    barrier = pltpu.get_barrier_semaphore()

    @pl.loop(1, n_seq)
    def _(o):
        pl.semaphore_signal(barrier, inc=1, device_id=(lax.rem(me_s + o, n_seq), me_d),
                            device_id_type=MESH)

    pl.semaphore_wait(barrier, n_seq - 1)

    own = [
        pltpu.make_async_copy(ctx.at[me_s], back_ctx.at[me_s], ls.at[0]),
        pltpu.make_async_copy(stats.at[me_s], back_stats.at[me_s], ls.at[1]),
    ]
    for c in own:
        c.start()

    @pl.loop(1, n_seq)
    def _(o):
        d = lax.rem(me_s + o, n_seq)
        peer_copy(stats.at[d], back_stats.at[me_s], ss.at[d], sr.at[me_s], (d, me_d)).start()
        peer_copy(ctx.at[d], back_ctx.at[me_s], cs.at[d], cr.at[me_s], (d, me_d)).start()

    for c in own:
        c.wait()

    @pl.loop(1, n_seq)
    def _(o):
        d = lax.rem(me_s + o, n_seq)
        s = lax.rem(me_s + n_seq - o, n_seq)
        peer_copy(stats.at[d], back_stats.at[me_s], ss.at[d], sr.at[me_s], (d, me_d)).wait_send()
        peer_copy(ctx.at[d], back_ctx.at[me_s], cs.at[d], cr.at[me_s], (d, me_d)).wait_send()
        peer_copy(stats.at[me_s], back_stats.at[s], ss.at[s], sr.at[s], (s, me_d)).wait_recv()
        peer_copy(ctx.at[me_s], back_ctx.at[s], cs.at[s], cr.at[s], (s, me_d)).wait_recv()


def attend_kernel(scale, heads, rows, e_ref, q_ref, kv_ref, ctx_ref, stats_ref):
    key_len = SPAN * 2
    keys_total, width = kv_ref.shape[0], heads * HD
    per_tile = rows // SPAN
    col_block = lax.broadcasted_iota(jnp.int32, (1, keys_total), 1) // key_len
    row_block = lax.broadcasted_iota(jnp.int32, (rows, 1), 0) // SPAN

    def one_tile(t, carry):
        start = pl.multiple_of(t * rows, rows)
        row_entry = jnp.zeros((rows, 1), jnp.int32)
        for j in range(per_tile):
            row_entry = jnp.where(row_block == j, e_ref[t * per_tile + j], row_entry)
        named = col_block == row_entry
        for h in range(heads):
            q = q_ref[pl.ds(start, rows), h * HD:(h + 1) * HD]
            k = kv_ref[:, h * HD:(h + 1) * HD]
            v = kv_ref[:, width + h * HD:width + (h + 1) * HD]
            s = lax.dot_general(
                q, k, (((1,), (1,)), ((), ())), preferred_element_type=jnp.float32
            ) * scale
            s = jnp.where(named, s, -jnp.inf)
            top = jnp.max(s, axis=1, keepdims=True)
            w = jnp.exp(s - top)
            total = jnp.sum(w, axis=1, keepdims=True)
            ctx = jnp.dot(w.astype(jnp.bfloat16), v, preferred_element_type=jnp.float32)
            ctx_ref[pl.ds(start, rows), h * HD:(h + 1) * HD] = (ctx / total).astype(ctx_ref.dtype)
            stats_ref[pl.ds(start, rows), 2 * h:2 * h + 1] = top
            stats_ref[pl.ds(start, rows), 2 * h + 1:2 * h + 2] = total
        return carry

    lax.fori_loop(0, q_ref.shape[0] // rows, one_tile, 0)


def vmem_whole(shape):
    return pl.BlockSpec(shape, lambda *_: (0,) * len(shape))


def attend(recv_q, recv_e, kv_flat, heads):
    n_src, cap, span, width = recv_q.shape
    q_rows = recv_q.reshape(n_src * cap * span, width)
    kv_rows = kv_flat.reshape(-1, kv_flat.shape[2])
    stats_shape = (q_rows.shape[0], 2 * heads)
    grid_spec = pltpu.PrefetchScalarGridSpec(
        num_scalar_prefetch=1,
        grid=(1,),
        in_specs=[vmem_whole(q_rows.shape), vmem_whole(kv_rows.shape)],
        out_specs=[vmem_whole(q_rows.shape), vmem_whole(stats_shape)],
    )
    ctx, stats = pl.pallas_call(
        functools.partial(attend_kernel, 1.0 / math.sqrt(HD), heads, 4 * span),
        grid_spec=grid_spec,
        out_shape=(
            jax.ShapeDtypeStruct(q_rows.shape, jnp.bfloat16),
            jax.ShapeDtypeStruct(stats_shape, jnp.float32),
        ),
    )(recv_e, q_rows, kv_rows)
    return ctx.reshape(recv_q.shape), stats.reshape(n_src, cap, span, 2 * heads)


def attend_back_kernel(n_seq, n_db, heads, scale, e_ref, q_ref, kv_ref, w_loc, back_ctx,
                       back_stats, stage_ctx, stage_stats, w_cols, ctx_v, stats_v, cs, cr,
                       ss, sr, ws, wr, ls):
    me_s = lax.axis_index("seq")
    me_d = lax.axis_index("db")
    rows = stage_ctx.shape[1]
    keys_total = kv_ref.shape[0]
    width = heads * HD
    cap = rows // SPAN
    key_block = lax.broadcasted_iota(jnp.int32, (keys_total, 1), 0) // (2 * SPAN)
    lane_place = lax.broadcasted_iota(jnp.int32, (1, rows), 1) // SPAN

    barrier = pltpu.get_barrier_semaphore()

    @pl.loop(1, n_seq)
    def _(o):
        pl.semaphore_signal(barrier, inc=1, device_id=(lax.rem(me_s + o, n_seq), me_d),
                            device_id_type=MESH)

    @pl.loop(1, n_db)
    def _(o):
        pl.semaphore_signal(barrier, inc=1, device_id=(me_s, lax.rem(me_d + o, n_db)),
                            device_id_type=MESH)

    pl.semaphore_wait(barrier, (n_seq - 1) + (n_db - 1))

    features = w_cols.shape[2]

    def w_src(d):
        return w_loc.at[:, pl.ds(pl.multiple_of(d * features, features), features)]

    own_w = pltpu.make_async_copy(w_src(me_d), w_cols.at[me_d], ls.at[4])
    own_w.start()

    @pl.loop(1, n_db)
    def _(o):
        d = lax.rem(me_d + o, n_db)
        peer_copy(w_src(d), w_cols.at[me_d], ws.at[d], wr.at[me_d], (me_s, d)).start()

    def compute(d):
        entry = jnp.zeros((1, rows), jnp.int32)
        for j in range(cap):
            entry = jnp.where(lane_place == j, e_ref[d, j], entry)
        named = key_block == entry
        start = pl.multiple_of(d * rows, rows)
        stats_v[...] = jnp.zeros_like(stats_v)
        for h in range(heads):
            q = q_ref[pl.ds(start, rows), h * HD:(h + 1) * HD]
            k = kv_ref[:, h * HD:(h + 1) * HD]
            v = kv_ref[:, width + h * HD:width + (h + 1) * HD]
            st = lax.dot_general(
                k, q, (((1,), (1,)), ((), ())), preferred_element_type=jnp.float32
            ) * scale
            st = jnp.where(named, st, -jnp.inf)
            top = jnp.max(st, axis=0, keepdims=True)
            w = jnp.exp(st - top)
            total = jnp.sum(w, axis=0, keepdims=True)
            u = lax.dot_general(
                w.astype(jnp.bfloat16), v, (((0,), (0,)), ((), ())),
                preferred_element_type=jnp.float32,
            )
            ctx_v[:, h * HD:(h + 1) * HD] = u.astype(ctx_v.dtype)
            stats_v[2 * h:2 * h + 1, 0:rows] = top
            stats_v[2 * h + 1:2 * h + 2, 0:rows] = total
        staged = [
            pltpu.make_async_copy(ctx_v, stage_ctx.at[d], ls.at[0]),
            pltpu.make_async_copy(stats_v, stage_stats.at[d], ls.at[1]),
        ]
        for c in staged:
            c.start()
        for c in staged:
            c.wait()

    compute(me_s)
    own = [
        pltpu.make_async_copy(stage_ctx.at[me_s], back_ctx.at[me_s], ls.at[2]),
        pltpu.make_async_copy(stage_stats.at[me_s], back_stats.at[me_s], ls.at[3]),
    ]
    for c in own:
        c.start()

    @pl.loop(1, n_seq)
    def _(o):
        d = lax.rem(me_s + o, n_seq)
        compute(d)
        peer_copy(stage_stats.at[d], back_stats.at[me_s], ss.at[d], sr.at[me_s], (d, me_d)).start()
        peer_copy(stage_ctx.at[d], back_ctx.at[me_s], cs.at[d], cr.at[me_s], (d, me_d)).start()

    for c in own:
        c.wait()

    @pl.loop(1, n_seq)
    def _(o):
        d = lax.rem(me_s + o, n_seq)
        s = lax.rem(me_s + n_seq - o, n_seq)
        peer_copy(stage_stats.at[d], back_stats.at[me_s], ss.at[d], sr.at[me_s], (d, me_d)).wait_send()
        peer_copy(stage_ctx.at[d], back_ctx.at[me_s], cs.at[d], cr.at[me_s], (d, me_d)).wait_send()
        peer_copy(stage_stats.at[me_s], back_stats.at[s], ss.at[s], sr.at[s], (s, me_d)).wait_recv()
        peer_copy(stage_ctx.at[me_s], back_ctx.at[s], cs.at[s], cr.at[s], (s, me_d)).wait_recv()

    own_w.wait()

    @pl.loop(1, n_db)
    def _(o):
        d = lax.rem(me_d + o, n_db)
        s = lax.rem(me_d + n_db - o, n_db)
        peer_copy(w_src(d), w_cols.at[me_d], ws.at[d], wr.at[me_d], (me_s, d)).wait_send()
        peer_copy(w_src(me_d), w_cols.at[s], ws.at[s], wr.at[s], (me_s, s)).wait_recv()


def attend_back(recv_q, recv_e, kv_flat, w_loc, heads, n_seq, n_db):
    n_src, cap, span, width = recv_q.shape
    rows = cap * span
    q_rows = recv_q.reshape(n_src * rows, width)
    kv_rows = kv_flat.reshape(-1, kv_flat.shape[2])
    stats_shape = (n_src, 8, 2 * LANES)
    ctx_shape = (n_src, rows, width)
    dma = pltpu.SemaphoreType.DMA
    outs = pl.pallas_call(
        functools.partial(attend_back_kernel, n_seq, n_db, heads, 1.0 / math.sqrt(HD)),
        out_shape=(
            jax.ShapeDtypeStruct(ctx_shape, jnp.bfloat16),
            jax.ShapeDtypeStruct(stats_shape, jnp.float32),
            jax.ShapeDtypeStruct(ctx_shape, jnp.bfloat16),
            jax.ShapeDtypeStruct(stats_shape, jnp.float32),
            jax.ShapeDtypeStruct((n_db, w_loc.shape[0], w_loc.shape[1] // n_db), w_loc.dtype),
        ),
        in_specs=[
            pl.BlockSpec(memory_space=pltpu.SMEM),
            pl.BlockSpec(memory_space=pltpu.VMEM),
            pl.BlockSpec(memory_space=pltpu.VMEM),
            any_spec(),
        ],
        out_specs=(any_spec(), any_spec(), any_spec(), any_spec(), any_spec()),
        scratch_shapes=[
            pltpu.VMEM((rows, width), jnp.bfloat16),
            pltpu.VMEM(stats_shape[1:], jnp.float32),
            dma((n_seq,)), dma((n_seq,)), dma((n_seq,)), dma((n_seq,)),
            dma((n_db,)), dma((n_db,)), dma((5,)),
        ],
        compiler_params=pltpu.CompilerParams(collective_id=1, has_side_effects=True),
    )(recv_e, q_rows, kv_rows, w_loc)
    return outs[0], outs[1], outs[4]


def combine_kernel(heads, place_ref, count_ref, ctx_ref, stats_ref, out_ref, stats_t):
    for s in range(stats_ref.shape[0]):
        stats_t[s] = jnp.transpose(stats_ref[s])

    def one_span(c, carry):
        p0 = place_ref[c * K]
        p1 = place_ref[c * K + 1]
        r0 = pl.multiple_of(lax.rem(p0, CAP) * SPAN, SPAN)
        r1 = pl.multiple_of(lax.rem(p1, CAP) * SPAN, SPAN)
        st0 = stats_t[p0 // CAP, pl.ds(r0, SPAN), :]
        st1 = stats_t[p1 // CAP, pl.ds(r1, SPAN), :]
        live1 = count_ref[c] > 1
        for h in range(heads):
            cols = slice(h * HD, (h + 1) * HD)
            m0, l0 = st0[:, 2 * h:2 * h + 1], st0[:, 2 * h + 1:2 * h + 2]
            m1, l1 = st1[:, 2 * h:2 * h + 1], st1[:, 2 * h + 1:2 * h + 2]
            best = jnp.where(live1, jnp.maximum(m0, m1), m0)
            a0 = jnp.exp(m0 - best)
            a1 = jnp.where(live1, jnp.exp(m1 - best), 0.0)
            u0 = ctx_ref[p0, :, cols].astype(jnp.float32)
            u1 = jnp.where(live1, ctx_ref[p1, :, cols].astype(jnp.float32), 0.0)
            out_ref[c, :, cols] = (
                (a0 * u0 + a1 * u1) / (a0 * l0 + a1 * l1)
            ).astype(out_ref.dtype)
        return carry

    lax.fori_loop(0, out_ref.shape[0], one_span, 0)


def combine(back_ctx, back_stats, place, neighbour_count, heads):
    places, span, width = back_ctx.shape
    spans = neighbour_count.shape[0]
    n_src, st_rows, st_cols = back_stats.shape
    grid_spec = pltpu.PrefetchScalarGridSpec(
        num_scalar_prefetch=2,
        grid=(1,),
        in_specs=[vmem_whole(back_ctx.shape), vmem_whole(back_stats.shape)],
        out_specs=vmem_whole((spans, span, width)),
        scratch_shapes=[pltpu.VMEM((n_src, st_cols, st_rows), jnp.float32)],
    )
    return pl.pallas_call(
        functools.partial(combine_kernel, heads),
        grid_spec=grid_spec,
        out_shape=jax.ShapeDtypeStruct((spans, span, width), jnp.bfloat16),
    )(place, neighbour_count, back_ctx, back_stats)


def any_spec():
    return pl.BlockSpec(memory_space=pl.ANY)


def exchange_out(send_q, send_e, n_seq):
    dma = pltpu.SemaphoreType.DMA
    return pl.pallas_call(
        functools.partial(out_kernel, n_seq),
        out_shape=(
            jax.ShapeDtypeStruct(send_q.shape, send_q.dtype),
            jax.ShapeDtypeStruct(send_e.shape, send_e.dtype),
        ),
        in_specs=[any_spec()] * 2,
        out_specs=(any_spec(), any_spec()),
        scratch_shapes=[dma((n_seq,)), dma((n_seq,)), dma((n_seq,)), dma((n_seq,)), dma((2,))],
        compiler_params=pltpu.CompilerParams(collective_id=0, has_side_effects=True),
    )(send_q, send_e)


def exchange_back(ctx, stats, n_seq):
    dma = pltpu.SemaphoreType.DMA
    return pl.pallas_call(
        functools.partial(back_kernel, n_seq),
        out_shape=(
            jax.ShapeDtypeStruct(ctx.shape, ctx.dtype),
            jax.ShapeDtypeStruct(stats.shape, stats.dtype),
        ),
        in_specs=[any_spec()] * 2,
        out_specs=(any_spec(), any_spec()),
        scratch_shapes=[dma((n_seq,)), dma((n_seq,)), dma((n_seq,)), dma((n_seq,)), dma((2,))],
        compiler_params=pltpu.CompilerParams(collective_id=1, has_side_effects=True),
    )(ctx, stats)


def on_device(
    decoder_states,
    query_weight,
    output_weight,
    neighbour_kv,
    neighbour_shard,
    neighbour_entry,
    neighbour_count,
):
    tok_rows = decoder_states.shape[0]
    span_total = tok_rows // SPAN
    row_width = query_weight.shape[1]
    heads_here = row_width // HD
    key_len = neighbour_kv.shape[1]
    n_seq = lax.psum(1, "seq")
    n_db = lax.psum(1, "db")
    places_total = n_seq * CAP
    queries = jnp.dot(decoder_states, query_weight, preferred_element_type=jnp.float32).astype(
        jnp.bfloat16
    )
    queries = queries.reshape(span_total, SPAN, row_width)

    live, place = slot_places(neighbour_shard, neighbour_count)
    target = jnp.where(live, place, places_total)
    span_of_slot = jnp.arange(span_total * K, dtype=jnp.int32) // K
    send_q = jnp.zeros((places_total, SPAN, row_width), jnp.bfloat16)
    send_q = send_q.at[target].set(queries[span_of_slot], mode="drop")
    send_e = jnp.zeros((places_total,), jnp.int32)
    send_e = send_e.at[target].set(neighbour_entry.reshape(-1), mode="drop")
    send_e = jnp.pad(send_e.reshape(n_seq, CAP), ((0, 0), (0, LANES - CAP)))
    recv_q, recv_e = exchange_out(send_q.reshape(n_seq, CAP, SPAN, row_width), send_e, n_seq)
    kv_flat = neighbour_kv.reshape(neighbour_kv.shape[0], key_len, 2 * row_width)
    back_ctx, back_stats, weight_cols = attend_back(
        recv_q, recv_e, kv_flat, output_weight, heads_here, n_seq, n_db
    )
    back_ctx = back_ctx.reshape(places_total, SPAN, row_width)
    context = combine(back_ctx, back_stats, place, neighbour_count, heads_here)
    context = context.reshape(tok_rows, row_width)

    contexts = lax.all_gather(context, "db", axis=0, tiled=False)
    out = jnp.einsum(
        "str,srf->tf", contexts, weight_cols, preferred_element_type=jnp.float32
    )
    return out.astype(jnp.bfloat16)


def solution(mesh):
    in_specs = (
        P("seq", None),
        P(None, "db"),
        P("db", None),
        P("seq", None, None, "db"),
        P("seq", None),
        P("seq", None),
        P("seq"),
    )
    out_specs = P("seq", "db")
    return jax.shard_map(
        on_device, mesh=mesh, in_specs=in_specs, out_specs=out_specs, check_vma=False
    )
```

```python
import functools
import math

import jax
import jax.numpy as jnp
from jax import lax
from jax.experimental import pallas as pl
from jax.experimental.pallas import tpu as pltpu
from jax.sharding import PartitionSpec as P

HD = 128
SPAN = 64
K = 2
CAP = 3
LANES = 128
MESH = pl.DeviceIdType.MESH


def slot_places(neighbour_shard, neighbour_count):
    own_shard = neighbour_shard.reshape(-1)
    slots = own_shard.shape[0]
    own_live = (
        jnp.arange(K, dtype=jnp.int32)[None, :] < neighbour_count[:, None]
    ).reshape(-1)
    same = (own_shard[None, :] == own_shard[:, None]) & own_live[None, :]
    earlier = jnp.arange(slots)[None, :] < jnp.arange(slots)[:, None]
    own_rank = jnp.minimum(jnp.sum((same & earlier).astype(jnp.int32), axis=1), CAP - 1)
    return own_live, own_shard * CAP + own_rank


def peer_copy(src, dst, send_sem, recv_sem, device):
    return pltpu.make_async_remote_copy(
        src_ref=src, dst_ref=dst, send_sem=send_sem, recv_sem=recv_sem,
        device_id=device, device_id_type=MESH,
    )


def out_kernel(n_seq, send_q, send_e, recv_q, recv_e, qs, qr, es, er, ls):
    me_s = lax.axis_index("seq")
    me_d = lax.axis_index("db")

    barrier = pltpu.get_barrier_semaphore()

    @pl.loop(1, n_seq)
    def _(o):
        pl.semaphore_signal(barrier, inc=1, device_id=(lax.rem(me_s + o, n_seq), me_d),
                            device_id_type=MESH)

    pl.semaphore_wait(barrier, n_seq - 1)

    own = [
        pltpu.make_async_copy(send_q.at[me_s], recv_q.at[me_s], ls.at[0]),
        pltpu.make_async_copy(send_e.at[me_s], recv_e.at[me_s], ls.at[1]),
    ]
    for c in own:
        c.start()

    @pl.loop(1, n_seq)
    def _(o):
        d = lax.rem(me_s + o, n_seq)
        peer_copy(send_e.at[d], recv_e.at[me_s], es.at[d], er.at[me_s], (d, me_d)).start()
        peer_copy(send_q.at[d], recv_q.at[me_s], qs.at[d], qr.at[me_s], (d, me_d)).start()

    for c in own:
        c.wait()

    @pl.loop(1, n_seq)
    def _(o):
        d = lax.rem(me_s + o, n_seq)
        s = lax.rem(me_s + n_seq - o, n_seq)
        peer_copy(send_e.at[d], recv_e.at[me_s], es.at[d], er.at[me_s], (d, me_d)).wait_send()
        peer_copy(send_q.at[d], recv_q.at[me_s], qs.at[d], qr.at[me_s], (d, me_d)).wait_send()
        peer_copy(send_e.at[me_s], recv_e.at[s], es.at[s], er.at[s], (s, me_d)).wait_recv()
        peer_copy(send_q.at[me_s], recv_q.at[s], qs.at[s], qr.at[s], (s, me_d)).wait_recv()


def back_kernel(n_seq, ctx, stats, back_ctx, back_stats, cs, cr, ss, sr, ls):
    me_s = lax.axis_index("seq")
    me_d = lax.axis_index("db")
    barrier = pltpu.get_barrier_semaphore()

    @pl.loop(1, n_seq)
    def _(o):
        pl.semaphore_signal(barrier, inc=1, device_id=(lax.rem(me_s + o, n_seq), me_d),
                            device_id_type=MESH)

    pl.semaphore_wait(barrier, n_seq - 1)

    own = [
        pltpu.make_async_copy(ctx.at[me_s], back_ctx.at[me_s], ls.at[0]),
        pltpu.make_async_copy(stats.at[me_s], back_stats.at[me_s], ls.at[1]),
    ]
    for c in own:
        c.start()

    @pl.loop(1, n_seq)
    def _(o):
        d = lax.rem(me_s + o, n_seq)
        peer_copy(stats.at[d], back_stats.at[me_s], ss.at[d], sr.at[me_s], (d, me_d)).start()
        peer_copy(ctx.at[d], back_ctx.at[me_s], cs.at[d], cr.at[me_s], (d, me_d)).start()

    for c in own:
        c.wait()

    @pl.loop(1, n_seq)
    def _(o):
        d = lax.rem(me_s + o, n_seq)
        s = lax.rem(me_s + n_seq - o, n_seq)
        peer_copy(stats.at[d], back_stats.at[me_s], ss.at[d], sr.at[me_s], (d, me_d)).wait_send()
        peer_copy(ctx.at[d], back_ctx.at[me_s], cs.at[d], cr.at[me_s], (d, me_d)).wait_send()
        peer_copy(stats.at[me_s], back_stats.at[s], ss.at[s], sr.at[s], (s, me_d)).wait_recv()
        peer_copy(ctx.at[me_s], back_ctx.at[s], cs.at[s], cr.at[s], (s, me_d)).wait_recv()


def attend_kernel(scale, heads, rows, e_ref, q_ref, kv_ref, ctx_ref, stats_ref):
    key_len = SPAN * 2
    keys_total, width = kv_ref.shape[0], heads * HD
    per_tile = rows // SPAN
    col_block = lax.broadcasted_iota(jnp.int32, (1, keys_total), 1) // key_len
    row_block = lax.broadcasted_iota(jnp.int32, (rows, 1), 0) // SPAN

    def one_tile(t, carry):
        start = pl.multiple_of(t * rows, rows)
        row_entry = jnp.zeros((rows, 1), jnp.int32)
        for j in range(per_tile):
            row_entry = jnp.where(row_block == j, e_ref[t * per_tile + j], row_entry)
        named = col_block == row_entry
        for h in range(heads):
            q = q_ref[pl.ds(start, rows), h * HD:(h + 1) * HD]
            k = kv_ref[:, h * HD:(h + 1) * HD]
            v = kv_ref[:, width + h * HD:width + (h + 1) * HD]
            s = lax.dot_general(
                q, k, (((1,), (1,)), ((), ())), preferred_element_type=jnp.float32
            ) * scale
            s = jnp.where(named, s, -jnp.inf)
            top = jnp.max(s, axis=1, keepdims=True)
            w = jnp.exp(s - top)
            total = jnp.sum(w, axis=1, keepdims=True)
            ctx = jnp.dot(w.astype(jnp.bfloat16), v, preferred_element_type=jnp.float32)
            ctx_ref[pl.ds(start, rows), h * HD:(h + 1) * HD] = (ctx / total).astype(ctx_ref.dtype)
            stats_ref[pl.ds(start, rows), 2 * h:2 * h + 1] = top
            stats_ref[pl.ds(start, rows), 2 * h + 1:2 * h + 2] = total
        return carry

    lax.fori_loop(0, q_ref.shape[0] // rows, one_tile, 0)


def vmem_whole(shape):
    return pl.BlockSpec(shape, lambda *_: (0,) * len(shape))


def attend(recv_q, recv_e, kv_flat, heads):
    n_src, cap, span, width = recv_q.shape
    q_rows = recv_q.reshape(n_src * cap * span, width)
    kv_rows = kv_flat.reshape(-1, kv_flat.shape[2])
    stats_shape = (q_rows.shape[0], 2 * heads)
    grid_spec = pltpu.PrefetchScalarGridSpec(
        num_scalar_prefetch=1,
        grid=(1,),
        in_specs=[vmem_whole(q_rows.shape), vmem_whole(kv_rows.shape)],
        out_specs=[vmem_whole(q_rows.shape), vmem_whole(stats_shape)],
    )
    ctx, stats = pl.pallas_call(
        functools.partial(attend_kernel, 1.0 / math.sqrt(HD), heads, 4 * span),
        grid_spec=grid_spec,
        out_shape=(
            jax.ShapeDtypeStruct(q_rows.shape, jnp.bfloat16),
            jax.ShapeDtypeStruct(stats_shape, jnp.float32),
        ),
    )(recv_e, q_rows, kv_rows)
    return ctx.reshape(recv_q.shape), stats.reshape(n_src, cap, span, 2 * heads)


def attend_back_kernel(n_seq, n_db, heads, scale, e_ref, q_ref, kv_ref, w_loc, back_ctx,
                       back_stats, stage_ctx, stage_stats, w_cols, ctx_v, stats_v, cs, cr,
                       ss, sr, ws, wr, ls):
    me_s = lax.axis_index("seq")
    me_d = lax.axis_index("db")
    rows = stage_ctx.shape[1]
    keys_total = kv_ref.shape[0]
    width = heads * HD
    cap = rows // SPAN
    key_block = lax.broadcasted_iota(jnp.int32, (keys_total, 1), 0) // (2 * SPAN)
    lane_place = lax.broadcasted_iota(jnp.int32, (1, rows), 1) // SPAN

    barrier = pltpu.get_barrier_semaphore()

    @pl.loop(1, n_seq)
    def _(o):
        pl.semaphore_signal(barrier, inc=1, device_id=(lax.rem(me_s + o, n_seq), me_d),
                            device_id_type=MESH)

    @pl.loop(1, n_db)
    def _(o):
        pl.semaphore_signal(barrier, inc=1, device_id=(me_s, lax.rem(me_d + o, n_db)),
                            device_id_type=MESH)

    pl.semaphore_wait(barrier, (n_seq - 1) + (n_db - 1))

    features = w_cols.shape[2]

    def w_src(d):
        return w_loc.at[:, pl.ds(pl.multiple_of(d * features, features), features)]

    own_w = pltpu.make_async_copy(w_src(me_d), w_cols.at[me_d], ls.at[4])
    own_w.start()

    @pl.loop(1, n_db)
    def _(o):
        d = lax.rem(me_d + o, n_db)
        peer_copy(w_src(d), w_cols.at[me_d], ws.at[d], wr.at[me_d], (me_s, d)).start()

    def compute(d):
        entry = jnp.zeros((1, rows), jnp.int32)
        for j in range(cap):
            entry = jnp.where(lane_place == j, e_ref[d, j], entry)
        named = key_block == entry
        start = pl.multiple_of(d * rows, rows)
        stats_v[...] = jnp.zeros_like(stats_v)
        for h in range(heads):
            q = q_ref[pl.ds(start, rows), h * HD:(h + 1) * HD]
            k = kv_ref[:, h * HD:(h + 1) * HD]
            v = kv_ref[:, width + h * HD:width + (h + 1) * HD]
            st = lax.dot_general(
                k, q, (((1,), (1,)), ((), ())), preferred_element_type=jnp.float32
            ) * scale
            st = jnp.where(named, st, -jnp.inf)
            top = jnp.max(st, axis=0, keepdims=True)
            w = jnp.exp(st - top)
            total = jnp.sum(w, axis=0, keepdims=True)
            u = lax.dot_general(
                w.astype(jnp.bfloat16), v, (((0,), (0,)), ((), ())),
                preferred_element_type=jnp.float32,
            )
            ctx_v[:, h * HD:(h + 1) * HD] = u.astype(ctx_v.dtype)
            stats_v[2 * h:2 * h + 1, 0:rows] = top
            stats_v[2 * h + 1:2 * h + 2, 0:rows] = total
        staged = [
            pltpu.make_async_copy(ctx_v, stage_ctx.at[d], ls.at[0]),
            pltpu.make_async_copy(stats_v, stage_stats.at[d], ls.at[1]),
        ]
        for c in staged:
            c.start()
        for c in staged:
            c.wait()

    compute(me_s)
    own = [
        pltpu.make_async_copy(stage_ctx.at[me_s], back_ctx.at[me_s], ls.at[2]),
        pltpu.make_async_copy(stage_stats.at[me_s], back_stats.at[me_s], ls.at[3]),
    ]
    for c in own:
        c.start()

    @pl.loop(1, n_seq)
    def _(o):
        d = lax.rem(me_s + o, n_seq)
        compute(d)
        peer_copy(stage_stats.at[d], back_stats.at[me_s], ss.at[d], sr.at[me_s], (d, me_d)).start()
        peer_copy(stage_ctx.at[d], back_ctx.at[me_s], cs.at[d], cr.at[me_s], (d, me_d)).start()

    for c in own:
        c.wait()

    @pl.loop(1, n_seq)
    def _(o):
        d = lax.rem(me_s + o, n_seq)
        s = lax.rem(me_s + n_seq - o, n_seq)
        peer_copy(stage_stats.at[d], back_stats.at[me_s], ss.at[d], sr.at[me_s], (d, me_d)).wait_send()
        peer_copy(stage_ctx.at[d], back_ctx.at[me_s], cs.at[d], cr.at[me_s], (d, me_d)).wait_send()
        peer_copy(stage_stats.at[me_s], back_stats.at[s], ss.at[s], sr.at[s], (s, me_d)).wait_recv()
        peer_copy(stage_ctx.at[me_s], back_ctx.at[s], cs.at[s], cr.at[s], (s, me_d)).wait_recv()

    own_w.wait()

    @pl.loop(1, n_db)
    def _(o):
        d = lax.rem(me_d + o, n_db)
        s = lax.rem(me_d + n_db - o, n_db)
        peer_copy(w_src(d), w_cols.at[me_d], ws.at[d], wr.at[me_d], (me_s, d)).wait_send()
        peer_copy(w_src(me_d), w_cols.at[s], ws.at[s], wr.at[s], (me_s, s)).wait_recv()


def attend_back(recv_q, recv_e, kv_flat, w_loc, heads, n_seq, n_db):
    n_src, cap, span, width = recv_q.shape
    rows = cap * span
    q_rows = recv_q.reshape(n_src * rows, width)
    kv_rows = kv_flat.reshape(-1, kv_flat.shape[2])
    stats_shape = (n_src, 8, 2 * LANES)
    ctx_shape = (n_src, rows, width)
    dma = pltpu.SemaphoreType.DMA
    outs = pl.pallas_call(
        functools.partial(attend_back_kernel, n_seq, n_db, heads, 1.0 / math.sqrt(HD)),
        out_shape=(
            jax.ShapeDtypeStruct(ctx_shape, jnp.bfloat16),
            jax.ShapeDtypeStruct(stats_shape, jnp.float32),
            jax.ShapeDtypeStruct(ctx_shape, jnp.bfloat16),
            jax.ShapeDtypeStruct(stats_shape, jnp.float32),
            jax.ShapeDtypeStruct((n_db, w_loc.shape[0], w_loc.shape[1] // n_db), w_loc.dtype),
        ),
        in_specs=[
            pl.BlockSpec(memory_space=pltpu.SMEM),
            pl.BlockSpec(memory_space=pltpu.VMEM),
            pl.BlockSpec(memory_space=pltpu.VMEM),
            any_spec(),
        ],
        out_specs=(any_spec(), any_spec(), any_spec(), any_spec(), any_spec()),
        scratch_shapes=[
            pltpu.VMEM((rows, width), jnp.bfloat16),
            pltpu.VMEM(stats_shape[1:], jnp.float32),
            dma((n_seq,)), dma((n_seq,)), dma((n_seq,)), dma((n_seq,)),
            dma((n_db,)), dma((n_db,)), dma((5,)),
        ],
        compiler_params=pltpu.CompilerParams(collective_id=1, has_side_effects=True),
    )(recv_e, q_rows, kv_rows, w_loc)
    return outs[0], outs[1], outs[4]


def combine_kernel(heads, place_ref, count_ref, ctx_ref, stats_ref, out_ref, stats_t):
    for s in range(stats_ref.shape[0]):
        stats_t[s] = jnp.transpose(stats_ref[s])

    def one_span(c, carry):
        p0 = place_ref[c * K]
        p1 = place_ref[c * K + 1]
        r0 = pl.multiple_of(lax.rem(p0, CAP) * SPAN, SPAN)
        r1 = pl.multiple_of(lax.rem(p1, CAP) * SPAN, SPAN)
        st0 = stats_t[p0 // CAP, pl.ds(r0, SPAN), :]
        st1 = stats_t[p1 // CAP, pl.ds(r1, SPAN), :]
        live1 = count_ref[c] > 1
        for h in range(heads):
            cols = slice(h * HD, (h + 1) * HD)
            m0, l0 = st0[:, 2 * h:2 * h + 1], st0[:, 2 * h + 1:2 * h + 2]
            m1, l1 = st1[:, 2 * h:2 * h + 1], st1[:, 2 * h + 1:2 * h + 2]
            best = jnp.where(live1, jnp.maximum(m0, m1), m0)
            a0 = jnp.exp(m0 - best)
            a1 = jnp.where(live1, jnp.exp(m1 - best), 0.0)
            u0 = ctx_ref[p0, :, cols].astype(jnp.float32)
            u1 = jnp.where(live1, ctx_ref[p1, :, cols].astype(jnp.float32), 0.0)
            out_ref[c, :, cols] = (
                (a0 * u0 + a1 * u1) / (a0 * l0 + a1 * l1)
            ).astype(out_ref.dtype)
        return carry

    lax.fori_loop(0, out_ref.shape[0], one_span, 0)


def combine(back_ctx, back_stats, place, neighbour_count, heads):
    places, span, width = back_ctx.shape
    spans = neighbour_count.shape[0]
    n_src, st_rows, st_cols = back_stats.shape
    grid_spec = pltpu.PrefetchScalarGridSpec(
        num_scalar_prefetch=2,
        grid=(1,),
        in_specs=[vmem_whole(back_ctx.shape), vmem_whole(back_stats.shape)],
        out_specs=vmem_whole((spans, span, width)),
        scratch_shapes=[pltpu.VMEM((n_src, st_cols, st_rows), jnp.float32)],
    )
    return pl.pallas_call(
        functools.partial(combine_kernel, heads),
        grid_spec=grid_spec,
        out_shape=jax.ShapeDtypeStruct((spans, span, width), jnp.bfloat16),
    )(place, neighbour_count, back_ctx, back_stats)


def pack_kernel(src_ref, q_ref, out_ref):
    def one_place(p, carry):
        span = src_ref[p]
        rows = q_ref[jnp.maximum(span, 0)]
        out_ref[p] = jnp.where(span >= 0, rows, jnp.zeros_like(rows))
        return carry

    lax.fori_loop(0, out_ref.shape[0], one_place, 0)


def pack(queries, src_span, places):
    grid_spec = pltpu.PrefetchScalarGridSpec(
        num_scalar_prefetch=1,
        grid=(1,),
        in_specs=[vmem_whole(queries.shape)],
        out_specs=vmem_whole((places,) + queries.shape[1:]),
    )
    return pl.pallas_call(
        pack_kernel,
        grid_spec=grid_spec,
        out_shape=jax.ShapeDtypeStruct((places,) + queries.shape[1:], queries.dtype),
    )(src_span, queries)


def any_spec():
    return pl.BlockSpec(memory_space=pl.ANY)


def exchange_out(send_q, send_e, n_seq):
    dma = pltpu.SemaphoreType.DMA
    return pl.pallas_call(
        functools.partial(out_kernel, n_seq),
        out_shape=(
            jax.ShapeDtypeStruct(send_q.shape, send_q.dtype),
            jax.ShapeDtypeStruct(send_e.shape, send_e.dtype),
        ),
        in_specs=[any_spec()] * 2,
        out_specs=(any_spec(), any_spec()),
        scratch_shapes=[dma((n_seq,)), dma((n_seq,)), dma((n_seq,)), dma((n_seq,)), dma((2,))],
        compiler_params=pltpu.CompilerParams(collective_id=0, has_side_effects=True),
    )(send_q, send_e)


def exchange_back(ctx, stats, n_seq):
    dma = pltpu.SemaphoreType.DMA
    return pl.pallas_call(
        functools.partial(back_kernel, n_seq),
        out_shape=(
            jax.ShapeDtypeStruct(ctx.shape, ctx.dtype),
            jax.ShapeDtypeStruct(stats.shape, stats.dtype),
        ),
        in_specs=[any_spec()] * 2,
        out_specs=(any_spec(), any_spec()),
        scratch_shapes=[dma((n_seq,)), dma((n_seq,)), dma((n_seq,)), dma((n_seq,)), dma((2,))],
        compiler_params=pltpu.CompilerParams(collective_id=1, has_side_effects=True),
    )(ctx, stats)


def on_device(
    decoder_states,
    query_weight,
    output_weight,
    neighbour_kv,
    neighbour_shard,
    neighbour_entry,
    neighbour_count,
):
    tok_rows = decoder_states.shape[0]
    span_total = tok_rows // SPAN
    row_width = query_weight.shape[1]
    heads_here = row_width // HD
    key_len = neighbour_kv.shape[1]
    n_seq = lax.psum(1, "seq")
    n_db = lax.psum(1, "db")
    places_total = n_seq * CAP
    queries = jnp.dot(decoder_states, query_weight, preferred_element_type=jnp.float32).astype(
        jnp.bfloat16
    )
    queries = queries.reshape(span_total, SPAN, row_width)

    live, place = slot_places(neighbour_shard, neighbour_count)
    target = jnp.where(live, place, places_total)
    span_of_slot = jnp.arange(span_total * K, dtype=jnp.int32) // K
    src_span = jnp.full((places_total,), -1, jnp.int32)
    src_span = src_span.at[target].set(span_of_slot, mode="drop")
    send_q = pack(queries, src_span, places_total)
    send_e = jnp.zeros((places_total,), jnp.int32)
    send_e = send_e.at[target].set(neighbour_entry.reshape(-1), mode="drop")
    send_e = jnp.pad(send_e.reshape(n_seq, CAP), ((0, 0), (0, LANES - CAP)))
    recv_q, recv_e = exchange_out(send_q.reshape(n_seq, CAP, SPAN, row_width), send_e, n_seq)
    kv_flat = neighbour_kv.reshape(neighbour_kv.shape[0], key_len, 2 * row_width)
    back_ctx, back_stats, weight_cols = attend_back(
        recv_q, recv_e, kv_flat, output_weight, heads_here, n_seq, n_db
    )
    back_ctx = back_ctx.reshape(places_total, SPAN, row_width)
    context = combine(back_ctx, back_stats, place, neighbour_count, heads_here)
    context = context.reshape(tok_rows, row_width)

    contexts = lax.all_gather(context, "db", axis=0, tiled=False)
    out = jnp.einsum(
        "str,srf->tf", contexts, weight_cols, preferred_element_type=jnp.float32
    )
    return out.astype(jnp.bfloat16)


def solution(mesh):
    in_specs = (
        P("seq", None),
        P(None, "db"),
        P("db", None),
        P("seq", None, None, "db"),
        P("seq", None),
        P("seq", None),
        P("seq"),
    )
    out_specs = P("seq", "db")
    return jax.shard_map(
        on_device, mesh=mesh, in_specs=in_specs, out_specs=out_specs, check_vma=False
    )
```

```python
import functools
import math

import jax
import jax.numpy as jnp
from jax import lax
from jax.experimental import pallas as pl
from jax.experimental.pallas import tpu as pltpu
from jax.sharding import PartitionSpec as P

HD = 128
SPAN = 64
K = 2
CAP = 3
LANES = 128
MESH = pl.DeviceIdType.MESH


def slot_places(neighbour_shard, neighbour_count):
    own_shard = neighbour_shard.reshape(-1)
    slots = own_shard.shape[0]
    own_live = (
        jnp.arange(K, dtype=jnp.int32)[None, :] < neighbour_count[:, None]
    ).reshape(-1)
    same = (own_shard[None, :] == own_shard[:, None]) & own_live[None, :]
    earlier = jnp.arange(slots)[None, :] < jnp.arange(slots)[:, None]
    own_rank = jnp.minimum(jnp.sum((same & earlier).astype(jnp.int32), axis=1), CAP - 1)
    return own_live, own_shard * CAP + own_rank


def peer_copy(src, dst, send_sem, recv_sem, device):
    return pltpu.make_async_remote_copy(
        src_ref=src, dst_ref=dst, send_sem=send_sem, recv_sem=recv_sem,
        device_id=device, device_id_type=MESH,
    )


def out_kernel(n_seq, send_q, send_e, recv_q, recv_e, qs, qr, es, er, ls):
    me_s = lax.axis_index("seq")
    me_d = lax.axis_index("db")

    barrier = pltpu.get_barrier_semaphore()

    @pl.loop(1, n_seq)
    def _(o):
        pl.semaphore_signal(barrier, inc=1, device_id=(lax.rem(me_s + o, n_seq), me_d),
                            device_id_type=MESH)

    pl.semaphore_wait(barrier, n_seq - 1)

    own = [
        pltpu.make_async_copy(send_q.at[me_s], recv_q.at[me_s], ls.at[0]),
        pltpu.make_async_copy(send_e.at[me_s], recv_e.at[me_s], ls.at[1]),
    ]
    for c in own:
        c.start()

    @pl.loop(1, n_seq)
    def _(o):
        d = lax.rem(me_s + o, n_seq)
        peer_copy(send_e.at[d], recv_e.at[me_s], es.at[d], er.at[me_s], (d, me_d)).start()
        peer_copy(send_q.at[d], recv_q.at[me_s], qs.at[d], qr.at[me_s], (d, me_d)).start()

    for c in own:
        c.wait()

    @pl.loop(1, n_seq)
    def _(o):
        d = lax.rem(me_s + o, n_seq)
        s = lax.rem(me_s + n_seq - o, n_seq)
        peer_copy(send_e.at[d], recv_e.at[me_s], es.at[d], er.at[me_s], (d, me_d)).wait_send()
        peer_copy(send_q.at[d], recv_q.at[me_s], qs.at[d], qr.at[me_s], (d, me_d)).wait_send()
        peer_copy(send_e.at[me_s], recv_e.at[s], es.at[s], er.at[s], (s, me_d)).wait_recv()
        peer_copy(send_q.at[me_s], recv_q.at[s], qs.at[s], qr.at[s], (s, me_d)).wait_recv()


def back_kernel(n_seq, ctx, stats, back_ctx, back_stats, cs, cr, ss, sr, ls):
    me_s = lax.axis_index("seq")
    me_d = lax.axis_index("db")
    barrier = pltpu.get_barrier_semaphore()

    @pl.loop(1, n_seq)
    def _(o):
        pl.semaphore_signal(barrier, inc=1, device_id=(lax.rem(me_s + o, n_seq), me_d),
                            device_id_type=MESH)

    pl.semaphore_wait(barrier, n_seq - 1)

    own = [
        pltpu.make_async_copy(ctx.at[me_s], back_ctx.at[me_s], ls.at[0]),
        pltpu.make_async_copy(stats.at[me_s], back_stats.at[me_s], ls.at[1]),
    ]
    for c in own:
        c.start()

    @pl.loop(1, n_seq)
    def _(o):
        d = lax.rem(me_s + o, n_seq)
        peer_copy(stats.at[d], back_stats.at[me_s], ss.at[d], sr.at[me_s], (d, me_d)).start()
        peer_copy(ctx.at[d], back_ctx.at[me_s], cs.at[d], cr.at[me_s], (d, me_d)).start()

    for c in own:
        c.wait()

    @pl.loop(1, n_seq)
    def _(o):
        d = lax.rem(me_s + o, n_seq)
        s = lax.rem(me_s + n_seq - o, n_seq)
        peer_copy(stats.at[d], back_stats.at[me_s], ss.at[d], sr.at[me_s], (d, me_d)).wait_send()
        peer_copy(ctx.at[d], back_ctx.at[me_s], cs.at[d], cr.at[me_s], (d, me_d)).wait_send()
        peer_copy(stats.at[me_s], back_stats.at[s], ss.at[s], sr.at[s], (s, me_d)).wait_recv()
        peer_copy(ctx.at[me_s], back_ctx.at[s], cs.at[s], cr.at[s], (s, me_d)).wait_recv()


def attend_kernel(scale, heads, rows, e_ref, q_ref, kv_ref, ctx_ref, stats_ref):
    key_len = SPAN * 2
    keys_total, width = kv_ref.shape[0], heads * HD
    per_tile = rows // SPAN
    col_block = lax.broadcasted_iota(jnp.int32, (1, keys_total), 1) // key_len
    row_block = lax.broadcasted_iota(jnp.int32, (rows, 1), 0) // SPAN

    def one_tile(t, carry):
        start = pl.multiple_of(t * rows, rows)
        row_entry = jnp.zeros((rows, 1), jnp.int32)
        for j in range(per_tile):
            row_entry = jnp.where(row_block == j, e_ref[t * per_tile + j], row_entry)
        named = col_block == row_entry
        for h in range(heads):
            q = q_ref[pl.ds(start, rows), h * HD:(h + 1) * HD]
            k = kv_ref[:, h * HD:(h + 1) * HD]
            v = kv_ref[:, width + h * HD:width + (h + 1) * HD]
            s = lax.dot_general(
                q, k, (((1,), (1,)), ((), ())), preferred_element_type=jnp.float32
            ) * scale
            s = jnp.where(named, s, -jnp.inf)
            top = jnp.max(s, axis=1, keepdims=True)
            w = jnp.exp(s - top)
            total = jnp.sum(w, axis=1, keepdims=True)
            ctx = jnp.dot(w.astype(jnp.bfloat16), v, preferred_element_type=jnp.float32)
            ctx_ref[pl.ds(start, rows), h * HD:(h + 1) * HD] = (ctx / total).astype(ctx_ref.dtype)
            stats_ref[pl.ds(start, rows), 2 * h:2 * h + 1] = top
            stats_ref[pl.ds(start, rows), 2 * h + 1:2 * h + 2] = total
        return carry

    lax.fori_loop(0, q_ref.shape[0] // rows, one_tile, 0)


def vmem_whole(shape):
    return pl.BlockSpec(shape, lambda *_: (0,) * len(shape))


def attend(recv_q, recv_e, kv_flat, heads):
    n_src, cap, span, width = recv_q.shape
    q_rows = recv_q.reshape(n_src * cap * span, width)
    kv_rows = kv_flat.reshape(-1, kv_flat.shape[2])
    stats_shape = (q_rows.shape[0], 2 * heads)
    grid_spec = pltpu.PrefetchScalarGridSpec(
        num_scalar_prefetch=1,
        grid=(1,),
        in_specs=[vmem_whole(q_rows.shape), vmem_whole(kv_rows.shape)],
        out_specs=[vmem_whole(q_rows.shape), vmem_whole(stats_shape)],
    )
    ctx, stats = pl.pallas_call(
        functools.partial(attend_kernel, 1.0 / math.sqrt(HD), heads, 4 * span),
        grid_spec=grid_spec,
        out_shape=(
            jax.ShapeDtypeStruct(q_rows.shape, jnp.bfloat16),
            jax.ShapeDtypeStruct(stats_shape, jnp.float32),
        ),
    )(recv_e, q_rows, kv_rows)
    return ctx.reshape(recv_q.shape), stats.reshape(n_src, cap, span, 2 * heads)


def attend_back_kernel(n_seq, n_db, heads, scale, e_ref, q_ref, kv_ref, w_loc, back_ctx,
                       back_stats, stage_ctx, stage_stats, w_cols, ctx_v, stats_v, cs, cr,
                       ss, sr, ws, wr, ls, stg):
    me_s = lax.axis_index("seq")
    me_d = lax.axis_index("db")
    rows = stage_ctx.shape[1]
    keys_total = kv_ref.shape[0]
    width = heads * HD
    cap = rows // SPAN
    key_block = lax.broadcasted_iota(jnp.int32, (keys_total, 1), 0) // (2 * SPAN)
    lane_place = lax.broadcasted_iota(jnp.int32, (1, rows), 1) // SPAN

    barrier = pltpu.get_barrier_semaphore()

    @pl.loop(1, n_seq)
    def _(o):
        pl.semaphore_signal(barrier, inc=1, device_id=(lax.rem(me_s + o, n_seq), me_d),
                            device_id_type=MESH)

    @pl.loop(1, n_db)
    def _(o):
        pl.semaphore_signal(barrier, inc=1, device_id=(me_s, lax.rem(me_d + o, n_db)),
                            device_id_type=MESH)

    pl.semaphore_wait(barrier, (n_seq - 1) + (n_db - 1))

    features = w_cols.shape[2]

    def w_src(d):
        return w_loc.at[:, pl.ds(pl.multiple_of(d * features, features), features)]

    own_w = pltpu.make_async_copy(w_src(me_d), w_cols.at[me_d], ls.at[4])
    own_w.start()

    @pl.loop(1, n_db)
    def _(o):
        d = lax.rem(me_d + o, n_db)
        peer_copy(w_src(d), w_cols.at[me_d], ws.at[d], wr.at[me_d], (me_s, d)).start()

    def compute(d, slot):
        entry = jnp.zeros((1, rows), jnp.int32)
        for j in range(cap):
            entry = jnp.where(lane_place == j, e_ref[d, j], entry)
        named = key_block == entry
        start = pl.multiple_of(d * rows, rows)
        stats_v[slot] = jnp.zeros(stats_v.shape[1:], stats_v.dtype)
        for h in range(heads):
            q = q_ref[pl.ds(start, rows), h * HD:(h + 1) * HD]
            k = kv_ref[:, h * HD:(h + 1) * HD]
            v = kv_ref[:, width + h * HD:width + (h + 1) * HD]
            st = lax.dot_general(
                k, q, (((1,), (1,)), ((), ())), preferred_element_type=jnp.float32
            ) * scale
            st = jnp.where(named, st, -jnp.inf)
            top = jnp.max(st, axis=0, keepdims=True)
            w = jnp.exp(st - top)
            total = jnp.sum(w, axis=0, keepdims=True)
            u = lax.dot_general(
                w.astype(jnp.bfloat16), v, (((0,), (0,)), ((), ())),
                preferred_element_type=jnp.float32,
            )
            ctx_v[slot, :, h * HD:(h + 1) * HD] = u.astype(ctx_v.dtype)
            stats_v[slot, 2 * h:2 * h + 1, 0:rows] = top
            stats_v[slot, 2 * h + 1:2 * h + 2, 0:rows] = total

    def staged(d, slot):
        return [
            pltpu.make_async_copy(ctx_v.at[slot], stage_ctx.at[d], stg.at[0, slot]),
            pltpu.make_async_copy(stats_v.at[slot], stage_stats.at[d], stg.at[1, slot]),
        ]

    def send(d):
        peer_copy(stage_stats.at[d], back_stats.at[me_s], ss.at[d], sr.at[me_s], (d, me_d)).start()
        peer_copy(stage_ctx.at[d], back_ctx.at[me_s], cs.at[d], cr.at[me_s], (d, me_d)).start()

    compute(me_s, 0)
    for c in staged(me_s, 0):
        c.start()
    for c in staged(me_s, 0):
        c.wait()
    own = [
        pltpu.make_async_copy(stage_ctx.at[me_s], back_ctx.at[me_s], ls.at[2]),
        pltpu.make_async_copy(stage_stats.at[me_s], back_stats.at[me_s], ls.at[3]),
    ]
    for c in own:
        c.start()

    @pl.loop(1, n_seq)
    def _(o):
        d = lax.rem(me_s + o, n_seq)
        slot = lax.rem(o, 2)
        compute(d, slot)
        for c in staged(d, slot):
            c.start()

        @pl.when(o > 1)
        def _():
            prev = lax.rem(me_s + o - 1, n_seq)
            for c in staged(prev, 1 - slot):
                c.wait()
            send(prev)

    last = lax.rem(me_s + n_seq - 1, n_seq)
    for c in staged(last, (n_seq - 1) % 2):
        c.wait()
    send(last)

    for c in own:
        c.wait()

    @pl.loop(1, n_seq)
    def _(o):
        d = lax.rem(me_s + o, n_seq)
        s = lax.rem(me_s + n_seq - o, n_seq)
        peer_copy(stage_stats.at[d], back_stats.at[me_s], ss.at[d], sr.at[me_s], (d, me_d)).wait_send()
        peer_copy(stage_ctx.at[d], back_ctx.at[me_s], cs.at[d], cr.at[me_s], (d, me_d)).wait_send()
        peer_copy(stage_stats.at[me_s], back_stats.at[s], ss.at[s], sr.at[s], (s, me_d)).wait_recv()
        peer_copy(stage_ctx.at[me_s], back_ctx.at[s], cs.at[s], cr.at[s], (s, me_d)).wait_recv()

    own_w.wait()

    @pl.loop(1, n_db)
    def _(o):
        d = lax.rem(me_d + o, n_db)
        s = lax.rem(me_d + n_db - o, n_db)
        peer_copy(w_src(d), w_cols.at[me_d], ws.at[d], wr.at[me_d], (me_s, d)).wait_send()
        peer_copy(w_src(me_d), w_cols.at[s], ws.at[s], wr.at[s], (me_s, s)).wait_recv()


def attend_back(recv_q, recv_e, kv_flat, w_loc, heads, n_seq, n_db):
    n_src, cap, span, width = recv_q.shape
    rows = cap * span
    q_rows = recv_q.reshape(n_src * rows, width)
    kv_rows = kv_flat.reshape(-1, kv_flat.shape[2])
    stats_shape = (n_src, 8, 2 * LANES)
    ctx_shape = (n_src, rows, width)
    dma = pltpu.SemaphoreType.DMA
    outs = pl.pallas_call(
        functools.partial(attend_back_kernel, n_seq, n_db, heads, 1.0 / math.sqrt(HD)),
        out_shape=(
            jax.ShapeDtypeStruct(ctx_shape, jnp.bfloat16),
            jax.ShapeDtypeStruct(stats_shape, jnp.float32),
            jax.ShapeDtypeStruct(ctx_shape, jnp.bfloat16),
            jax.ShapeDtypeStruct(stats_shape, jnp.float32),
            jax.ShapeDtypeStruct((n_db, w_loc.shape[0], w_loc.shape[1] // n_db), w_loc.dtype),
        ),
        in_specs=[
            pl.BlockSpec(memory_space=pltpu.SMEM),
            pl.BlockSpec(memory_space=pltpu.VMEM),
            pl.BlockSpec(memory_space=pltpu.VMEM),
            any_spec(),
        ],
        out_specs=(any_spec(), any_spec(), any_spec(), any_spec(), any_spec()),
        scratch_shapes=[
            pltpu.VMEM((2, rows, width), jnp.bfloat16),
            pltpu.VMEM((2,) + stats_shape[1:], jnp.float32),
            dma((n_seq,)), dma((n_seq,)), dma((n_seq,)), dma((n_seq,)),
            dma((n_db,)), dma((n_db,)), dma((5,)), dma((2, 2)),
        ],
        compiler_params=pltpu.CompilerParams(collective_id=1, has_side_effects=True),
    )(recv_e, q_rows, kv_rows, w_loc)
    return outs[0], outs[1], outs[4]


def combine_kernel(heads, place_ref, count_ref, ctx_ref, stats_ref, out_ref, stats_t):
    for s in range(stats_ref.shape[0]):
        stats_t[s] = jnp.transpose(stats_ref[s])

    def one_span(c, carry):
        p0 = place_ref[c * K]
        p1 = place_ref[c * K + 1]
        r0 = pl.multiple_of(lax.rem(p0, CAP) * SPAN, SPAN)
        r1 = pl.multiple_of(lax.rem(p1, CAP) * SPAN, SPAN)
        st0 = stats_t[p0 // CAP, pl.ds(r0, SPAN), :]
        st1 = stats_t[p1 // CAP, pl.ds(r1, SPAN), :]
        live1 = count_ref[c] > 1
        for h in range(heads):
            cols = slice(h * HD, (h + 1) * HD)
            m0, l0 = st0[:, 2 * h:2 * h + 1], st0[:, 2 * h + 1:2 * h + 2]
            m1, l1 = st1[:, 2 * h:2 * h + 1], st1[:, 2 * h + 1:2 * h + 2]
            best = jnp.where(live1, jnp.maximum(m0, m1), m0)
            a0 = jnp.exp(m0 - best)
            a1 = jnp.where(live1, jnp.exp(m1 - best), 0.0)
            u0 = ctx_ref[p0, :, cols].astype(jnp.float32)
            u1 = jnp.where(live1, ctx_ref[p1, :, cols].astype(jnp.float32), 0.0)
            out_ref[c, :, cols] = (
                (a0 * u0 + a1 * u1) / (a0 * l0 + a1 * l1)
            ).astype(out_ref.dtype)
        return carry

    lax.fori_loop(0, out_ref.shape[0], one_span, 0)


def combine(back_ctx, back_stats, place, neighbour_count, heads):
    places, span, width = back_ctx.shape
    spans = neighbour_count.shape[0]
    n_src, st_rows, st_cols = back_stats.shape
    grid_spec = pltpu.PrefetchScalarGridSpec(
        num_scalar_prefetch=2,
        grid=(1,),
        in_specs=[vmem_whole(back_ctx.shape), vmem_whole(back_stats.shape)],
        out_specs=vmem_whole((spans, span, width)),
        scratch_shapes=[pltpu.VMEM((n_src, st_cols, st_rows), jnp.float32)],
    )
    return pl.pallas_call(
        functools.partial(combine_kernel, heads),
        grid_spec=grid_spec,
        out_shape=jax.ShapeDtypeStruct((spans, span, width), jnp.bfloat16),
    )(place, neighbour_count, back_ctx, back_stats)


def pack_kernel(src_ref, q_ref, out_ref):
    def one_place(p, carry):
        span = src_ref[p]
        rows = q_ref[jnp.maximum(span, 0)]
        out_ref[p] = jnp.where(span >= 0, rows, jnp.zeros_like(rows))
        return carry

    lax.fori_loop(0, out_ref.shape[0], one_place, 0)


def pack(queries, src_span, places):
    grid_spec = pltpu.PrefetchScalarGridSpec(
        num_scalar_prefetch=1,
        grid=(1,),
        in_specs=[vmem_whole(queries.shape)],
        out_specs=vmem_whole((places,) + queries.shape[1:]),
    )
    return pl.pallas_call(
        pack_kernel,
        grid_spec=grid_spec,
        out_shape=jax.ShapeDtypeStruct((places,) + queries.shape[1:], queries.dtype),
    )(src_span, queries)


def any_spec():
    return pl.BlockSpec(memory_space=pl.ANY)


def exchange_out(send_q, send_e, n_seq):
    dma = pltpu.SemaphoreType.DMA
    return pl.pallas_call(
        functools.partial(out_kernel, n_seq),
        out_shape=(
            jax.ShapeDtypeStruct(send_q.shape, send_q.dtype),
            jax.ShapeDtypeStruct(send_e.shape, send_e.dtype),
        ),
        in_specs=[any_spec()] * 2,
        out_specs=(any_spec(), any_spec()),
        scratch_shapes=[dma((n_seq,)), dma((n_seq,)), dma((n_seq,)), dma((n_seq,)), dma((2,))],
        compiler_params=pltpu.CompilerParams(collective_id=0, has_side_effects=True),
    )(send_q, send_e)


def exchange_back(ctx, stats, n_seq):
    dma = pltpu.SemaphoreType.DMA
    return pl.pallas_call(
        functools.partial(back_kernel, n_seq),
        out_shape=(
            jax.ShapeDtypeStruct(ctx.shape, ctx.dtype),
            jax.ShapeDtypeStruct(stats.shape, stats.dtype),
        ),
        in_specs=[any_spec()] * 2,
        out_specs=(any_spec(), any_spec()),
        scratch_shapes=[dma((n_seq,)), dma((n_seq,)), dma((n_seq,)), dma((n_seq,)), dma((2,))],
        compiler_params=pltpu.CompilerParams(collective_id=1, has_side_effects=True),
    )(ctx, stats)


def on_device(
    decoder_states,
    query_weight,
    output_weight,
    neighbour_kv,
    neighbour_shard,
    neighbour_entry,
    neighbour_count,
):
    tok_rows = decoder_states.shape[0]
    span_total = tok_rows // SPAN
    row_width = query_weight.shape[1]
    heads_here = row_width // HD
    key_len = neighbour_kv.shape[1]
    n_seq = lax.psum(1, "seq")
    n_db = lax.psum(1, "db")
    places_total = n_seq * CAP
    queries = jnp.dot(decoder_states, query_weight, preferred_element_type=jnp.float32).astype(
        jnp.bfloat16
    )
    queries = queries.reshape(span_total, SPAN, row_width)

    live, place = slot_places(neighbour_shard, neighbour_count)
    target = jnp.where(live, place, places_total)
    span_of_slot = jnp.arange(span_total * K, dtype=jnp.int32) // K
    src_span = jnp.full((places_total,), -1, jnp.int32)
    src_span = src_span.at[target].set(span_of_slot, mode="drop")
    send_q = pack(queries, src_span, places_total)
    send_e = jnp.zeros((places_total,), jnp.int32)
    send_e = send_e.at[target].set(neighbour_entry.reshape(-1), mode="drop")
    send_e = jnp.pad(send_e.reshape(n_seq, CAP), ((0, 0), (0, LANES - CAP)))
    recv_q, recv_e = exchange_out(send_q.reshape(n_seq, CAP, SPAN, row_width), send_e, n_seq)
    kv_flat = neighbour_kv.reshape(neighbour_kv.shape[0], key_len, 2 * row_width)
    back_ctx, back_stats, weight_cols = attend_back(
        recv_q, recv_e, kv_flat, output_weight, heads_here, n_seq, n_db
    )
    back_ctx = back_ctx.reshape(places_total, SPAN, row_width)
    context = combine(back_ctx, back_stats, place, neighbour_count, heads_here)
    context = context.reshape(tok_rows, row_width)

    contexts = lax.all_gather(context, "db", axis=0, tiled=False)
    out = jnp.einsum(
        "str,srf->tf", contexts, weight_cols, preferred_element_type=jnp.float32
    )
    return out.astype(jnp.bfloat16)


def solution(mesh):
    in_specs = (
        P("seq", None),
        P(None, "db"),
        P("db", None),
        P("seq", None, None, "db"),
        P("seq", None),
        P("seq", None),
        P("seq"),
    )
    out_specs = P("seq", "db")
    return jax.shard_map(
        on_device, mesh=mesh, in_specs=in_specs, out_specs=out_specs, check_vma=False
    )
```

```python
import functools
import math

import jax
import jax.numpy as jnp
from jax import lax
from jax.experimental import pallas as pl
from jax.experimental.pallas import tpu as pltpu
from jax.sharding import PartitionSpec as P

HD = 128
SPAN = 64
K = 2
CAP = 3
LANES = 128
MESH = pl.DeviceIdType.MESH


def slot_places(neighbour_shard, neighbour_count):
    own_shard = neighbour_shard.reshape(-1)
    slots = own_shard.shape[0]
    own_live = (
        jnp.arange(K, dtype=jnp.int32)[None, :] < neighbour_count[:, None]
    ).reshape(-1)
    same = (own_shard[None, :] == own_shard[:, None]) & own_live[None, :]
    earlier = jnp.arange(slots)[None, :] < jnp.arange(slots)[:, None]
    own_rank = jnp.minimum(jnp.sum((same & earlier).astype(jnp.int32), axis=1), CAP - 1)
    return own_live, own_shard * CAP + own_rank


def peer_copy(src, dst, send_sem, recv_sem, device):
    return pltpu.make_async_remote_copy(
        src_ref=src, dst_ref=dst, send_sem=send_sem, recv_sem=recv_sem,
        device_id=device, device_id_type=MESH,
    )


def out_kernel(n_seq, send_q, send_e, recv_q, recv_e, qs, qr, es, er, ls):
    me_s = lax.axis_index("seq")
    me_d = lax.axis_index("db")

    barrier = pltpu.get_barrier_semaphore()

    @pl.loop(1, n_seq)
    def _(o):
        pl.semaphore_signal(barrier, inc=1, device_id=(lax.rem(me_s + o, n_seq), me_d),
                            device_id_type=MESH)

    pl.semaphore_wait(barrier, n_seq - 1)

    own = [
        pltpu.make_async_copy(send_q.at[me_s], recv_q.at[me_s], ls.at[0]),
        pltpu.make_async_copy(send_e.at[me_s], recv_e.at[me_s], ls.at[1]),
    ]
    for c in own:
        c.start()

    @pl.loop(1, n_seq)
    def _(o):
        d = lax.rem(me_s + o, n_seq)
        peer_copy(send_e.at[d], recv_e.at[me_s], es.at[d], er.at[me_s], (d, me_d)).start()
        peer_copy(send_q.at[d], recv_q.at[me_s], qs.at[d], qr.at[me_s], (d, me_d)).start()

    for c in own:
        c.wait()

    @pl.loop(1, n_seq)
    def _(o):
        d = lax.rem(me_s + o, n_seq)
        s = lax.rem(me_s + n_seq - o, n_seq)
        peer_copy(send_e.at[d], recv_e.at[me_s], es.at[d], er.at[me_s], (d, me_d)).wait_send()
        peer_copy(send_q.at[d], recv_q.at[me_s], qs.at[d], qr.at[me_s], (d, me_d)).wait_send()
        peer_copy(send_e.at[me_s], recv_e.at[s], es.at[s], er.at[s], (s, me_d)).wait_recv()
        peer_copy(send_q.at[me_s], recv_q.at[s], qs.at[s], qr.at[s], (s, me_d)).wait_recv()


def back_kernel(n_seq, ctx, stats, back_ctx, back_stats, cs, cr, ss, sr, ls):
    me_s = lax.axis_index("seq")
    me_d = lax.axis_index("db")
    barrier = pltpu.get_barrier_semaphore()

    @pl.loop(1, n_seq)
    def _(o):
        pl.semaphore_signal(barrier, inc=1, device_id=(lax.rem(me_s + o, n_seq), me_d),
                            device_id_type=MESH)

    pl.semaphore_wait(barrier, n_seq - 1)

    own = [
        pltpu.make_async_copy(ctx.at[me_s], back_ctx.at[me_s], ls.at[0]),
        pltpu.make_async_copy(stats.at[me_s], back_stats.at[me_s], ls.at[1]),
    ]
    for c in own:
        c.start()

    @pl.loop(1, n_seq)
    def _(o):
        d = lax.rem(me_s + o, n_seq)
        peer_copy(stats.at[d], back_stats.at[me_s], ss.at[d], sr.at[me_s], (d, me_d)).start()
        peer_copy(ctx.at[d], back_ctx.at[me_s], cs.at[d], cr.at[me_s], (d, me_d)).start()

    for c in own:
        c.wait()

    @pl.loop(1, n_seq)
    def _(o):
        d = lax.rem(me_s + o, n_seq)
        s = lax.rem(me_s + n_seq - o, n_seq)
        peer_copy(stats.at[d], back_stats.at[me_s], ss.at[d], sr.at[me_s], (d, me_d)).wait_send()
        peer_copy(ctx.at[d], back_ctx.at[me_s], cs.at[d], cr.at[me_s], (d, me_d)).wait_send()
        peer_copy(stats.at[me_s], back_stats.at[s], ss.at[s], sr.at[s], (s, me_d)).wait_recv()
        peer_copy(ctx.at[me_s], back_ctx.at[s], cs.at[s], cr.at[s], (s, me_d)).wait_recv()


def attend_kernel(scale, heads, rows, e_ref, q_ref, kv_ref, ctx_ref, stats_ref):
    key_len = SPAN * 2
    keys_total, width = kv_ref.shape[0], heads * HD
    per_tile = rows // SPAN
    col_block = lax.broadcasted_iota(jnp.int32, (1, keys_total), 1) // key_len
    row_block = lax.broadcasted_iota(jnp.int32, (rows, 1), 0) // SPAN

    def one_tile(t, carry):
        start = pl.multiple_of(t * rows, rows)
        row_entry = jnp.zeros((rows, 1), jnp.int32)
        for j in range(per_tile):
            row_entry = jnp.where(row_block == j, e_ref[t * per_tile + j], row_entry)
        named = col_block == row_entry
        for h in range(heads):
            q = q_ref[pl.ds(start, rows), h * HD:(h + 1) * HD]
            k = kv_ref[:, h * HD:(h + 1) * HD]
            v = kv_ref[:, width + h * HD:width + (h + 1) * HD]
            s = lax.dot_general(
                q, k, (((1,), (1,)), ((), ())), preferred_element_type=jnp.float32
            ) * scale
            s = jnp.where(named, s, -jnp.inf)
            top = jnp.max(s, axis=1, keepdims=True)
            w = jnp.exp(s - top)
            total = jnp.sum(w, axis=1, keepdims=True)
            ctx = jnp.dot(w.astype(jnp.bfloat16), v, preferred_element_type=jnp.float32)
            ctx_ref[pl.ds(start, rows), h * HD:(h + 1) * HD] = (ctx / total).astype(ctx_ref.dtype)
            stats_ref[pl.ds(start, rows), 2 * h:2 * h + 1] = top
            stats_ref[pl.ds(start, rows), 2 * h + 1:2 * h + 2] = total
        return carry

    lax.fori_loop(0, q_ref.shape[0] // rows, one_tile, 0)


def vmem_whole(shape):
    return pl.BlockSpec(shape, lambda *_: (0,) * len(shape))


def attend(recv_q, recv_e, kv_flat, heads):
    n_src, cap, span, width = recv_q.shape
    q_rows = recv_q.reshape(n_src * cap * span, width)
    kv_rows = kv_flat.reshape(-1, kv_flat.shape[2])
    stats_shape = (q_rows.shape[0], 2 * heads)
    grid_spec = pltpu.PrefetchScalarGridSpec(
        num_scalar_prefetch=1,
        grid=(1,),
        in_specs=[vmem_whole(q_rows.shape), vmem_whole(kv_rows.shape)],
        out_specs=[vmem_whole(q_rows.shape), vmem_whole(stats_shape)],
    )
    ctx, stats = pl.pallas_call(
        functools.partial(attend_kernel, 1.0 / math.sqrt(HD), heads, 4 * span),
        grid_spec=grid_spec,
        out_shape=(
            jax.ShapeDtypeStruct(q_rows.shape, jnp.bfloat16),
            jax.ShapeDtypeStruct(stats_shape, jnp.float32),
        ),
    )(recv_e, q_rows, kv_rows)
    return ctx.reshape(recv_q.shape), stats.reshape(n_src, cap, span, 2 * heads)


def attend_back_kernel(n_seq, n_db, heads, scale, send_e, send_q, kv_ref, w_loc, back_ctx,
                       back_stats, stage_ctx, stage_stats, w_cols, ctx_v, stats_v, recv_q,
                       recv_e, cs, cr, ss, sr, ws, wr, ls, stg, qs, qr, es, er):
    me_s = lax.axis_index("seq")
    me_d = lax.axis_index("db")
    rows = stage_ctx.shape[1]
    keys_total = kv_ref.shape[0]
    width = heads * HD
    cap = rows // SPAN
    key_block = lax.broadcasted_iota(jnp.int32, (keys_total, 1), 0) // (2 * SPAN)
    lane_place = lax.broadcasted_iota(jnp.int32, (1, rows), 1) // SPAN

    barrier = pltpu.get_barrier_semaphore()

    @pl.loop(1, n_seq)
    def _(o):
        pl.semaphore_signal(barrier, inc=1, device_id=(lax.rem(me_s + o, n_seq), me_d),
                            device_id_type=MESH)

    @pl.loop(1, n_db)
    def _(o):
        pl.semaphore_signal(barrier, inc=1, device_id=(me_s, lax.rem(me_d + o, n_db)),
                            device_id_type=MESH)

    pl.semaphore_wait(barrier, (n_seq - 1) + (n_db - 1))

    features = w_cols.shape[2]

    def w_src(d):
        return w_loc.at[:, pl.ds(pl.multiple_of(d * features, features), features)]

    own_w = pltpu.make_async_copy(w_src(me_d), w_cols.at[me_d], ls.at[4])
    own_w.start()

    own_in = [
        pltpu.make_async_copy(send_q.at[me_s], recv_q.at[me_s], ls.at[0]),
        pltpu.make_async_copy(send_e.at[me_s], recv_e.at[me_s], ls.at[1]),
    ]
    for c in own_in:
        c.start()

    def q_in(d, s):
        return peer_copy(send_q.at[d], recv_q.at[s], qs.at[d], qr.at[s], (d, me_d))

    def e_in(d, s):
        return peer_copy(send_e.at[d], recv_e.at[s], es.at[d], er.at[s], (d, me_d))

    @pl.loop(1, n_seq)
    def _(o):
        d = lax.rem(me_s + o, n_seq)
        e_in(d, me_s).start()
        q_in(d, me_s).start()

    @pl.loop(1, n_db)
    def _(o):
        d = lax.rem(me_d + o, n_db)
        peer_copy(w_src(d), w_cols.at[me_d], ws.at[d], wr.at[me_d], (me_s, d)).start()

    def compute(d, slot):
        entry = recv_e[pl.ds(d, 1), 0:rows]
        named = key_block == entry
        stats_v[slot] = jnp.zeros(stats_v.shape[1:], stats_v.dtype)
        for h in range(heads):
            q = recv_q[d, :, h * HD:(h + 1) * HD]
            k = kv_ref[:, h * HD:(h + 1) * HD]
            v = kv_ref[:, width + h * HD:width + (h + 1) * HD]
            st = lax.dot_general(
                k, q, (((1,), (1,)), ((), ())), preferred_element_type=jnp.float32
            ) * scale
            st = jnp.where(named, st, -jnp.inf)
            top = jnp.max(st, axis=0, keepdims=True)
            w = jnp.exp(st - top)
            total = jnp.sum(w, axis=0, keepdims=True)
            u = lax.dot_general(
                w.astype(jnp.bfloat16), v, (((0,), (0,)), ((), ())),
                preferred_element_type=jnp.float32,
            )
            ctx_v[slot, :, h * HD:(h + 1) * HD] = u.astype(ctx_v.dtype)
            stats_v[slot, 2 * h:2 * h + 1, 0:rows] = top
            stats_v[slot, 2 * h + 1:2 * h + 2, 0:rows] = total

    def staged(d, slot):
        return [
            pltpu.make_async_copy(ctx_v.at[slot], stage_ctx.at[d], stg.at[0, slot]),
            pltpu.make_async_copy(stats_v.at[slot], stage_stats.at[d], stg.at[1, slot]),
        ]

    def send(d):
        peer_copy(stage_stats.at[d], back_stats.at[me_s], ss.at[d], sr.at[me_s], (d, me_d)).start()
        peer_copy(stage_ctx.at[d], back_ctx.at[me_s], cs.at[d], cr.at[me_s], (d, me_d)).start()

    for c in own_in:
        c.wait()
    compute(me_s, 0)
    for c in staged(me_s, 0):
        c.start()
    for c in staged(me_s, 0):
        c.wait()
    own = [
        pltpu.make_async_copy(stage_ctx.at[me_s], back_ctx.at[me_s], ls.at[2]),
        pltpu.make_async_copy(stage_stats.at[me_s], back_stats.at[me_s], ls.at[3]),
    ]
    for c in own:
        c.start()

    @pl.loop(1, n_seq)
    def _(o):
        d = lax.rem(me_s + o, n_seq)
        slot = lax.rem(o, 2)
        e_in(me_s, d).wait_recv()
        q_in(me_s, d).wait_recv()
        compute(d, slot)
        for c in staged(d, slot):
            c.start()

        @pl.when(o > 1)
        def _():
            prev = lax.rem(me_s + o - 1, n_seq)
            for c in staged(prev, 1 - slot):
                c.wait()
            send(prev)

    last = lax.rem(me_s + n_seq - 1, n_seq)
    for c in staged(last, (n_seq - 1) % 2):
        c.wait()
    send(last)

    for c in own:
        c.wait()

    @pl.loop(1, n_seq)
    def _(o):
        d = lax.rem(me_s + o, n_seq)
        e_in(d, me_s).wait_send()
        q_in(d, me_s).wait_send()

    @pl.loop(1, n_seq)
    def _(o):
        d = lax.rem(me_s + o, n_seq)
        s = lax.rem(me_s + n_seq - o, n_seq)
        peer_copy(stage_stats.at[d], back_stats.at[me_s], ss.at[d], sr.at[me_s], (d, me_d)).wait_send()
        peer_copy(stage_ctx.at[d], back_ctx.at[me_s], cs.at[d], cr.at[me_s], (d, me_d)).wait_send()
        peer_copy(stage_stats.at[me_s], back_stats.at[s], ss.at[s], sr.at[s], (s, me_d)).wait_recv()
        peer_copy(stage_ctx.at[me_s], back_ctx.at[s], cs.at[s], cr.at[s], (s, me_d)).wait_recv()

    own_w.wait()

    @pl.loop(1, n_db)
    def _(o):
        d = lax.rem(me_d + o, n_db)
        s = lax.rem(me_d + n_db - o, n_db)
        peer_copy(w_src(d), w_cols.at[me_d], ws.at[d], wr.at[me_d], (me_s, d)).wait_send()
        peer_copy(w_src(me_d), w_cols.at[s], ws.at[s], wr.at[s], (me_s, s)).wait_recv()


def attend_back(send_q, send_e, kv_flat, w_loc, heads, n_seq, n_db):
    n_src, rows, width = send_q.shape
    kv_rows = kv_flat.reshape(-1, kv_flat.shape[2])
    stats_shape = (n_src, 8, 2 * LANES)
    ctx_shape = (n_src, rows, width)
    dma = pltpu.SemaphoreType.DMA
    outs = pl.pallas_call(
        functools.partial(attend_back_kernel, n_seq, n_db, heads, 1.0 / math.sqrt(HD)),
        out_shape=(
            jax.ShapeDtypeStruct(ctx_shape, jnp.bfloat16),
            jax.ShapeDtypeStruct(stats_shape, jnp.float32),
            jax.ShapeDtypeStruct(ctx_shape, jnp.bfloat16),
            jax.ShapeDtypeStruct(stats_shape, jnp.float32),
            jax.ShapeDtypeStruct((n_db, w_loc.shape[0], w_loc.shape[1] // n_db), w_loc.dtype),
        ),
        in_specs=[
            any_spec(),
            any_spec(),
            pl.BlockSpec(memory_space=pltpu.VMEM),
            any_spec(),
        ],
        out_specs=(any_spec(), any_spec(), any_spec(), any_spec(), any_spec()),
        scratch_shapes=[
            pltpu.VMEM((2, rows, width), jnp.bfloat16),
            pltpu.VMEM((2,) + stats_shape[1:], jnp.float32),
            pltpu.VMEM(send_q.shape, send_q.dtype),
            pltpu.VMEM(send_e.shape, send_e.dtype),
            dma((n_seq,)), dma((n_seq,)), dma((n_seq,)), dma((n_seq,)),
            dma((n_db,)), dma((n_db,)), dma((5,)), dma((2, 2)),
            dma((n_seq,)), dma((n_seq,)), dma((n_seq,)), dma((n_seq,)),
        ],
        compiler_params=pltpu.CompilerParams(collective_id=1, has_side_effects=True),
    )(send_e, send_q, kv_rows, w_loc)
    return outs[0], outs[1], outs[4]


def combine_kernel(heads, place_ref, count_ref, ctx_ref, stats_ref, out_ref, stats_t):
    for s in range(stats_ref.shape[0]):
        stats_t[s] = jnp.transpose(stats_ref[s])

    def one_span(c, carry):
        p0 = place_ref[c * K]
        p1 = place_ref[c * K + 1]
        r0 = pl.multiple_of(lax.rem(p0, CAP) * SPAN, SPAN)
        r1 = pl.multiple_of(lax.rem(p1, CAP) * SPAN, SPAN)
        st0 = stats_t[p0 // CAP, pl.ds(r0, SPAN), :]
        st1 = stats_t[p1 // CAP, pl.ds(r1, SPAN), :]
        live1 = count_ref[c] > 1
        for h in range(heads):
            cols = slice(h * HD, (h + 1) * HD)
            m0, l0 = st0[:, 2 * h:2 * h + 1], st0[:, 2 * h + 1:2 * h + 2]
            m1, l1 = st1[:, 2 * h:2 * h + 1], st1[:, 2 * h + 1:2 * h + 2]
            best = jnp.where(live1, jnp.maximum(m0, m1), m0)
            a0 = jnp.exp(m0 - best)
            a1 = jnp.where(live1, jnp.exp(m1 - best), 0.0)
            u0 = ctx_ref[p0, :, cols].astype(jnp.float32)
            u1 = jnp.where(live1, ctx_ref[p1, :, cols].astype(jnp.float32), 0.0)
            out_ref[c, :, cols] = (
                (a0 * u0 + a1 * u1) / (a0 * l0 + a1 * l1)
            ).astype(out_ref.dtype)
        return carry

    lax.fori_loop(0, out_ref.shape[0], one_span, 0)


def combine(back_ctx, back_stats, place, neighbour_count, heads):
    places, span, width = back_ctx.shape
    spans = neighbour_count.shape[0]
    n_src, st_rows, st_cols = back_stats.shape
    grid_spec = pltpu.PrefetchScalarGridSpec(
        num_scalar_prefetch=2,
        grid=(1,),
        in_specs=[vmem_whole(back_ctx.shape), vmem_whole(back_stats.shape)],
        out_specs=vmem_whole((spans, span, width)),
        scratch_shapes=[pltpu.VMEM((n_src, st_cols, st_rows), jnp.float32)],
    )
    return pl.pallas_call(
        functools.partial(combine_kernel, heads),
        grid_spec=grid_spec,
        out_shape=jax.ShapeDtypeStruct((spans, span, width), jnp.bfloat16),
    )(place, neighbour_count, back_ctx, back_stats)


def pack_kernel(src_ref, q_ref, out_ref):
    def one_place(p, carry):
        span = src_ref[p]
        rows = q_ref[jnp.maximum(span, 0)]
        out_ref[p] = jnp.where(span >= 0, rows, jnp.zeros_like(rows))
        return carry

    lax.fori_loop(0, out_ref.shape[0], one_place, 0)


def pack(queries, src_span, places):
    grid_spec = pltpu.PrefetchScalarGridSpec(
        num_scalar_prefetch=1,
        grid=(1,),
        in_specs=[vmem_whole(queries.shape)],
        out_specs=vmem_whole((places,) + queries.shape[1:]),
    )
    return pl.pallas_call(
        pack_kernel,
        grid_spec=grid_spec,
        out_shape=jax.ShapeDtypeStruct((places,) + queries.shape[1:], queries.dtype),
    )(src_span, queries)


def any_spec():
    return pl.BlockSpec(memory_space=pl.ANY)


def exchange_out(send_q, send_e, n_seq):
    dma = pltpu.SemaphoreType.DMA
    return pl.pallas_call(
        functools.partial(out_kernel, n_seq),
        out_shape=(
            jax.ShapeDtypeStruct(send_q.shape, send_q.dtype),
            jax.ShapeDtypeStruct(send_e.shape, send_e.dtype),
        ),
        in_specs=[any_spec()] * 2,
        out_specs=(any_spec(), any_spec()),
        scratch_shapes=[dma((n_seq,)), dma((n_seq,)), dma((n_seq,)), dma((n_seq,)), dma((2,))],
        compiler_params=pltpu.CompilerParams(collective_id=0, has_side_effects=True),
    )(send_q, send_e)


def exchange_back(ctx, stats, n_seq):
    dma = pltpu.SemaphoreType.DMA
    return pl.pallas_call(
        functools.partial(back_kernel, n_seq),
        out_shape=(
            jax.ShapeDtypeStruct(ctx.shape, ctx.dtype),
            jax.ShapeDtypeStruct(stats.shape, stats.dtype),
        ),
        in_specs=[any_spec()] * 2,
        out_specs=(any_spec(), any_spec()),
        scratch_shapes=[dma((n_seq,)), dma((n_seq,)), dma((n_seq,)), dma((n_seq,)), dma((2,))],
        compiler_params=pltpu.CompilerParams(collective_id=1, has_side_effects=True),
    )(ctx, stats)


def on_device(
    decoder_states,
    query_weight,
    output_weight,
    neighbour_kv,
    neighbour_shard,
    neighbour_entry,
    neighbour_count,
):
    tok_rows = decoder_states.shape[0]
    span_total = tok_rows // SPAN
    row_width = query_weight.shape[1]
    heads_here = row_width // HD
    key_len = neighbour_kv.shape[1]
    n_seq = lax.psum(1, "seq")
    n_db = lax.psum(1, "db")
    places_total = n_seq * CAP
    queries = jnp.dot(decoder_states, query_weight, preferred_element_type=jnp.float32).astype(
        jnp.bfloat16
    )
    queries = queries.reshape(span_total, SPAN, row_width)

    live, place = slot_places(neighbour_shard, neighbour_count)
    target = jnp.where(live, place, places_total)
    span_of_slot = jnp.arange(span_total * K, dtype=jnp.int32) // K
    src_span = jnp.full((places_total,), -1, jnp.int32)
    src_span = src_span.at[target].set(span_of_slot, mode="drop")
    send_q = pack(queries, src_span, places_total)
    send_e = jnp.zeros((places_total,), jnp.int32)
    send_e = send_e.at[target].set(neighbour_entry.reshape(-1), mode="drop")
    send_e = jnp.repeat(send_e.reshape(n_seq, CAP), SPAN, axis=1)
    send_e = jnp.pad(send_e, ((0, 0), (0, 2 * LANES - CAP * SPAN)))
    kv_flat = neighbour_kv.reshape(neighbour_kv.shape[0], key_len, 2 * row_width)
    back_ctx, back_stats, weight_cols = attend_back(
        send_q.reshape(n_seq, CAP * SPAN, row_width), send_e, kv_flat, output_weight,
        heads_here, n_seq, n_db
    )
    back_ctx = back_ctx.reshape(places_total, SPAN, row_width)
    context = combine(back_ctx, back_stats, place, neighbour_count, heads_here)
    context = context.reshape(tok_rows, row_width)

    contexts = lax.all_gather(context, "db", axis=0, tiled=False)
    out = jnp.einsum(
        "str,srf->tf", contexts, weight_cols, preferred_element_type=jnp.float32
    )
    return out.astype(jnp.bfloat16)


def solution(mesh):
    in_specs = (
        P("seq", None),
        P(None, "db"),
        P("db", None),
        P("seq", None, None, "db"),
        P("seq", None),
        P("seq", None),
        P("seq"),
    )
    out_specs = P("seq", "db")
    return jax.shard_map(
        on_device, mesh=mesh, in_specs=in_specs, out_specs=out_specs, check_vma=False
    )
```

```python
import functools
import math

import jax
import jax.numpy as jnp
from jax import lax
from jax.experimental import pallas as pl
from jax.experimental.pallas import tpu as pltpu
from jax.sharding import PartitionSpec as P

HD = 128
SPAN = 64
K = 2
CAP = 3
LANES = 128
MESH = pl.DeviceIdType.MESH


def slot_places(neighbour_shard, neighbour_count):
    own_shard = neighbour_shard.reshape(-1)
    slots = own_shard.shape[0]
    own_live = (
        jnp.arange(K, dtype=jnp.int32)[None, :] < neighbour_count[:, None]
    ).reshape(-1)
    same = (own_shard[None, :] == own_shard[:, None]) & own_live[None, :]
    earlier = jnp.arange(slots)[None, :] < jnp.arange(slots)[:, None]
    own_rank = jnp.minimum(jnp.sum((same & earlier).astype(jnp.int32), axis=1), CAP - 1)
    return own_live, own_shard * CAP + own_rank


def peer_copy(src, dst, send_sem, recv_sem, device):
    return pltpu.make_async_remote_copy(
        src_ref=src, dst_ref=dst, send_sem=send_sem, recv_sem=recv_sem,
        device_id=device, device_id_type=MESH,
    )


def out_kernel(n_seq, send_q, send_e, recv_q, recv_e, qs, qr, es, er, ls):
    me_s = lax.axis_index("seq")
    me_d = lax.axis_index("db")

    barrier = pltpu.get_barrier_semaphore()

    @pl.loop(1, n_seq)
    def _(o):
        pl.semaphore_signal(barrier, inc=1, device_id=(lax.rem(me_s + o, n_seq), me_d),
                            device_id_type=MESH)

    pl.semaphore_wait(barrier, n_seq - 1)

    own = [
        pltpu.make_async_copy(send_q.at[me_s], recv_q.at[me_s], ls.at[0]),
        pltpu.make_async_copy(send_e.at[me_s], recv_e.at[me_s], ls.at[1]),
    ]
    for c in own:
        c.start()

    @pl.loop(1, n_seq)
    def _(o):
        d = lax.rem(me_s + o, n_seq)
        peer_copy(send_e.at[d], recv_e.at[me_s], es.at[d], er.at[me_s], (d, me_d)).start()
        peer_copy(send_q.at[d], recv_q.at[me_s], qs.at[d], qr.at[me_s], (d, me_d)).start()

    for c in own:
        c.wait()

    @pl.loop(1, n_seq)
    def _(o):
        d = lax.rem(me_s + o, n_seq)
        s = lax.rem(me_s + n_seq - o, n_seq)
        peer_copy(send_e.at[d], recv_e.at[me_s], es.at[d], er.at[me_s], (d, me_d)).wait_send()
        peer_copy(send_q.at[d], recv_q.at[me_s], qs.at[d], qr.at[me_s], (d, me_d)).wait_send()
        peer_copy(send_e.at[me_s], recv_e.at[s], es.at[s], er.at[s], (s, me_d)).wait_recv()
        peer_copy(send_q.at[me_s], recv_q.at[s], qs.at[s], qr.at[s], (s, me_d)).wait_recv()


def back_kernel(n_seq, ctx, stats, back_ctx, back_stats, cs, cr, ss, sr, ls):
    me_s = lax.axis_index("seq")
    me_d = lax.axis_index("db")
    barrier = pltpu.get_barrier_semaphore()

    @pl.loop(1, n_seq)
    def _(o):
        pl.semaphore_signal(barrier, inc=1, device_id=(lax.rem(me_s + o, n_seq), me_d),
                            device_id_type=MESH)

    pl.semaphore_wait(barrier, n_seq - 1)

    own = [
        pltpu.make_async_copy(ctx.at[me_s], back_ctx.at[me_s], ls.at[0]),
        pltpu.make_async_copy(stats.at[me_s], back_stats.at[me_s], ls.at[1]),
    ]
    for c in own:
        c.start()

    @pl.loop(1, n_seq)
    def _(o):
        d = lax.rem(me_s + o, n_seq)
        peer_copy(stats.at[d], back_stats.at[me_s], ss.at[d], sr.at[me_s], (d, me_d)).start()
        peer_copy(ctx.at[d], back_ctx.at[me_s], cs.at[d], cr.at[me_s], (d, me_d)).start()

    for c in own:
        c.wait()

    @pl.loop(1, n_seq)
    def _(o):
        d = lax.rem(me_s + o, n_seq)
        s = lax.rem(me_s + n_seq - o, n_seq)
        peer_copy(stats.at[d], back_stats.at[me_s], ss.at[d], sr.at[me_s], (d, me_d)).wait_send()
        peer_copy(ctx.at[d], back_ctx.at[me_s], cs.at[d], cr.at[me_s], (d, me_d)).wait_send()
        peer_copy(stats.at[me_s], back_stats.at[s], ss.at[s], sr.at[s], (s, me_d)).wait_recv()
        peer_copy(ctx.at[me_s], back_ctx.at[s], cs.at[s], cr.at[s], (s, me_d)).wait_recv()


def attend_kernel(scale, heads, rows, e_ref, q_ref, kv_ref, ctx_ref, stats_ref):
    key_len = SPAN * 2
    keys_total, width = kv_ref.shape[0], heads * HD
    per_tile = rows // SPAN
    col_block = lax.broadcasted_iota(jnp.int32, (1, keys_total), 1) // key_len
    row_block = lax.broadcasted_iota(jnp.int32, (rows, 1), 0) // SPAN

    def one_tile(t, carry):
        start = pl.multiple_of(t * rows, rows)
        row_entry = jnp.zeros((rows, 1), jnp.int32)
        for j in range(per_tile):
            row_entry = jnp.where(row_block == j, e_ref[t * per_tile + j], row_entry)
        named = col_block == row_entry
        for h in range(heads):
            q = q_ref[pl.ds(start, rows), h * HD:(h + 1) * HD]
            k = kv_ref[:, h * HD:(h + 1) * HD]
            v = kv_ref[:, width + h * HD:width + (h + 1) * HD]
            s = lax.dot_general(
                q, k, (((1,), (1,)), ((), ())), preferred_element_type=jnp.float32
            ) * scale
            s = jnp.where(named, s, -jnp.inf)
            top = jnp.max(s, axis=1, keepdims=True)
            w = jnp.exp(s - top)
            total = jnp.sum(w, axis=1, keepdims=True)
            ctx = jnp.dot(w.astype(jnp.bfloat16), v, preferred_element_type=jnp.float32)
            ctx_ref[pl.ds(start, rows), h * HD:(h + 1) * HD] = (ctx / total).astype(ctx_ref.dtype)
            stats_ref[pl.ds(start, rows), 2 * h:2 * h + 1] = top
            stats_ref[pl.ds(start, rows), 2 * h + 1:2 * h + 2] = total
        return carry

    lax.fori_loop(0, q_ref.shape[0] // rows, one_tile, 0)


def vmem_whole(shape):
    return pl.BlockSpec(shape, lambda *_: (0,) * len(shape))


def attend(recv_q, recv_e, kv_flat, heads):
    n_src, cap, span, width = recv_q.shape
    q_rows = recv_q.reshape(n_src * cap * span, width)
    kv_rows = kv_flat.reshape(-1, kv_flat.shape[2])
    stats_shape = (q_rows.shape[0], 2 * heads)
    grid_spec = pltpu.PrefetchScalarGridSpec(
        num_scalar_prefetch=1,
        grid=(1,),
        in_specs=[vmem_whole(q_rows.shape), vmem_whole(kv_rows.shape)],
        out_specs=[vmem_whole(q_rows.shape), vmem_whole(stats_shape)],
    )
    ctx, stats = pl.pallas_call(
        functools.partial(attend_kernel, 1.0 / math.sqrt(HD), heads, 4 * span),
        grid_spec=grid_spec,
        out_shape=(
            jax.ShapeDtypeStruct(q_rows.shape, jnp.bfloat16),
            jax.ShapeDtypeStruct(stats_shape, jnp.float32),
        ),
    )(recv_e, q_rows, kv_rows)
    return ctx.reshape(recv_q.shape), stats.reshape(n_src, cap, span, 2 * heads)


def attend_back_kernel(n_seq, n_db, heads, scale, send_e, send_q, kv_ref, w_loc, back_ctx,
                       back_stats, stage_ctx, stage_stats, w_cols, ctx_v, stats_v, recv_q,
                       recv_e, cs, cr, ss, sr, ws, wr, ls, stg, qs, qr, es, er):
    me_s = lax.axis_index("seq")
    me_d = lax.axis_index("db")
    rows = stage_ctx.shape[1]
    keys_total = kv_ref.shape[0]
    width = heads * HD
    cap = rows // SPAN
    key_block = lax.broadcasted_iota(jnp.int32, (keys_total, 1), 0) // (2 * SPAN)
    lane_place = lax.broadcasted_iota(jnp.int32, (1, rows), 1) // SPAN

    barrier = pltpu.get_barrier_semaphore()

    @pl.loop(1, n_seq)
    def _(o):
        pl.semaphore_signal(barrier, inc=1, device_id=(lax.rem(me_s + o, n_seq), me_d),
                            device_id_type=MESH)

    @pl.loop(1, n_db)
    def _(o):
        pl.semaphore_signal(barrier, inc=1, device_id=(me_s, lax.rem(me_d + o, n_db)),
                            device_id_type=MESH)

    pl.semaphore_wait(barrier, (n_seq - 1) + (n_db - 1))

    features = w_cols.shape[2]

    def w_src(d):
        return w_loc.at[:, pl.ds(pl.multiple_of(d * features, features), features)]

    own_in = [
        pltpu.make_async_copy(send_q.at[me_s], recv_q.at[me_s], ls.at[0]),
        pltpu.make_async_copy(send_e.at[me_s], recv_e.at[me_s], ls.at[1]),
    ]
    for c in own_in:
        c.start()

    def q_in(d, s):
        return peer_copy(send_q.at[d], recv_q.at[s], qs.at[d], qr.at[s], (d, me_d))

    def e_in(d, s):
        return peer_copy(send_e.at[d], recv_e.at[s], es.at[d], er.at[s], (d, me_d))

    @pl.loop(1, n_seq)
    def _(o):
        d = lax.rem(me_s + o, n_seq)
        e_in(d, me_s).start()
        q_in(d, me_s).start()

    own_w = pltpu.make_async_copy(w_src(me_d), w_cols.at[me_d], ls.at[4])
    own_w.start()

    @pl.loop(1, n_db)
    def _(o):
        d = lax.rem(me_d + o, n_db)
        peer_copy(w_src(d), w_cols.at[me_d], ws.at[d], wr.at[me_d], (me_s, d)).start()

    def compute(d, slot):
        entry = recv_e[pl.ds(d, 1), 0:rows]
        named = key_block == entry
        stats_v[slot] = jnp.zeros(stats_v.shape[1:], stats_v.dtype)
        for h in range(heads):
            q = recv_q[d, :, h * HD:(h + 1) * HD]
            k = kv_ref[:, h * HD:(h + 1) * HD]
            v = kv_ref[:, width + h * HD:width + (h + 1) * HD]
            st = lax.dot_general(
                k, q, (((1,), (1,)), ((), ())), preferred_element_type=jnp.float32
            ) * scale
            st = jnp.where(named, st, -jnp.inf)
            top = jnp.max(st, axis=0, keepdims=True)
            w = jnp.exp(st - top)
            total = jnp.sum(w, axis=0, keepdims=True)
            u = lax.dot_general(
                w.astype(jnp.bfloat16), v, (((0,), (0,)), ((), ())),
                preferred_element_type=jnp.float32,
            )
            ctx_v[slot, :, h * HD:(h + 1) * HD] = u.astype(ctx_v.dtype)
            stats_v[slot, 2 * h:2 * h + 1, 0:rows] = top
            stats_v[slot, 2 * h + 1:2 * h + 2, 0:rows] = total

    def staged(d, slot):
        return [
            pltpu.make_async_copy(ctx_v.at[slot], stage_ctx.at[d], stg.at[0, slot]),
            pltpu.make_async_copy(stats_v.at[slot], stage_stats.at[d], stg.at[1, slot]),
        ]

    def send(d):
        peer_copy(stage_stats.at[d], back_stats.at[me_s], ss.at[d], sr.at[me_s], (d, me_d)).start()
        peer_copy(stage_ctx.at[d], back_ctx.at[me_s], cs.at[d], cr.at[me_s], (d, me_d)).start()

    for c in own_in:
        c.wait()
    compute(me_s, 0)
    for c in staged(me_s, 0):
        c.start()
    for c in staged(me_s, 0):
        c.wait()
    own = [
        pltpu.make_async_copy(stage_ctx.at[me_s], back_ctx.at[me_s], ls.at[2]),
        pltpu.make_async_copy(stage_stats.at[me_s], back_stats.at[me_s], ls.at[3]),
    ]
    for c in own:
        c.start()

    @pl.loop(1, n_seq)
    def _(o):
        d = lax.rem(me_s + o, n_seq)
        slot = lax.rem(o, 2)
        e_in(me_s, d).wait_recv()
        q_in(me_s, d).wait_recv()
        compute(d, slot)
        for c in staged(d, slot):
            c.start()

        @pl.when(o > 1)
        def _():
            prev = lax.rem(me_s + o - 1, n_seq)
            for c in staged(prev, 1 - slot):
                c.wait()
            send(prev)

    last = lax.rem(me_s + n_seq - 1, n_seq)
    for c in staged(last, (n_seq - 1) % 2):
        c.wait()
    send(last)

    for c in own:
        c.wait()

    @pl.loop(1, n_seq)
    def _(o):
        d = lax.rem(me_s + o, n_seq)
        e_in(d, me_s).wait_send()
        q_in(d, me_s).wait_send()

    @pl.loop(1, n_seq)
    def _(o):
        d = lax.rem(me_s + o, n_seq)
        s = lax.rem(me_s + n_seq - o, n_seq)
        peer_copy(stage_stats.at[d], back_stats.at[me_s], ss.at[d], sr.at[me_s], (d, me_d)).wait_send()
        peer_copy(stage_ctx.at[d], back_ctx.at[me_s], cs.at[d], cr.at[me_s], (d, me_d)).wait_send()
        peer_copy(stage_stats.at[me_s], back_stats.at[s], ss.at[s], sr.at[s], (s, me_d)).wait_recv()
        peer_copy(stage_ctx.at[me_s], back_ctx.at[s], cs.at[s], cr.at[s], (s, me_d)).wait_recv()

    own_w.wait()

    @pl.loop(1, n_db)
    def _(o):
        d = lax.rem(me_d + o, n_db)
        s = lax.rem(me_d + n_db - o, n_db)
        peer_copy(w_src(d), w_cols.at[me_d], ws.at[d], wr.at[me_d], (me_s, d)).wait_send()
        peer_copy(w_src(me_d), w_cols.at[s], ws.at[s], wr.at[s], (me_s, s)).wait_recv()


def attend_back(send_q, send_e, kv_flat, w_loc, heads, n_seq, n_db):
    n_src, rows, width = send_q.shape
    kv_rows = kv_flat.reshape(-1, kv_flat.shape[2])
    stats_shape = (n_src, 8, 2 * LANES)
    ctx_shape = (n_src, rows, width)
    dma = pltpu.SemaphoreType.DMA
    outs = pl.pallas_call(
        functools.partial(attend_back_kernel, n_seq, n_db, heads, 1.0 / math.sqrt(HD)),
        out_shape=(
            jax.ShapeDtypeStruct(ctx_shape, jnp.bfloat16),
            jax.ShapeDtypeStruct(stats_shape, jnp.float32),
            jax.ShapeDtypeStruct(ctx_shape, jnp.bfloat16),
            jax.ShapeDtypeStruct(stats_shape, jnp.float32),
            jax.ShapeDtypeStruct((n_db, w_loc.shape[0], w_loc.shape[1] // n_db), w_loc.dtype),
        ),
        in_specs=[
            any_spec(),
            any_spec(),
            pl.BlockSpec(memory_space=pltpu.VMEM),
            any_spec(),
        ],
        out_specs=(any_spec(), any_spec(), any_spec(), any_spec(), any_spec()),
        scratch_shapes=[
            pltpu.VMEM((2, rows, width), jnp.bfloat16),
            pltpu.VMEM((2,) + stats_shape[1:], jnp.float32),
            pltpu.VMEM(send_q.shape, send_q.dtype),
            pltpu.VMEM(send_e.shape, send_e.dtype),
            dma((n_seq,)), dma((n_seq,)), dma((n_seq,)), dma((n_seq,)),
            dma((n_db,)), dma((n_db,)), dma((5,)), dma((2, 2)),
            dma((n_seq,)), dma((n_seq,)), dma((n_seq,)), dma((n_seq,)),
        ],
        compiler_params=pltpu.CompilerParams(collective_id=1, has_side_effects=True),
    )(send_e, send_q, kv_rows, w_loc)
    return outs[0], outs[1], outs[4]


def combine_kernel(heads, place_ref, count_ref, ctx_ref, stats_ref, out_ref, stats_t):
    for s in range(stats_ref.shape[0]):
        stats_t[s] = jnp.transpose(stats_ref[s])

    def one_span(c, carry):
        p0 = place_ref[c * K]
        p1 = place_ref[c * K + 1]
        r0 = pl.multiple_of(lax.rem(p0, CAP) * SPAN, SPAN)
        r1 = pl.multiple_of(lax.rem(p1, CAP) * SPAN, SPAN)
        st0 = stats_t[p0 // CAP, pl.ds(r0, SPAN), :]
        st1 = stats_t[p1 // CAP, pl.ds(r1, SPAN), :]
        live1 = count_ref[c] > 1
        for h in range(heads):
            cols = slice(h * HD, (h + 1) * HD)
            m0, l0 = st0[:, 2 * h:2 * h + 1], st0[:, 2 * h + 1:2 * h + 2]
            m1, l1 = st1[:, 2 * h:2 * h + 1], st1[:, 2 * h + 1:2 * h + 2]
            best = jnp.where(live1, jnp.maximum(m0, m1), m0)
            a0 = jnp.exp(m0 - best)
            a1 = jnp.where(live1, jnp.exp(m1 - best), 0.0)
            u0 = ctx_ref[p0, :, cols].astype(jnp.float32)
            u1 = jnp.where(live1, ctx_ref[p1, :, cols].astype(jnp.float32), 0.0)
            out_ref[c, :, cols] = (
                (a0 * u0 + a1 * u1) / (a0 * l0 + a1 * l1)
            ).astype(out_ref.dtype)
        return carry

    lax.fori_loop(0, out_ref.shape[0], one_span, 0)


def combine(back_ctx, back_stats, place, neighbour_count, heads):
    places, span, width = back_ctx.shape
    spans = neighbour_count.shape[0]
    n_src, st_rows, st_cols = back_stats.shape
    grid_spec = pltpu.PrefetchScalarGridSpec(
        num_scalar_prefetch=2,
        grid=(1,),
        in_specs=[vmem_whole(back_ctx.shape), vmem_whole(back_stats.shape)],
        out_specs=vmem_whole((spans, span, width)),
        scratch_shapes=[pltpu.VMEM((n_src, st_cols, st_rows), jnp.float32)],
    )
    return pl.pallas_call(
        functools.partial(combine_kernel, heads),
        grid_spec=grid_spec,
        out_shape=jax.ShapeDtypeStruct((spans, span, width), jnp.bfloat16),
    )(place, neighbour_count, back_ctx, back_stats)


def pack_kernel(src_ref, q_ref, out_ref):
    def one_place(p, carry):
        span = src_ref[p]
        rows = q_ref[jnp.maximum(span, 0)]
        out_ref[p] = jnp.where(span >= 0, rows, jnp.zeros_like(rows))
        return carry

    lax.fori_loop(0, out_ref.shape[0], one_place, 0)


def pack(queries, src_span, places):
    grid_spec = pltpu.PrefetchScalarGridSpec(
        num_scalar_prefetch=1,
        grid=(1,),
        in_specs=[vmem_whole(queries.shape)],
        out_specs=vmem_whole((places,) + queries.shape[1:]),
    )
    return pl.pallas_call(
        pack_kernel,
        grid_spec=grid_spec,
        out_shape=jax.ShapeDtypeStruct((places,) + queries.shape[1:], queries.dtype),
    )(src_span, queries)


def any_spec():
    return pl.BlockSpec(memory_space=pl.ANY)


def exchange_out(send_q, send_e, n_seq):
    dma = pltpu.SemaphoreType.DMA
    return pl.pallas_call(
        functools.partial(out_kernel, n_seq),
        out_shape=(
            jax.ShapeDtypeStruct(send_q.shape, send_q.dtype),
            jax.ShapeDtypeStruct(send_e.shape, send_e.dtype),
        ),
        in_specs=[any_spec()] * 2,
        out_specs=(any_spec(), any_spec()),
        scratch_shapes=[dma((n_seq,)), dma((n_seq,)), dma((n_seq,)), dma((n_seq,)), dma((2,))],
        compiler_params=pltpu.CompilerParams(collective_id=0, has_side_effects=True),
    )(send_q, send_e)


def exchange_back(ctx, stats, n_seq):
    dma = pltpu.SemaphoreType.DMA
    return pl.pallas_call(
        functools.partial(back_kernel, n_seq),
        out_shape=(
            jax.ShapeDtypeStruct(ctx.shape, ctx.dtype),
            jax.ShapeDtypeStruct(stats.shape, stats.dtype),
        ),
        in_specs=[any_spec()] * 2,
        out_specs=(any_spec(), any_spec()),
        scratch_shapes=[dma((n_seq,)), dma((n_seq,)), dma((n_seq,)), dma((n_seq,)), dma((2,))],
        compiler_params=pltpu.CompilerParams(collective_id=1, has_side_effects=True),
    )(ctx, stats)


def on_device(
    decoder_states,
    query_weight,
    output_weight,
    neighbour_kv,
    neighbour_shard,
    neighbour_entry,
    neighbour_count,
):
    tok_rows = decoder_states.shape[0]
    span_total = tok_rows // SPAN
    row_width = query_weight.shape[1]
    heads_here = row_width // HD
    key_len = neighbour_kv.shape[1]
    n_seq = lax.psum(1, "seq")
    n_db = lax.psum(1, "db")
    places_total = n_seq * CAP
    queries = jnp.dot(decoder_states, query_weight, preferred_element_type=jnp.float32).astype(
        jnp.bfloat16
    )
    queries = queries.reshape(span_total, SPAN, row_width)

    live, place = slot_places(neighbour_shard, neighbour_count)
    target = jnp.where(live, place, places_total)
    span_of_slot = jnp.arange(span_total * K, dtype=jnp.int32) // K
    src_span = jnp.full((places_total,), -1, jnp.int32)
    src_span = src_span.at[target].set(span_of_slot, mode="drop")
    send_q = pack(queries, src_span, places_total)
    send_e = jnp.zeros((places_total,), jnp.int32)
    send_e = send_e.at[target].set(neighbour_entry.reshape(-1), mode="drop")
    send_e = jnp.repeat(send_e.reshape(n_seq, CAP), SPAN, axis=1)
    send_e = jnp.pad(send_e, ((0, 0), (0, 2 * LANES - CAP * SPAN)))
    kv_flat = neighbour_kv.reshape(neighbour_kv.shape[0], key_len, 2 * row_width)
    back_ctx, back_stats, weight_cols = attend_back(
        send_q.reshape(n_seq, CAP * SPAN, row_width), send_e, kv_flat, output_weight,
        heads_here, n_seq, n_db
    )
    back_ctx = back_ctx.reshape(places_total, SPAN, row_width)
    context = combine(back_ctx, back_stats, place, neighbour_count, heads_here)
    context = context.reshape(tok_rows, row_width)

    contexts = lax.all_gather(context, "db", axis=0, tiled=False)
    out = jnp.einsum(
        "str,srf->tf", contexts, weight_cols, preferred_element_type=jnp.float32
    )
    return out.astype(jnp.bfloat16)


def solution(mesh):
    in_specs = (
        P("seq", None),
        P(None, "db"),
        P("db", None),
        P("seq", None, None, "db"),
        P("seq", None),
        P("seq", None),
        P("seq"),
    )
    out_specs = P("seq", "db")
    return jax.shard_map(
        on_device, mesh=mesh, in_specs=in_specs, out_specs=out_specs, check_vma=False
    )
```

```python
import functools
import math

import jax
import jax.numpy as jnp
from jax import lax
from jax.experimental import pallas as pl
from jax.experimental.pallas import tpu as pltpu
from jax.sharding import PartitionSpec as P

HD = 128
SPAN = 64
K = 2
CAP = 3
LANES = 128
MESH = pl.DeviceIdType.MESH


def slot_places(neighbour_shard, neighbour_count):
    own_shard = neighbour_shard.reshape(-1)
    slots = own_shard.shape[0]
    own_live = (
        jnp.arange(K, dtype=jnp.int32)[None, :] < neighbour_count[:, None]
    ).reshape(-1)
    same = (own_shard[None, :] == own_shard[:, None]) & own_live[None, :]
    earlier = jnp.arange(slots)[None, :] < jnp.arange(slots)[:, None]
    own_rank = jnp.minimum(jnp.sum((same & earlier).astype(jnp.int32), axis=1), CAP - 1)
    return own_live, own_shard * CAP + own_rank


def peer_copy(src, dst, send_sem, recv_sem, device):
    return pltpu.make_async_remote_copy(
        src_ref=src, dst_ref=dst, send_sem=send_sem, recv_sem=recv_sem,
        device_id=device, device_id_type=MESH,
    )


def out_kernel(n_seq, send_q, send_e, recv_q, recv_e, qs, qr, es, er, ls):
    me_s = lax.axis_index("seq")
    me_d = lax.axis_index("db")

    barrier = pltpu.get_barrier_semaphore()

    @pl.loop(1, n_seq)
    def _(o):
        pl.semaphore_signal(barrier, inc=1, device_id=(lax.rem(me_s + o, n_seq), me_d),
                            device_id_type=MESH)

    pl.semaphore_wait(barrier, n_seq - 1)

    own = [
        pltpu.make_async_copy(send_q.at[me_s], recv_q.at[me_s], ls.at[0]),
        pltpu.make_async_copy(send_e.at[me_s], recv_e.at[me_s], ls.at[1]),
    ]
    for c in own:
        c.start()

    @pl.loop(1, n_seq)
    def _(o):
        d = lax.rem(me_s + o, n_seq)
        peer_copy(send_e.at[d], recv_e.at[me_s], es.at[d], er.at[me_s], (d, me_d)).start()
        peer_copy(send_q.at[d], recv_q.at[me_s], qs.at[d], qr.at[me_s], (d, me_d)).start()

    for c in own:
        c.wait()

    @pl.loop(1, n_seq)
    def _(o):
        d = lax.rem(me_s + o, n_seq)
        s = lax.rem(me_s + n_seq - o, n_seq)
        peer_copy(send_e.at[d], recv_e.at[me_s], es.at[d], er.at[me_s], (d, me_d)).wait_send()
        peer_copy(send_q.at[d], recv_q.at[me_s], qs.at[d], qr.at[me_s], (d, me_d)).wait_send()
        peer_copy(send_e.at[me_s], recv_e.at[s], es.at[s], er.at[s], (s, me_d)).wait_recv()
        peer_copy(send_q.at[me_s], recv_q.at[s], qs.at[s], qr.at[s], (s, me_d)).wait_recv()


def back_kernel(n_seq, ctx, stats, back_ctx, back_stats, cs, cr, ss, sr, ls):
    me_s = lax.axis_index("seq")
    me_d = lax.axis_index("db")
    barrier = pltpu.get_barrier_semaphore()

    @pl.loop(1, n_seq)
    def _(o):
        pl.semaphore_signal(barrier, inc=1, device_id=(lax.rem(me_s + o, n_seq), me_d),
                            device_id_type=MESH)

    pl.semaphore_wait(barrier, n_seq - 1)

    own = [
        pltpu.make_async_copy(ctx.at[me_s], back_ctx.at[me_s], ls.at[0]),
        pltpu.make_async_copy(stats.at[me_s], back_stats.at[me_s], ls.at[1]),
    ]
    for c in own:
        c.start()

    @pl.loop(1, n_seq)
    def _(o):
        d = lax.rem(me_s + o, n_seq)
        peer_copy(stats.at[d], back_stats.at[me_s], ss.at[d], sr.at[me_s], (d, me_d)).start()
        peer_copy(ctx.at[d], back_ctx.at[me_s], cs.at[d], cr.at[me_s], (d, me_d)).start()

    for c in own:
        c.wait()

    @pl.loop(1, n_seq)
    def _(o):
        d = lax.rem(me_s + o, n_seq)
        s = lax.rem(me_s + n_seq - o, n_seq)
        peer_copy(stats.at[d], back_stats.at[me_s], ss.at[d], sr.at[me_s], (d, me_d)).wait_send()
        peer_copy(ctx.at[d], back_ctx.at[me_s], cs.at[d], cr.at[me_s], (d, me_d)).wait_send()
        peer_copy(stats.at[me_s], back_stats.at[s], ss.at[s], sr.at[s], (s, me_d)).wait_recv()
        peer_copy(ctx.at[me_s], back_ctx.at[s], cs.at[s], cr.at[s], (s, me_d)).wait_recv()


def attend_kernel(scale, heads, rows, e_ref, q_ref, kv_ref, ctx_ref, stats_ref):
    key_len = SPAN * 2
    keys_total, width = kv_ref.shape[0], heads * HD
    per_tile = rows // SPAN
    col_block = lax.broadcasted_iota(jnp.int32, (1, keys_total), 1) // key_len
    row_block = lax.broadcasted_iota(jnp.int32, (rows, 1), 0) // SPAN

    def one_tile(t, carry):
        start = pl.multiple_of(t * rows, rows)
        row_entry = jnp.zeros((rows, 1), jnp.int32)
        for j in range(per_tile):
            row_entry = jnp.where(row_block == j, e_ref[t * per_tile + j], row_entry)
        named = col_block == row_entry
        for h in range(heads):
            q = q_ref[pl.ds(start, rows), h * HD:(h + 1) * HD]
            k = kv_ref[:, h * HD:(h + 1) * HD]
            v = kv_ref[:, width + h * HD:width + (h + 1) * HD]
            s = lax.dot_general(
                q, k, (((1,), (1,)), ((), ())), preferred_element_type=jnp.float32
            ) * scale
            s = jnp.where(named, s, -jnp.inf)
            top = jnp.max(s, axis=1, keepdims=True)
            w = jnp.exp(s - top)
            total = jnp.sum(w, axis=1, keepdims=True)
            ctx = jnp.dot(w.astype(jnp.bfloat16), v, preferred_element_type=jnp.float32)
            ctx_ref[pl.ds(start, rows), h * HD:(h + 1) * HD] = (ctx / total).astype(ctx_ref.dtype)
            stats_ref[pl.ds(start, rows), 2 * h:2 * h + 1] = top
            stats_ref[pl.ds(start, rows), 2 * h + 1:2 * h + 2] = total
        return carry

    lax.fori_loop(0, q_ref.shape[0] // rows, one_tile, 0)


def vmem_whole(shape):
    return pl.BlockSpec(shape, lambda *_: (0,) * len(shape))


def attend(recv_q, recv_e, kv_flat, heads):
    n_src, cap, span, width = recv_q.shape
    q_rows = recv_q.reshape(n_src * cap * span, width)
    kv_rows = kv_flat.reshape(-1, kv_flat.shape[2])
    stats_shape = (q_rows.shape[0], 2 * heads)
    grid_spec = pltpu.PrefetchScalarGridSpec(
        num_scalar_prefetch=1,
        grid=(1,),
        in_specs=[vmem_whole(q_rows.shape), vmem_whole(kv_rows.shape)],
        out_specs=[vmem_whole(q_rows.shape), vmem_whole(stats_shape)],
    )
    ctx, stats = pl.pallas_call(
        functools.partial(attend_kernel, 1.0 / math.sqrt(HD), heads, 4 * span),
        grid_spec=grid_spec,
        out_shape=(
            jax.ShapeDtypeStruct(q_rows.shape, jnp.bfloat16),
            jax.ShapeDtypeStruct(stats_shape, jnp.float32),
        ),
    )(recv_e, q_rows, kv_rows)
    return ctx.reshape(recv_q.shape), stats.reshape(n_src, cap, span, 2 * heads)


def attend_back_kernel(n_seq, n_db, heads, scale, send_e, send_q, kv_ref, w_loc, back_ctx,
                       back_stats, stage_ctx, stage_stats, w_cols, ctx_v, stats_v, recv_q,
                       recv_e, cs, cr, ss, sr, ws, wr, ls, stg, qs, qr, es, er):
    me_s = lax.axis_index("seq")
    me_d = lax.axis_index("db")
    rows = stage_ctx.shape[1]
    keys_total = kv_ref.shape[0]
    width = heads * HD
    cap = rows // SPAN
    key_block = lax.broadcasted_iota(jnp.int32, (keys_total, 1), 0) // (2 * SPAN)
    lane_place = lax.broadcasted_iota(jnp.int32, (1, rows), 1) // SPAN

    barrier = pltpu.get_barrier_semaphore()

    @pl.loop(1, n_seq)
    def _(o):
        pl.semaphore_signal(barrier, inc=1, device_id=(lax.rem(me_s + o, n_seq), me_d),
                            device_id_type=MESH)

    @pl.loop(1, n_db)
    def _(o):
        pl.semaphore_signal(barrier, inc=1, device_id=(me_s, lax.rem(me_d + o, n_db)),
                            device_id_type=MESH)

    pl.semaphore_wait(barrier, (n_seq - 1) + (n_db - 1))

    features = w_cols.shape[2]

    def w_src(d):
        return w_loc.at[:, pl.ds(pl.multiple_of(d * features, features), features)]

    own_w = pltpu.make_async_copy(w_src(me_d), w_cols.at[me_d], ls.at[4])
    own_w.start()

    own_in = [
        pltpu.make_async_copy(send_q.at[me_s], recv_q.at[me_s], ls.at[0]),
        pltpu.make_async_copy(send_e.at[me_s], recv_e.at[me_s], ls.at[1]),
    ]
    for c in own_in:
        c.start()

    def q_in(d, s):
        return peer_copy(send_q.at[d], recv_q.at[s], qs.at[d], qr.at[s], (d, me_d))

    def e_in(d, s):
        return peer_copy(send_e.at[d], recv_e.at[s], es.at[d], er.at[s], (d, me_d))

    @pl.loop(1, n_seq)
    def _(o):
        d = lax.rem(me_s + o, n_seq)
        e_in(d, me_s).start()
        q_in(d, me_s).start()

    @pl.loop(1, n_db)
    def _(o):
        d = lax.rem(me_d + o, n_db)
        peer_copy(w_src(d), w_cols.at[me_d], ws.at[d], wr.at[me_d], (me_s, d)).start()

    def compute(d, slot):
        entry = recv_e[pl.ds(d, 1), 0:rows]
        named = key_block == entry
        stats_v[slot] = jnp.zeros(stats_v.shape[1:], stats_v.dtype)
        for h in range(heads):
            q = recv_q[d, :, h * HD:(h + 1) * HD]
            k = kv_ref[:, h * HD:(h + 1) * HD]
            v = kv_ref[:, width + h * HD:width + (h + 1) * HD]
            st = lax.dot_general(
                k, q, (((1,), (1,)), ((), ())), preferred_element_type=jnp.float32
            ) * scale
            st = jnp.where(named, st, -jnp.inf)
            top = jnp.max(st, axis=0, keepdims=True)
            w = jnp.exp(st - top)
            total = jnp.sum(w, axis=0, keepdims=True)
            u = lax.dot_general(
                w.astype(jnp.bfloat16), v, (((0,), (0,)), ((), ())),
                preferred_element_type=jnp.float32,
            )
            ctx_v[slot, :, h * HD:(h + 1) * HD] = u.astype(ctx_v.dtype)
            stats_v[slot, 2 * h:2 * h + 1, 0:rows] = top
            stats_v[slot, 2 * h + 1:2 * h + 2, 0:rows] = total

    def staged(d, slot):
        return [
            pltpu.make_async_copy(ctx_v.at[slot], stage_ctx.at[d], stg.at[0, slot]),
            pltpu.make_async_copy(stats_v.at[slot], stage_stats.at[d], stg.at[1, slot]),
        ]

    def send(d):
        peer_copy(stage_stats.at[d], back_stats.at[me_s], ss.at[d], sr.at[me_s], (d, me_d)).start()
        peer_copy(stage_ctx.at[d], back_ctx.at[me_s], cs.at[d], cr.at[me_s], (d, me_d)).start()

    for c in own_in:
        c.wait()
    compute(me_s, 0)
    for c in staged(me_s, 0):
        c.start()
    for c in staged(me_s, 0):
        c.wait()
    own = [
        pltpu.make_async_copy(stage_ctx.at[me_s], back_ctx.at[me_s], ls.at[2]),
        pltpu.make_async_copy(stage_stats.at[me_s], back_stats.at[me_s], ls.at[3]),
    ]
    for c in own:
        c.start()

    @pl.loop(1, n_seq)
    def _(o):
        d = lax.rem(me_s + o, n_seq)
        slot = lax.rem(o, 2)
        e_in(me_s, d).wait_recv()
        q_in(me_s, d).wait_recv()
        compute(d, slot)
        for c in staged(d, slot):
            c.start()

        @pl.when(o > 1)
        def _():
            prev = lax.rem(me_s + o - 1, n_seq)
            for c in staged(prev, 1 - slot):
                c.wait()
            send(prev)

    last = lax.rem(me_s + n_seq - 1, n_seq)
    for c in staged(last, (n_seq - 1) % 2):
        c.wait()
    send(last)

    for c in own:
        c.wait()

    @pl.loop(1, n_seq)
    def _(o):
        d = lax.rem(me_s + o, n_seq)
        e_in(d, me_s).wait_send()
        q_in(d, me_s).wait_send()

    @pl.loop(1, n_seq)
    def _(o):
        d = lax.rem(me_s + o, n_seq)
        s = lax.rem(me_s + n_seq - o, n_seq)
        peer_copy(stage_stats.at[d], back_stats.at[me_s], ss.at[d], sr.at[me_s], (d, me_d)).wait_send()
        peer_copy(stage_ctx.at[d], back_ctx.at[me_s], cs.at[d], cr.at[me_s], (d, me_d)).wait_send()
        peer_copy(stage_stats.at[me_s], back_stats.at[s], ss.at[s], sr.at[s], (s, me_d)).wait_recv()
        peer_copy(stage_ctx.at[me_s], back_ctx.at[s], cs.at[s], cr.at[s], (s, me_d)).wait_recv()

    own_w.wait()

    @pl.loop(1, n_db)
    def _(o):
        d = lax.rem(me_d + o, n_db)
        s = lax.rem(me_d + n_db - o, n_db)
        peer_copy(w_src(d), w_cols.at[me_d], ws.at[d], wr.at[me_d], (me_s, d)).wait_send()
        peer_copy(w_src(me_d), w_cols.at[s], ws.at[s], wr.at[s], (me_s, s)).wait_recv()


def attend_back(send_q, send_e, kv_flat, w_loc, heads, n_seq, n_db):
    n_src, rows, width = send_q.shape
    kv_rows = kv_flat.reshape(-1, kv_flat.shape[2])
    stats_shape = (n_src, 8, 2 * LANES)
    ctx_shape = (n_src, rows, width)
    dma = pltpu.SemaphoreType.DMA
    outs = pl.pallas_call(
        functools.partial(attend_back_kernel, n_seq, n_db, heads, 1.0 / math.sqrt(HD)),
        out_shape=(
            jax.ShapeDtypeStruct(ctx_shape, jnp.bfloat16),
            jax.ShapeDtypeStruct(stats_shape, jnp.float32),
            jax.ShapeDtypeStruct(ctx_shape, jnp.bfloat16),
            jax.ShapeDtypeStruct(stats_shape, jnp.float32),
            jax.ShapeDtypeStruct((n_db, w_loc.shape[0], w_loc.shape[1] // n_db), w_loc.dtype),
        ),
        in_specs=[
            any_spec(),
            any_spec(),
            pl.BlockSpec(memory_space=pltpu.VMEM),
            any_spec(),
        ],
        out_specs=(any_spec(), any_spec(), any_spec(), any_spec(), any_spec()),
        scratch_shapes=[
            pltpu.VMEM((2, rows, width), jnp.bfloat16),
            pltpu.VMEM((2,) + stats_shape[1:], jnp.float32),
            pltpu.VMEM(send_q.shape, send_q.dtype),
            pltpu.VMEM(send_e.shape, send_e.dtype),
            dma((n_seq,)), dma((n_seq,)), dma((n_seq,)), dma((n_seq,)),
            dma((n_db,)), dma((n_db,)), dma((5,)), dma((2, 2)),
            dma((n_seq,)), dma((n_seq,)), dma((n_seq,)), dma((n_seq,)),
        ],
        compiler_params=pltpu.CompilerParams(collective_id=1, has_side_effects=True),
    )(send_e, send_q, kv_rows, w_loc)
    return outs[0], outs[1], outs[4]


def combine_kernel(heads, place_ref, count_ref, ctx_ref, stats_ref, out_ref, stats_t):
    for s in range(stats_ref.shape[0]):
        stats_t[s] = jnp.transpose(stats_ref[s])

    def one_span(c, carry):
        p0 = place_ref[c * K]
        p1 = place_ref[c * K + 1]
        r0 = pl.multiple_of(lax.rem(p0, CAP) * SPAN, SPAN)
        r1 = pl.multiple_of(lax.rem(p1, CAP) * SPAN, SPAN)
        st0 = stats_t[p0 // CAP, pl.ds(r0, SPAN), :]
        st1 = stats_t[p1 // CAP, pl.ds(r1, SPAN), :]
        live1 = count_ref[c] > 1
        for h in range(heads):
            cols = slice(h * HD, (h + 1) * HD)
            m0, l0 = st0[:, 2 * h:2 * h + 1], st0[:, 2 * h + 1:2 * h + 2]
            m1, l1 = st1[:, 2 * h:2 * h + 1], st1[:, 2 * h + 1:2 * h + 2]
            best = jnp.where(live1, jnp.maximum(m0, m1), m0)
            a0 = jnp.exp(m0 - best)
            a1 = jnp.where(live1, jnp.exp(m1 - best), 0.0)
            u0 = ctx_ref[p0, :, cols].astype(jnp.float32)
            u1 = jnp.where(live1, ctx_ref[p1, :, cols].astype(jnp.float32), 0.0)
            out_ref[c, :, cols] = (
                (a0 * u0 + a1 * u1) / (a0 * l0 + a1 * l1)
            ).astype(out_ref.dtype)
        return carry

    lax.fori_loop(0, out_ref.shape[0], one_span, 0, unroll=True)


def combine(back_ctx, back_stats, place, neighbour_count, heads):
    places, span, width = back_ctx.shape
    spans = neighbour_count.shape[0]
    n_src, st_rows, st_cols = back_stats.shape
    grid_spec = pltpu.PrefetchScalarGridSpec(
        num_scalar_prefetch=2,
        grid=(1,),
        in_specs=[vmem_whole(back_ctx.shape), vmem_whole(back_stats.shape)],
        out_specs=vmem_whole((spans, span, width)),
        scratch_shapes=[pltpu.VMEM((n_src, st_cols, st_rows), jnp.float32)],
    )
    return pl.pallas_call(
        functools.partial(combine_kernel, heads),
        grid_spec=grid_spec,
        out_shape=jax.ShapeDtypeStruct((spans, span, width), jnp.bfloat16),
    )(place, neighbour_count, back_ctx, back_stats)


def pack_kernel(src_ref, q_ref, out_ref):
    def one_place(p, carry):
        span = src_ref[p]
        rows = q_ref[jnp.maximum(span, 0)]
        out_ref[p] = jnp.where(span >= 0, rows, jnp.zeros_like(rows))
        return carry

    lax.fori_loop(0, out_ref.shape[0], one_place, 0)


def pack(queries, src_span, places):
    grid_spec = pltpu.PrefetchScalarGridSpec(
        num_scalar_prefetch=1,
        grid=(1,),
        in_specs=[vmem_whole(queries.shape)],
        out_specs=vmem_whole((places,) + queries.shape[1:]),
    )
    return pl.pallas_call(
        pack_kernel,
        grid_spec=grid_spec,
        out_shape=jax.ShapeDtypeStruct((places,) + queries.shape[1:], queries.dtype),
    )(src_span, queries)


def any_spec():
    return pl.BlockSpec(memory_space=pl.ANY)


def exchange_out(send_q, send_e, n_seq):
    dma = pltpu.SemaphoreType.DMA
    return pl.pallas_call(
        functools.partial(out_kernel, n_seq),
        out_shape=(
            jax.ShapeDtypeStruct(send_q.shape, send_q.dtype),
            jax.ShapeDtypeStruct(send_e.shape, send_e.dtype),
        ),
        in_specs=[any_spec()] * 2,
        out_specs=(any_spec(), any_spec()),
        scratch_shapes=[dma((n_seq,)), dma((n_seq,)), dma((n_seq,)), dma((n_seq,)), dma((2,))],
        compiler_params=pltpu.CompilerParams(collective_id=0, has_side_effects=True),
    )(send_q, send_e)


def exchange_back(ctx, stats, n_seq):
    dma = pltpu.SemaphoreType.DMA
    return pl.pallas_call(
        functools.partial(back_kernel, n_seq),
        out_shape=(
            jax.ShapeDtypeStruct(ctx.shape, ctx.dtype),
            jax.ShapeDtypeStruct(stats.shape, stats.dtype),
        ),
        in_specs=[any_spec()] * 2,
        out_specs=(any_spec(), any_spec()),
        scratch_shapes=[dma((n_seq,)), dma((n_seq,)), dma((n_seq,)), dma((n_seq,)), dma((2,))],
        compiler_params=pltpu.CompilerParams(collective_id=1, has_side_effects=True),
    )(ctx, stats)


def on_device(
    decoder_states,
    query_weight,
    output_weight,
    neighbour_kv,
    neighbour_shard,
    neighbour_entry,
    neighbour_count,
):
    tok_rows = decoder_states.shape[0]
    span_total = tok_rows // SPAN
    row_width = query_weight.shape[1]
    heads_here = row_width // HD
    key_len = neighbour_kv.shape[1]
    n_seq = lax.psum(1, "seq")
    n_db = lax.psum(1, "db")
    places_total = n_seq * CAP
    queries = jnp.dot(decoder_states, query_weight, preferred_element_type=jnp.float32).astype(
        jnp.bfloat16
    )
    queries = queries.reshape(span_total, SPAN, row_width)

    live, place = slot_places(neighbour_shard, neighbour_count)
    target = jnp.where(live, place, places_total)
    span_of_slot = jnp.arange(span_total * K, dtype=jnp.int32) // K
    src_span = jnp.full((places_total,), -1, jnp.int32)
    src_span = src_span.at[target].set(span_of_slot, mode="drop")
    send_q = pack(queries, src_span, places_total)
    send_e = jnp.zeros((places_total,), jnp.int32)
    send_e = send_e.at[target].set(neighbour_entry.reshape(-1), mode="drop")
    send_e = jnp.repeat(send_e.reshape(n_seq, CAP), SPAN, axis=1)
    send_e = jnp.pad(send_e, ((0, 0), (0, 2 * LANES - CAP * SPAN)))
    kv_flat = neighbour_kv.reshape(neighbour_kv.shape[0], key_len, 2 * row_width)
    back_ctx, back_stats, weight_cols = attend_back(
        send_q.reshape(n_seq, CAP * SPAN, row_width), send_e, kv_flat, output_weight,
        heads_here, n_seq, n_db
    )
    back_ctx = back_ctx.reshape(places_total, SPAN, row_width)
    context = combine(back_ctx, back_stats, place, neighbour_count, heads_here)
    context = context.reshape(tok_rows, row_width)

    contexts = lax.all_gather(context, "db", axis=0, tiled=False)
    out = jnp.einsum(
        "str,srf->tf", contexts, weight_cols, preferred_element_type=jnp.float32
    )
    return out.astype(jnp.bfloat16)


def solution(mesh):
    in_specs = (
        P("seq", None),
        P(None, "db"),
        P("db", None),
        P("seq", None, None, "db"),
        P("seq", None),
        P("seq", None),
        P("seq"),
    )
    out_specs = P("seq", "db")
    return jax.shard_map(
        on_device, mesh=mesh, in_specs=in_specs, out_specs=out_specs, check_vma=False
    )
```

```python
import functools
import math

import jax
import jax.numpy as jnp
from jax import lax
from jax.experimental import pallas as pl
from jax.experimental.pallas import tpu as pltpu
from jax.sharding import PartitionSpec as P

HD = 128
SPAN = 64
K = 2
CAP = 3
LANES = 128
MESH = pl.DeviceIdType.MESH


def slot_places(neighbour_shard, neighbour_count):
    own_shard = neighbour_shard.reshape(-1)
    slots = own_shard.shape[0]
    own_live = (
        jnp.arange(K, dtype=jnp.int32)[None, :] < neighbour_count[:, None]
    ).reshape(-1)
    same = (own_shard[None, :] == own_shard[:, None]) & own_live[None, :]
    earlier = jnp.arange(slots)[None, :] < jnp.arange(slots)[:, None]
    own_rank = jnp.minimum(jnp.sum((same & earlier).astype(jnp.int32), axis=1), CAP - 1)
    return own_live, own_shard * CAP + own_rank


def peer_copy(src, dst, send_sem, recv_sem, device):
    return pltpu.make_async_remote_copy(
        src_ref=src, dst_ref=dst, send_sem=send_sem, recv_sem=recv_sem,
        device_id=device, device_id_type=MESH,
    )


def out_kernel(n_seq, send_q, send_e, recv_q, recv_e, qs, qr, es, er, ls):
    me_s = lax.axis_index("seq")
    me_d = lax.axis_index("db")

    barrier = pltpu.get_barrier_semaphore()

    @pl.loop(1, n_seq)
    def _(o):
        pl.semaphore_signal(barrier, inc=1, device_id=(lax.rem(me_s + o, n_seq), me_d),
                            device_id_type=MESH)

    pl.semaphore_wait(barrier, n_seq - 1)

    own = [
        pltpu.make_async_copy(send_q.at[me_s], recv_q.at[me_s], ls.at[0]),
        pltpu.make_async_copy(send_e.at[me_s], recv_e.at[me_s], ls.at[1]),
    ]
    for c in own:
        c.start()

    @pl.loop(1, n_seq)
    def _(o):
        d = lax.rem(me_s + o, n_seq)
        peer_copy(send_e.at[d], recv_e.at[me_s], es.at[d], er.at[me_s], (d, me_d)).start()
        peer_copy(send_q.at[d], recv_q.at[me_s], qs.at[d], qr.at[me_s], (d, me_d)).start()

    for c in own:
        c.wait()

    @pl.loop(1, n_seq)
    def _(o):
        d = lax.rem(me_s + o, n_seq)
        s = lax.rem(me_s + n_seq - o, n_seq)
        peer_copy(send_e.at[d], recv_e.at[me_s], es.at[d], er.at[me_s], (d, me_d)).wait_send()
        peer_copy(send_q.at[d], recv_q.at[me_s], qs.at[d], qr.at[me_s], (d, me_d)).wait_send()
        peer_copy(send_e.at[me_s], recv_e.at[s], es.at[s], er.at[s], (s, me_d)).wait_recv()
        peer_copy(send_q.at[me_s], recv_q.at[s], qs.at[s], qr.at[s], (s, me_d)).wait_recv()


def back_kernel(n_seq, ctx, stats, back_ctx, back_stats, cs, cr, ss, sr, ls):
    me_s = lax.axis_index("seq")
    me_d = lax.axis_index("db")
    barrier = pltpu.get_barrier_semaphore()

    @pl.loop(1, n_seq)
    def _(o):
        pl.semaphore_signal(barrier, inc=1, device_id=(lax.rem(me_s + o, n_seq), me_d),
                            device_id_type=MESH)

    pl.semaphore_wait(barrier, n_seq - 1)

    own = [
        pltpu.make_async_copy(ctx.at[me_s], back_ctx.at[me_s], ls.at[0]),
        pltpu.make_async_copy(stats.at[me_s], back_stats.at[me_s], ls.at[1]),
    ]
    for c in own:
        c.start()

    @pl.loop(1, n_seq)
    def _(o):
        d = lax.rem(me_s + o, n_seq)
        peer_copy(stats.at[d], back_stats.at[me_s], ss.at[d], sr.at[me_s], (d, me_d)).start()
        peer_copy(ctx.at[d], back_ctx.at[me_s], cs.at[d], cr.at[me_s], (d, me_d)).start()

    for c in own:
        c.wait()

    @pl.loop(1, n_seq)
    def _(o):
        d = lax.rem(me_s + o, n_seq)
        s = lax.rem(me_s + n_seq - o, n_seq)
        peer_copy(stats.at[d], back_stats.at[me_s], ss.at[d], sr.at[me_s], (d, me_d)).wait_send()
        peer_copy(ctx.at[d], back_ctx.at[me_s], cs.at[d], cr.at[me_s], (d, me_d)).wait_send()
        peer_copy(stats.at[me_s], back_stats.at[s], ss.at[s], sr.at[s], (s, me_d)).wait_recv()
        peer_copy(ctx.at[me_s], back_ctx.at[s], cs.at[s], cr.at[s], (s, me_d)).wait_recv()


def attend_kernel(scale, heads, rows, e_ref, q_ref, kv_ref, ctx_ref, stats_ref):
    key_len = SPAN * 2
    keys_total, width = kv_ref.shape[0], heads * HD
    per_tile = rows // SPAN
    col_block = lax.broadcasted_iota(jnp.int32, (1, keys_total), 1) // key_len
    row_block = lax.broadcasted_iota(jnp.int32, (rows, 1), 0) // SPAN

    def one_tile(t, carry):
        start = pl.multiple_of(t * rows, rows)
        row_entry = jnp.zeros((rows, 1), jnp.int32)
        for j in range(per_tile):
            row_entry = jnp.where(row_block == j, e_ref[t * per_tile + j], row_entry)
        named = col_block == row_entry
        for h in range(heads):
            q = q_ref[pl.ds(start, rows), h * HD:(h + 1) * HD]
            k = kv_ref[:, h * HD:(h + 1) * HD]
            v = kv_ref[:, width + h * HD:width + (h + 1) * HD]
            s = lax.dot_general(
                q, k, (((1,), (1,)), ((), ())), preferred_element_type=jnp.float32
            ) * scale
            s = jnp.where(named, s, -jnp.inf)
            top = jnp.max(s, axis=1, keepdims=True)
            w = jnp.exp(s - top)
            total = jnp.sum(w, axis=1, keepdims=True)
            ctx = jnp.dot(w.astype(jnp.bfloat16), v, preferred_element_type=jnp.float32)
            ctx_ref[pl.ds(start, rows), h * HD:(h + 1) * HD] = (ctx / total).astype(ctx_ref.dtype)
            stats_ref[pl.ds(start, rows), 2 * h:2 * h + 1] = top
            stats_ref[pl.ds(start, rows), 2 * h + 1:2 * h + 2] = total
        return carry

    lax.fori_loop(0, q_ref.shape[0] // rows, one_tile, 0)


def vmem_whole(shape):
    return pl.BlockSpec(shape, lambda *_: (0,) * len(shape))


def attend(recv_q, recv_e, kv_flat, heads):
    n_src, cap, span, width = recv_q.shape
    q_rows = recv_q.reshape(n_src * cap * span, width)
    kv_rows = kv_flat.reshape(-1, kv_flat.shape[2])
    stats_shape = (q_rows.shape[0], 2 * heads)
    grid_spec = pltpu.PrefetchScalarGridSpec(
        num_scalar_prefetch=1,
        grid=(1,),
        in_specs=[vmem_whole(q_rows.shape), vmem_whole(kv_rows.shape)],
        out_specs=[vmem_whole(q_rows.shape), vmem_whole(stats_shape)],
    )
    ctx, stats = pl.pallas_call(
        functools.partial(attend_kernel, 1.0 / math.sqrt(HD), heads, 4 * span),
        grid_spec=grid_spec,
        out_shape=(
            jax.ShapeDtypeStruct(q_rows.shape, jnp.bfloat16),
            jax.ShapeDtypeStruct(stats_shape, jnp.float32),
        ),
    )(recv_e, q_rows, kv_rows)
    return ctx.reshape(recv_q.shape), stats.reshape(n_src, cap, span, 2 * heads)


def attend_back_kernel(n_seq, n_db, heads, scale, send_e, send_q, kv_ref, w_loc, back_ctx,
                       back_stats, stage_ctx, stage_stats, w_cols, ctx_v, stats_v, recv_q,
                       recv_e, cs, cr, ss, sr, ws, wr, ls, stg, qs, qr, es, er):
    me_s = lax.axis_index("seq")
    me_d = lax.axis_index("db")
    rows = stage_ctx.shape[1]
    keys_total = kv_ref.shape[0]
    width = heads * HD
    cap = rows // SPAN
    key_block = lax.broadcasted_iota(jnp.int32, (keys_total, 1), 0) // (2 * SPAN)
    lane_place = lax.broadcasted_iota(jnp.int32, (1, rows), 1) // SPAN

    barrier = pltpu.get_barrier_semaphore()

    @pl.loop(1, n_seq)
    def _(o):
        pl.semaphore_signal(barrier, inc=1, device_id=(lax.rem(me_s + o, n_seq), me_d),
                            device_id_type=MESH)

    @pl.loop(1, n_db)
    def _(o):
        pl.semaphore_signal(barrier, inc=1, device_id=(me_s, lax.rem(me_d + o, n_db)),
                            device_id_type=MESH)

    pl.semaphore_wait(barrier, (n_seq - 1) + (n_db - 1))

    features = w_cols.shape[2]

    def w_src(d):
        return w_loc.at[:, pl.ds(pl.multiple_of(d * features, features), features)]

    own_w = pltpu.make_async_copy(w_src(me_d), w_cols.at[me_d], ls.at[4])
    own_w.start()

    own_in = [
        pltpu.make_async_copy(send_q.at[me_s], recv_q.at[me_s], ls.at[0]),
        pltpu.make_async_copy(send_e.at[me_s], recv_e.at[me_s], ls.at[1]),
    ]
    for c in own_in:
        c.start()

    def q_in(d, s):
        return peer_copy(send_q.at[d], recv_q.at[s], qs.at[d], qr.at[s], (d, me_d))

    def e_in(d, s):
        return peer_copy(send_e.at[d], recv_e.at[s], es.at[d], er.at[s], (d, me_d))

    @pl.loop(1, n_seq)
    def _(o):
        d = lax.rem(me_s + o, n_seq)
        e_in(d, me_s).start()
        q_in(d, me_s).start()

    @pl.loop(1, n_db)
    def _(o):
        d = lax.rem(me_d + o, n_db)
        peer_copy(w_src(d), w_cols.at[me_d], ws.at[d], wr.at[me_d], (me_s, d)).start()

    def compute(d, slot):
        entry = recv_e[pl.ds(d, 1), 0:rows]
        named = key_block == entry
        stats_v[slot] = jnp.zeros(stats_v.shape[1:], stats_v.dtype)
        for h in range(heads):
            q = recv_q[d, :, h * HD:(h + 1) * HD]
            k = kv_ref[:, h * HD:(h + 1) * HD]
            v = kv_ref[:, width + h * HD:width + (h + 1) * HD]
            st = lax.dot_general(
                k, q, (((1,), (1,)), ((), ())), preferred_element_type=jnp.float32
            ) * scale
            st = jnp.where(named, st, -jnp.inf)
            top = jnp.max(st, axis=0, keepdims=True)
            w = jnp.exp(st - top)
            total = jnp.sum(w, axis=0, keepdims=True)
            u = lax.dot_general(
                w.astype(jnp.bfloat16), v, (((0,), (0,)), ((), ())),
                preferred_element_type=jnp.float32,
            )
            ctx_v[slot, :, h * HD:(h + 1) * HD] = u.astype(ctx_v.dtype)
            stats_v[slot, 2 * h:2 * h + 1, 0:rows] = top
            stats_v[slot, 2 * h + 1:2 * h + 2, 0:rows] = total

    def staged(d, slot):
        return [
            pltpu.make_async_copy(ctx_v.at[slot], stage_ctx.at[d], stg.at[0, slot]),
            pltpu.make_async_copy(stats_v.at[slot], stage_stats.at[d], stg.at[1, slot]),
        ]

    def send(d):
        peer_copy(stage_stats.at[d], back_stats.at[me_s], ss.at[d], sr.at[me_s], (d, me_d)).start()
        peer_copy(stage_ctx.at[d], back_ctx.at[me_s], cs.at[d], cr.at[me_s], (d, me_d)).start()

    for c in own_in:
        c.wait()
    compute(me_s, 0)
    for c in staged(me_s, 0):
        c.start()
    for c in staged(me_s, 0):
        c.wait()
    own = [
        pltpu.make_async_copy(stage_ctx.at[me_s], back_ctx.at[me_s], ls.at[2]),
        pltpu.make_async_copy(stage_stats.at[me_s], back_stats.at[me_s], ls.at[3]),
    ]
    for c in own:
        c.start()

    @pl.loop(1, n_seq)
    def _(o):
        d = lax.rem(me_s + o, n_seq)
        slot = lax.rem(o, 2)
        e_in(me_s, d).wait_recv()
        q_in(me_s, d).wait_recv()
        compute(d, slot)
        for c in staged(d, slot):
            c.start()

        @pl.when(o > 1)
        def _():
            prev = lax.rem(me_s + o - 1, n_seq)
            for c in staged(prev, 1 - slot):
                c.wait()
            send(prev)

    last = lax.rem(me_s + n_seq - 1, n_seq)
    for c in staged(last, (n_seq - 1) % 2):
        c.wait()
    send(last)

    for c in own:
        c.wait()

    @pl.loop(1, n_seq)
    def _(o):
        d = lax.rem(me_s + o, n_seq)
        e_in(d, me_s).wait_send()
        q_in(d, me_s).wait_send()

    @pl.loop(1, n_seq)
    def _(o):
        d = lax.rem(me_s + o, n_seq)
        s = lax.rem(me_s + n_seq - o, n_seq)
        peer_copy(stage_stats.at[d], back_stats.at[me_s], ss.at[d], sr.at[me_s], (d, me_d)).wait_send()
        peer_copy(stage_ctx.at[d], back_ctx.at[me_s], cs.at[d], cr.at[me_s], (d, me_d)).wait_send()
        peer_copy(stage_stats.at[me_s], back_stats.at[s], ss.at[s], sr.at[s], (s, me_d)).wait_recv()
        peer_copy(stage_ctx.at[me_s], back_ctx.at[s], cs.at[s], cr.at[s], (s, me_d)).wait_recv()

    own_w.wait()

    @pl.loop(1, n_db)
    def _(o):
        d = lax.rem(me_d + o, n_db)
        s = lax.rem(me_d + n_db - o, n_db)
        peer_copy(w_src(d), w_cols.at[me_d], ws.at[d], wr.at[me_d], (me_s, d)).wait_send()
        peer_copy(w_src(me_d), w_cols.at[s], ws.at[s], wr.at[s], (me_s, s)).wait_recv()


def attend_back(send_q, send_e, kv_flat, w_loc, heads, n_seq, n_db):
    n_src, rows, width = send_q.shape
    kv_rows = kv_flat.reshape(-1, kv_flat.shape[2])
    stats_shape = (n_src, 8, 2 * LANES)
    ctx_shape = (n_src, rows, width)
    dma = pltpu.SemaphoreType.DMA
    outs = pl.pallas_call(
        functools.partial(attend_back_kernel, n_seq, n_db, heads, 1.0 / math.sqrt(HD)),
        out_shape=(
            jax.ShapeDtypeStruct(ctx_shape, jnp.bfloat16),
            jax.ShapeDtypeStruct(stats_shape, jnp.float32),
            jax.ShapeDtypeStruct(ctx_shape, jnp.bfloat16),
            jax.ShapeDtypeStruct(stats_shape, jnp.float32),
            jax.ShapeDtypeStruct((n_db, w_loc.shape[0], w_loc.shape[1] // n_db), w_loc.dtype),
        ),
        in_specs=[
            any_spec(),
            any_spec(),
            pl.BlockSpec(memory_space=pltpu.VMEM),
            any_spec(),
        ],
        out_specs=(any_spec(), any_spec(), any_spec(), any_spec(), any_spec()),
        scratch_shapes=[
            pltpu.VMEM((2, rows, width), jnp.bfloat16),
            pltpu.VMEM((2,) + stats_shape[1:], jnp.float32),
            pltpu.VMEM(send_q.shape, send_q.dtype),
            pltpu.VMEM(send_e.shape, send_e.dtype),
            dma((n_seq,)), dma((n_seq,)), dma((n_seq,)), dma((n_seq,)),
            dma((n_db,)), dma((n_db,)), dma((5,)), dma((2, 2)),
            dma((n_seq,)), dma((n_seq,)), dma((n_seq,)), dma((n_seq,)),
        ],
        compiler_params=pltpu.CompilerParams(collective_id=1, has_side_effects=True),
    )(send_e, send_q, kv_rows, w_loc)
    return outs[0], outs[1], outs[4]


def combine_kernel(heads, place_ref, count_ref, ctx_ref, stats_ref, out_ref, stats_t):
    for s in range(stats_ref.shape[0]):
        stats_t[s] = jnp.transpose(stats_ref[s])

    def one_span(c, carry):
        p0 = place_ref[c * K]
        p1 = place_ref[c * K + 1]
        r0 = pl.multiple_of(lax.rem(p0, CAP) * SPAN, SPAN)
        r1 = pl.multiple_of(lax.rem(p1, CAP) * SPAN, SPAN)
        st0 = stats_t[p0 // CAP, pl.ds(r0, SPAN), :]
        st1 = stats_t[p1 // CAP, pl.ds(r1, SPAN), :]
        live1 = count_ref[c] > 1
        for h in range(heads):
            cols = slice(h * HD, (h + 1) * HD)
            m0, l0 = st0[:, 2 * h:2 * h + 1], st0[:, 2 * h + 1:2 * h + 2]
            m1, l1 = st1[:, 2 * h:2 * h + 1], st1[:, 2 * h + 1:2 * h + 2]
            best = jnp.where(live1, jnp.maximum(m0, m1), m0)
            a0 = jnp.exp(m0 - best)
            a1 = jnp.where(live1, jnp.exp(m1 - best), 0.0)
            u0 = ctx_ref[p0, :, cols].astype(jnp.float32)
            u1 = jnp.where(live1, ctx_ref[p1, :, cols].astype(jnp.float32), 0.0)
            out_ref[c, :, cols] = (
                (a0 * u0 + a1 * u1) / (a0 * l0 + a1 * l1)
            ).astype(out_ref.dtype)
        return carry

    lax.fori_loop(0, out_ref.shape[0], one_span, 0, unroll=True)


def combine(back_ctx, back_stats, place, neighbour_count, heads):
    places, span, width = back_ctx.shape
    spans = neighbour_count.shape[0]
    n_src, st_rows, st_cols = back_stats.shape
    grid_spec = pltpu.PrefetchScalarGridSpec(
        num_scalar_prefetch=2,
        grid=(1,),
        in_specs=[vmem_whole(back_ctx.shape), vmem_whole(back_stats.shape)],
        out_specs=vmem_whole((spans, span, width)),
        scratch_shapes=[pltpu.VMEM((n_src, st_cols, st_rows), jnp.float32)],
    )
    return pl.pallas_call(
        functools.partial(combine_kernel, heads),
        grid_spec=grid_spec,
        out_shape=jax.ShapeDtypeStruct((spans, span, width), jnp.bfloat16),
    )(place, neighbour_count, back_ctx, back_stats)


def pack_kernel(src_ref, q_ref, out_ref):
    def one_place(p, carry):
        span = src_ref[p]
        rows = q_ref[jnp.maximum(span, 0)]
        out_ref[p] = jnp.where(span >= 0, rows, jnp.zeros_like(rows))
        return carry

    lax.fori_loop(0, out_ref.shape[0], one_place, 0, unroll=8)


def pack(queries, src_span, places):
    grid_spec = pltpu.PrefetchScalarGridSpec(
        num_scalar_prefetch=1,
        grid=(1,),
        in_specs=[vmem_whole(queries.shape)],
        out_specs=vmem_whole((places,) + queries.shape[1:]),
    )
    return pl.pallas_call(
        pack_kernel,
        grid_spec=grid_spec,
        out_shape=jax.ShapeDtypeStruct((places,) + queries.shape[1:], queries.dtype),
    )(src_span, queries)


def any_spec():
    return pl.BlockSpec(memory_space=pl.ANY)


def exchange_out(send_q, send_e, n_seq):
    dma = pltpu.SemaphoreType.DMA
    return pl.pallas_call(
        functools.partial(out_kernel, n_seq),
        out_shape=(
            jax.ShapeDtypeStruct(send_q.shape, send_q.dtype),
            jax.ShapeDtypeStruct(send_e.shape, send_e.dtype),
        ),
        in_specs=[any_spec()] * 2,
        out_specs=(any_spec(), any_spec()),
        scratch_shapes=[dma((n_seq,)), dma((n_seq,)), dma((n_seq,)), dma((n_seq,)), dma((2,))],
        compiler_params=pltpu.CompilerParams(collective_id=0, has_side_effects=True),
    )(send_q, send_e)


def exchange_back(ctx, stats, n_seq):
    dma = pltpu.SemaphoreType.DMA
    return pl.pallas_call(
        functools.partial(back_kernel, n_seq),
        out_shape=(
            jax.ShapeDtypeStruct(ctx.shape, ctx.dtype),
            jax.ShapeDtypeStruct(stats.shape, stats.dtype),
        ),
        in_specs=[any_spec()] * 2,
        out_specs=(any_spec(), any_spec()),
        scratch_shapes=[dma((n_seq,)), dma((n_seq,)), dma((n_seq,)), dma((n_seq,)), dma((2,))],
        compiler_params=pltpu.CompilerParams(collective_id=1, has_side_effects=True),
    )(ctx, stats)


def on_device(
    decoder_states,
    query_weight,
    output_weight,
    neighbour_kv,
    neighbour_shard,
    neighbour_entry,
    neighbour_count,
):
    tok_rows = decoder_states.shape[0]
    span_total = tok_rows // SPAN
    row_width = query_weight.shape[1]
    heads_here = row_width // HD
    key_len = neighbour_kv.shape[1]
    n_seq = lax.psum(1, "seq")
    n_db = lax.psum(1, "db")
    places_total = n_seq * CAP
    queries = jnp.dot(decoder_states, query_weight, preferred_element_type=jnp.float32).astype(
        jnp.bfloat16
    )
    queries = queries.reshape(span_total, SPAN, row_width)

    live, place = slot_places(neighbour_shard, neighbour_count)
    target = jnp.where(live, place, places_total)
    span_of_slot = jnp.arange(span_total * K, dtype=jnp.int32) // K
    src_span = jnp.full((places_total,), -1, jnp.int32)
    src_span = src_span.at[target].set(span_of_slot, mode="drop")
    send_q = pack(queries, src_span, places_total)
    send_e = jnp.zeros((places_total,), jnp.int32)
    send_e = send_e.at[target].set(neighbour_entry.reshape(-1), mode="drop")
    send_e = jnp.repeat(send_e.reshape(n_seq, CAP), SPAN, axis=1)
    send_e = jnp.pad(send_e, ((0, 0), (0, 2 * LANES - CAP * SPAN)))
    kv_flat = neighbour_kv.reshape(neighbour_kv.shape[0], key_len, 2 * row_width)
    back_ctx, back_stats, weight_cols = attend_back(
        send_q.reshape(n_seq, CAP * SPAN, row_width), send_e, kv_flat, output_weight,
        heads_here, n_seq, n_db
    )
    back_ctx = back_ctx.reshape(places_total, SPAN, row_width)
    context = combine(back_ctx, back_stats, place, neighbour_count, heads_here)
    context = context.reshape(tok_rows, row_width)

    contexts = lax.all_gather(context, "db", axis=0, tiled=False)
    out = jnp.einsum(
        "str,srf->tf", contexts, weight_cols, preferred_element_type=jnp.float32
    )
    return out.astype(jnp.bfloat16)


def solution(mesh):
    in_specs = (
        P("seq", None),
        P(None, "db"),
        P("db", None),
        P("seq", None, None, "db"),
        P("seq", None),
        P("seq", None),
        P("seq"),
    )
    out_specs = P("seq", "db")
    return jax.shard_map(
        on_device, mesh=mesh, in_specs=in_specs, out_specs=out_specs, check_vma=False
    )
```

```python
import functools
import math

import jax
import jax.numpy as jnp
from jax import lax
from jax.experimental import pallas as pl
from jax.experimental.pallas import tpu as pltpu
from jax.sharding import PartitionSpec as P

HD = 128
SPAN = 64
K = 2
CAP = 3
LANES = 128
MESH = pl.DeviceIdType.MESH


def slot_places(neighbour_shard, neighbour_count):
    own_shard = neighbour_shard.reshape(-1)
    slots = own_shard.shape[0]
    own_live = (
        jnp.arange(K, dtype=jnp.int32)[None, :] < neighbour_count[:, None]
    ).reshape(-1)
    same = (own_shard[None, :] == own_shard[:, None]) & own_live[None, :]
    earlier = jnp.arange(slots)[None, :] < jnp.arange(slots)[:, None]
    own_rank = jnp.minimum(jnp.sum((same & earlier).astype(jnp.int32), axis=1), CAP - 1)
    return own_live, own_shard * CAP + own_rank


def peer_copy(src, dst, send_sem, recv_sem, device):
    return pltpu.make_async_remote_copy(
        src_ref=src, dst_ref=dst, send_sem=send_sem, recv_sem=recv_sem,
        device_id=device, device_id_type=MESH,
    )


def out_kernel(n_seq, send_q, send_e, recv_q, recv_e, qs, qr, es, er, ls):
    me_s = lax.axis_index("seq")
    me_d = lax.axis_index("db")

    barrier = pltpu.get_barrier_semaphore()

    @pl.loop(1, n_seq)
    def _(o):
        pl.semaphore_signal(barrier, inc=1, device_id=(lax.rem(me_s + o, n_seq), me_d),
                            device_id_type=MESH)

    pl.semaphore_wait(barrier, n_seq - 1)

    own = [
        pltpu.make_async_copy(send_q.at[me_s], recv_q.at[me_s], ls.at[0]),
        pltpu.make_async_copy(send_e.at[me_s], recv_e.at[me_s], ls.at[1]),
    ]
    for c in own:
        c.start()

    @pl.loop(1, n_seq)
    def _(o):
        d = lax.rem(me_s + o, n_seq)
        peer_copy(send_e.at[d], recv_e.at[me_s], es.at[d], er.at[me_s], (d, me_d)).start()
        peer_copy(send_q.at[d], recv_q.at[me_s], qs.at[d], qr.at[me_s], (d, me_d)).start()

    for c in own:
        c.wait()

    @pl.loop(1, n_seq)
    def _(o):
        d = lax.rem(me_s + o, n_seq)
        s = lax.rem(me_s + n_seq - o, n_seq)
        peer_copy(send_e.at[d], recv_e.at[me_s], es.at[d], er.at[me_s], (d, me_d)).wait_send()
        peer_copy(send_q.at[d], recv_q.at[me_s], qs.at[d], qr.at[me_s], (d, me_d)).wait_send()
        peer_copy(send_e.at[me_s], recv_e.at[s], es.at[s], er.at[s], (s, me_d)).wait_recv()
        peer_copy(send_q.at[me_s], recv_q.at[s], qs.at[s], qr.at[s], (s, me_d)).wait_recv()


def back_kernel(n_seq, ctx, stats, back_ctx, back_stats, cs, cr, ss, sr, ls):
    me_s = lax.axis_index("seq")
    me_d = lax.axis_index("db")
    barrier = pltpu.get_barrier_semaphore()

    @pl.loop(1, n_seq)
    def _(o):
        pl.semaphore_signal(barrier, inc=1, device_id=(lax.rem(me_s + o, n_seq), me_d),
                            device_id_type=MESH)

    pl.semaphore_wait(barrier, n_seq - 1)

    own = [
        pltpu.make_async_copy(ctx.at[me_s], back_ctx.at[me_s], ls.at[0]),
        pltpu.make_async_copy(stats.at[me_s], back_stats.at[me_s], ls.at[1]),
    ]
    for c in own:
        c.start()

    @pl.loop(1, n_seq)
    def _(o):
        d = lax.rem(me_s + o, n_seq)
        peer_copy(stats.at[d], back_stats.at[me_s], ss.at[d], sr.at[me_s], (d, me_d)).start()
        peer_copy(ctx.at[d], back_ctx.at[me_s], cs.at[d], cr.at[me_s], (d, me_d)).start()

    for c in own:
        c.wait()

    @pl.loop(1, n_seq)
    def _(o):
        d = lax.rem(me_s + o, n_seq)
        s = lax.rem(me_s + n_seq - o, n_seq)
        peer_copy(stats.at[d], back_stats.at[me_s], ss.at[d], sr.at[me_s], (d, me_d)).wait_send()
        peer_copy(ctx.at[d], back_ctx.at[me_s], cs.at[d], cr.at[me_s], (d, me_d)).wait_send()
        peer_copy(stats.at[me_s], back_stats.at[s], ss.at[s], sr.at[s], (s, me_d)).wait_recv()
        peer_copy(ctx.at[me_s], back_ctx.at[s], cs.at[s], cr.at[s], (s, me_d)).wait_recv()


def attend_kernel(scale, heads, rows, e_ref, q_ref, kv_ref, ctx_ref, stats_ref):
    key_len = SPAN * 2
    keys_total, width = kv_ref.shape[0], heads * HD
    per_tile = rows // SPAN
    col_block = lax.broadcasted_iota(jnp.int32, (1, keys_total), 1) // key_len
    row_block = lax.broadcasted_iota(jnp.int32, (rows, 1), 0) // SPAN

    def one_tile(t, carry):
        start = pl.multiple_of(t * rows, rows)
        row_entry = jnp.zeros((rows, 1), jnp.int32)
        for j in range(per_tile):
            row_entry = jnp.where(row_block == j, e_ref[t * per_tile + j], row_entry)
        named = col_block == row_entry
        for h in range(heads):
            q = q_ref[pl.ds(start, rows), h * HD:(h + 1) * HD]
            k = kv_ref[:, h * HD:(h + 1) * HD]
            v = kv_ref[:, width + h * HD:width + (h + 1) * HD]
            s = lax.dot_general(
                q, k, (((1,), (1,)), ((), ())), preferred_element_type=jnp.float32
            ) * scale
            s = jnp.where(named, s, -jnp.inf)
            top = jnp.max(s, axis=1, keepdims=True)
            w = jnp.exp(s - top)
            total = jnp.sum(w, axis=1, keepdims=True)
            ctx = jnp.dot(w.astype(jnp.bfloat16), v, preferred_element_type=jnp.float32)
            ctx_ref[pl.ds(start, rows), h * HD:(h + 1) * HD] = (ctx / total).astype(ctx_ref.dtype)
            stats_ref[pl.ds(start, rows), 2 * h:2 * h + 1] = top
            stats_ref[pl.ds(start, rows), 2 * h + 1:2 * h + 2] = total
        return carry

    lax.fori_loop(0, q_ref.shape[0] // rows, one_tile, 0)


def vmem_whole(shape):
    return pl.BlockSpec(shape, lambda *_: (0,) * len(shape))


def attend(recv_q, recv_e, kv_flat, heads):
    n_src, cap, span, width = recv_q.shape
    q_rows = recv_q.reshape(n_src * cap * span, width)
    kv_rows = kv_flat.reshape(-1, kv_flat.shape[2])
    stats_shape = (q_rows.shape[0], 2 * heads)
    grid_spec = pltpu.PrefetchScalarGridSpec(
        num_scalar_prefetch=1,
        grid=(1,),
        in_specs=[vmem_whole(q_rows.shape), vmem_whole(kv_rows.shape)],
        out_specs=[vmem_whole(q_rows.shape), vmem_whole(stats_shape)],
    )
    ctx, stats = pl.pallas_call(
        functools.partial(attend_kernel, 1.0 / math.sqrt(HD), heads, 4 * span),
        grid_spec=grid_spec,
        out_shape=(
            jax.ShapeDtypeStruct(q_rows.shape, jnp.bfloat16),
            jax.ShapeDtypeStruct(stats_shape, jnp.float32),
        ),
    )(recv_e, q_rows, kv_rows)
    return ctx.reshape(recv_q.shape), stats.reshape(n_src, cap, span, 2 * heads)


def attend_back_kernel(n_seq, n_db, heads, scale, send_e, send_q, kv_ref, w_loc, back_ctx,
                       back_stats, stage_ctx, stage_stats, w_cols, ctx_v, stats_v, recv_q,
                       recv_e, cs, cr, ss, sr, ws, wr, ls, stg, qs, qr, es, er):
    me_s = lax.axis_index("seq")
    me_d = lax.axis_index("db")
    rows = stage_ctx.shape[1]
    keys_total = kv_ref.shape[0]
    width = heads * HD
    cap = rows // SPAN
    key_block = lax.broadcasted_iota(jnp.int32, (keys_total, 1), 0) // (2 * SPAN)
    lane_place = lax.broadcasted_iota(jnp.int32, (1, rows), 1) // SPAN

    barrier = pltpu.get_barrier_semaphore()

    @pl.loop(1, n_seq)
    def _(o):
        pl.semaphore_signal(barrier, inc=1, device_id=(lax.rem(me_s + o, n_seq), me_d),
                            device_id_type=MESH)

    @pl.loop(1, n_db)
    def _(o):
        pl.semaphore_signal(barrier, inc=1, device_id=(me_s, lax.rem(me_d + o, n_db)),
                            device_id_type=MESH)

    pl.semaphore_wait(barrier, (n_seq - 1) + (n_db - 1))

    features = w_cols.shape[2]

    def w_src(d):
        return w_loc.at[:, pl.ds(pl.multiple_of(d * features, features), features)]

    own_w = pltpu.make_async_copy(w_src(me_d), w_cols.at[me_d], ls.at[4])
    own_w.start()

    own_in = [
        pltpu.make_async_copy(send_q.at[me_s], recv_q.at[me_s], ls.at[0]),
        pltpu.make_async_copy(send_e.at[me_s], recv_e.at[me_s], ls.at[1]),
    ]
    for c in own_in:
        c.start()

    def q_in(d, s):
        return peer_copy(send_q.at[d], recv_q.at[s], qs.at[d], qr.at[s], (d, me_d))

    def e_in(d, s):
        return peer_copy(send_e.at[d], recv_e.at[s], es.at[d], er.at[s], (d, me_d))

    @pl.loop(1, n_seq)
    def _(o):
        d = lax.rem(me_s + o, n_seq)
        e_in(d, me_s).start()
        q_in(d, me_s).start()

    @pl.loop(1, n_db)
    def _(o):
        d = lax.rem(me_d + o, n_db)
        peer_copy(w_src(d), w_cols.at[me_d], ws.at[d], wr.at[me_d], (me_s, d)).start()

    def compute(d, slot):
        entry = recv_e[pl.ds(d, 1), 0:rows]
        named = key_block == entry
        for h in range(heads):
            q = recv_q[d, :, h * HD:(h + 1) * HD]
            k = kv_ref[:, h * HD:(h + 1) * HD]
            v = kv_ref[:, width + h * HD:width + (h + 1) * HD]
            st = lax.dot_general(
                k, q, (((1,), (1,)), ((), ())), preferred_element_type=jnp.float32
            ) * scale
            st = jnp.where(named, st, -jnp.inf)
            top = jnp.max(st, axis=0, keepdims=True)
            w = jnp.exp(st - top)
            total = jnp.sum(w, axis=0, keepdims=True)
            u = lax.dot_general(
                w.astype(jnp.bfloat16), v, (((0,), (0,)), ((), ())),
                preferred_element_type=jnp.float32,
            )
            ctx_v[slot, :, h * HD:(h + 1) * HD] = u.astype(ctx_v.dtype)
            stats_v[slot, 2 * h:2 * h + 1, 0:rows] = top
            stats_v[slot, 2 * h + 1:2 * h + 2, 0:rows] = total

    def staged(d, slot):
        return [
            pltpu.make_async_copy(ctx_v.at[slot], stage_ctx.at[d], stg.at[0, slot]),
            pltpu.make_async_copy(stats_v.at[slot], stage_stats.at[d], stg.at[1, slot]),
        ]

    def send(d):
        peer_copy(stage_stats.at[d], back_stats.at[me_s], ss.at[d], sr.at[me_s], (d, me_d)).start()
        peer_copy(stage_ctx.at[d], back_ctx.at[me_s], cs.at[d], cr.at[me_s], (d, me_d)).start()

    for c in own_in:
        c.wait()
    compute(me_s, 0)
    for c in staged(me_s, 0):
        c.start()
    for c in staged(me_s, 0):
        c.wait()
    own = [
        pltpu.make_async_copy(stage_ctx.at[me_s], back_ctx.at[me_s], ls.at[2]),
        pltpu.make_async_copy(stage_stats.at[me_s], back_stats.at[me_s], ls.at[3]),
    ]
    for c in own:
        c.start()

    @pl.loop(1, n_seq)
    def _(o):
        d = lax.rem(me_s + o, n_seq)
        slot = lax.rem(o, 2)
        e_in(me_s, d).wait_recv()
        q_in(me_s, d).wait_recv()
        compute(d, slot)
        for c in staged(d, slot):
            c.start()

        @pl.when(o > 1)
        def _():
            prev = lax.rem(me_s + o - 1, n_seq)
            for c in staged(prev, 1 - slot):
                c.wait()
            send(prev)

    last = lax.rem(me_s + n_seq - 1, n_seq)
    for c in staged(last, (n_seq - 1) % 2):
        c.wait()
    send(last)

    for c in own:
        c.wait()

    @pl.loop(1, n_seq)
    def _(o):
        d = lax.rem(me_s + o, n_seq)
        e_in(d, me_s).wait_send()
        q_in(d, me_s).wait_send()

    @pl.loop(1, n_seq)
    def _(o):
        d = lax.rem(me_s + o, n_seq)
        s = lax.rem(me_s + n_seq - o, n_seq)
        peer_copy(stage_stats.at[d], back_stats.at[me_s], ss.at[d], sr.at[me_s], (d, me_d)).wait_send()
        peer_copy(stage_ctx.at[d], back_ctx.at[me_s], cs.at[d], cr.at[me_s], (d, me_d)).wait_send()
        peer_copy(stage_stats.at[me_s], back_stats.at[s], ss.at[s], sr.at[s], (s, me_d)).wait_recv()
        peer_copy(stage_ctx.at[me_s], back_ctx.at[s], cs.at[s], cr.at[s], (s, me_d)).wait_recv()

    own_w.wait()

    @pl.loop(1, n_db)
    def _(o):
        d = lax.rem(me_d + o, n_db)
        s = lax.rem(me_d + n_db - o, n_db)
        peer_copy(w_src(d), w_cols.at[me_d], ws.at[d], wr.at[me_d], (me_s, d)).wait_send()
        peer_copy(w_src(me_d), w_cols.at[s], ws.at[s], wr.at[s], (me_s, s)).wait_recv()


def attend_back(send_q, send_e, kv_flat, w_loc, heads, n_seq, n_db):
    n_src, rows, width = send_q.shape
    kv_rows = kv_flat.reshape(-1, kv_flat.shape[2])
    stats_shape = (n_src, 8, 2 * LANES)
    ctx_shape = (n_src, rows, width)
    dma = pltpu.SemaphoreType.DMA
    outs = pl.pallas_call(
        functools.partial(attend_back_kernel, n_seq, n_db, heads, 1.0 / math.sqrt(HD)),
        out_shape=(
            jax.ShapeDtypeStruct(ctx_shape, jnp.bfloat16),
            jax.ShapeDtypeStruct(stats_shape, jnp.float32),
            jax.ShapeDtypeStruct(ctx_shape, jnp.bfloat16),
            jax.ShapeDtypeStruct(stats_shape, jnp.float32),
            jax.ShapeDtypeStruct((n_db, w_loc.shape[0], w_loc.shape[1] // n_db), w_loc.dtype),
        ),
        in_specs=[
            any_spec(),
            any_spec(),
            pl.BlockSpec(memory_space=pltpu.VMEM),
            any_spec(),
        ],
        out_specs=(any_spec(), any_spec(), any_spec(), any_spec(), any_spec()),
        scratch_shapes=[
            pltpu.VMEM((2, rows, width), jnp.bfloat16),
            pltpu.VMEM((2,) + stats_shape[1:], jnp.float32),
            pltpu.VMEM(send_q.shape, send_q.dtype),
            pltpu.VMEM(send_e.shape, send_e.dtype),
            dma((n_seq,)), dma((n_seq,)), dma((n_seq,)), dma((n_seq,)),
            dma((n_db,)), dma((n_db,)), dma((5,)), dma((2, 2)),
            dma((n_seq,)), dma((n_seq,)), dma((n_seq,)), dma((n_seq,)),
        ],
        compiler_params=pltpu.CompilerParams(collective_id=1, has_side_effects=True),
    )(send_e, send_q, kv_rows, w_loc)
    return outs[0], outs[1], outs[4]


def combine_kernel(heads, place_ref, count_ref, ctx_ref, stats_ref, out_ref, stats_t):
    for s in range(stats_ref.shape[0]):
        stats_t[s] = jnp.transpose(stats_ref[s])

    def one_span(c, carry):
        p0 = place_ref[c * K]
        p1 = place_ref[c * K + 1]
        r0 = pl.multiple_of(lax.rem(p0, CAP) * SPAN, SPAN)
        r1 = pl.multiple_of(lax.rem(p1, CAP) * SPAN, SPAN)
        st0 = stats_t[p0 // CAP, pl.ds(r0, SPAN), :]
        st1 = stats_t[p1 // CAP, pl.ds(r1, SPAN), :]
        live1 = count_ref[c] > 1
        for h in range(heads):
            cols = slice(h * HD, (h + 1) * HD)
            m0, l0 = st0[:, 2 * h:2 * h + 1], st0[:, 2 * h + 1:2 * h + 2]
            m1, l1 = st1[:, 2 * h:2 * h + 1], st1[:, 2 * h + 1:2 * h + 2]
            best = jnp.where(live1, jnp.maximum(m0, m1), m0)
            a0 = jnp.exp(m0 - best)
            a1 = jnp.where(live1, jnp.exp(m1 - best), 0.0)
            u0 = ctx_ref[p0, :, cols].astype(jnp.float32)
            u1 = jnp.where(live1, ctx_ref[p1, :, cols].astype(jnp.float32), 0.0)
            out_ref[c, :, cols] = (
                (a0 * u0 + a1 * u1) / (a0 * l0 + a1 * l1)
            ).astype(out_ref.dtype)
        return carry

    lax.fori_loop(0, out_ref.shape[0], one_span, 0, unroll=True)


def combine(back_ctx, back_stats, place, neighbour_count, heads):
    places, span, width = back_ctx.shape
    spans = neighbour_count.shape[0]
    n_src, st_rows, st_cols = back_stats.shape
    grid_spec = pltpu.PrefetchScalarGridSpec(
        num_scalar_prefetch=2,
        grid=(1,),
        in_specs=[vmem_whole(back_ctx.shape), vmem_whole(back_stats.shape)],
        out_specs=vmem_whole((spans, span, width)),
        scratch_shapes=[pltpu.VMEM((n_src, st_cols, st_rows), jnp.float32)],
    )
    return pl.pallas_call(
        functools.partial(combine_kernel, heads),
        grid_spec=grid_spec,
        out_shape=jax.ShapeDtypeStruct((spans, span, width), jnp.bfloat16),
    )(place, neighbour_count, back_ctx, back_stats)


def pack_kernel(src_ref, q_ref, out_ref):
    def one_place(p, carry):
        span = src_ref[p]
        rows = q_ref[jnp.maximum(span, 0)]
        out_ref[p] = jnp.where(span >= 0, rows, jnp.zeros_like(rows))
        return carry

    lax.fori_loop(0, out_ref.shape[0], one_place, 0, unroll=8)


def pack(queries, src_span, places):
    grid_spec = pltpu.PrefetchScalarGridSpec(
        num_scalar_prefetch=1,
        grid=(1,),
        in_specs=[vmem_whole(queries.shape)],
        out_specs=vmem_whole((places,) + queries.shape[1:]),
    )
    return pl.pallas_call(
        pack_kernel,
        grid_spec=grid_spec,
        out_shape=jax.ShapeDtypeStruct((places,) + queries.shape[1:], queries.dtype),
    )(src_span, queries)


def any_spec():
    return pl.BlockSpec(memory_space=pl.ANY)


def exchange_out(send_q, send_e, n_seq):
    dma = pltpu.SemaphoreType.DMA
    return pl.pallas_call(
        functools.partial(out_kernel, n_seq),
        out_shape=(
            jax.ShapeDtypeStruct(send_q.shape, send_q.dtype),
            jax.ShapeDtypeStruct(send_e.shape, send_e.dtype),
        ),
        in_specs=[any_spec()] * 2,
        out_specs=(any_spec(), any_spec()),
        scratch_shapes=[dma((n_seq,)), dma((n_seq,)), dma((n_seq,)), dma((n_seq,)), dma((2,))],
        compiler_params=pltpu.CompilerParams(collective_id=0, has_side_effects=True),
    )(send_q, send_e)


def exchange_back(ctx, stats, n_seq):
    dma = pltpu.SemaphoreType.DMA
    return pl.pallas_call(
        functools.partial(back_kernel, n_seq),
        out_shape=(
            jax.ShapeDtypeStruct(ctx.shape, ctx.dtype),
            jax.ShapeDtypeStruct(stats.shape, stats.dtype),
        ),
        in_specs=[any_spec()] * 2,
        out_specs=(any_spec(), any_spec()),
        scratch_shapes=[dma((n_seq,)), dma((n_seq,)), dma((n_seq,)), dma((n_seq,)), dma((2,))],
        compiler_params=pltpu.CompilerParams(collective_id=1, has_side_effects=True),
    )(ctx, stats)


def on_device(
    decoder_states,
    query_weight,
    output_weight,
    neighbour_kv,
    neighbour_shard,
    neighbour_entry,
    neighbour_count,
):
    tok_rows = decoder_states.shape[0]
    span_total = tok_rows // SPAN
    row_width = query_weight.shape[1]
    heads_here = row_width // HD
    key_len = neighbour_kv.shape[1]
    n_seq = lax.psum(1, "seq")
    n_db = lax.psum(1, "db")
    places_total = n_seq * CAP
    queries = jnp.dot(decoder_states, query_weight, preferred_element_type=jnp.float32).astype(
        jnp.bfloat16
    )
    queries = queries.reshape(span_total, SPAN, row_width)

    live, place = slot_places(neighbour_shard, neighbour_count)
    target = jnp.where(live, place, places_total)
    span_of_slot = jnp.arange(span_total * K, dtype=jnp.int32) // K
    src_span = jnp.full((places_total,), -1, jnp.int32)
    src_span = src_span.at[target].set(span_of_slot, mode="drop")
    send_q = pack(queries, src_span, places_total)
    send_e = jnp.zeros((places_total,), jnp.int32)
    send_e = send_e.at[target].set(neighbour_entry.reshape(-1), mode="drop")
    send_e = jnp.repeat(send_e.reshape(n_seq, CAP), SPAN, axis=1)
    send_e = jnp.pad(send_e, ((0, 0), (0, 2 * LANES - CAP * SPAN)))
    kv_flat = neighbour_kv.reshape(neighbour_kv.shape[0], key_len, 2 * row_width)
    back_ctx, back_stats, weight_cols = attend_back(
        send_q.reshape(n_seq, CAP * SPAN, row_width), send_e, kv_flat, output_weight,
        heads_here, n_seq, n_db
    )
    back_ctx = back_ctx.reshape(places_total, SPAN, row_width)
    context = combine(back_ctx, back_stats, place, neighbour_count, heads_here)
    context = context.reshape(tok_rows, row_width)

    contexts = lax.all_gather(context, "db", axis=0, tiled=False)
    out = jnp.einsum(
        "str,srf->tf", contexts, weight_cols, preferred_element_type=jnp.float32
    )
    return out.astype(jnp.bfloat16)


def solution(mesh):
    in_specs = (
        P("seq", None),
        P(None, "db"),
        P("db", None),
        P("seq", None, None, "db"),
        P("seq", None),
        P("seq", None),
        P("seq"),
    )
    out_specs = P("seq", "db")
    return jax.shard_map(
        on_device, mesh=mesh, in_specs=in_specs, out_specs=out_specs, check_vma=False
    )
```
